32 devices in a mesh: groups: 2 (over x), ctx: 16 (over z, y, core).
Axes of the slice: x: 2, y: 2, z: 4, core: 2. Of those that a mesh axis runs over, the one named last changes fastest.
Arguments:
- conv_input: bfloat16 [4096, 5120], P(('groups', 'ctx')), parts along dimension 0, may hold values from -6 to 6
- step_raw: float32 [4096, 64], P(('groups', 'ctx')), parts along dimension 0, may hold values from -5 to 5.5
- step_bias: float32 [64], replicated, may hold values from -14 to -2
- decay_log: float32 [64], replicated, may hold values from -3 to 0.7
- skip_gain: float32 [64], replicated, may hold values from 0.5 to 1.5
- conv_weight: float32 [4, 5120], replicated, may hold values from -3 to 3
- conv_bias: float32 [5120], replicated, may hold values from -1 to 0.5
- doc_lengths: int32 [8], P('groups'), parts along dimension 0, may hold values from 1 to 1024, 2048 in all
- grad_out: bfloat16 [4096, 4096], P(('groups', 'ctx')), parts along dimension 0, may hold values from -400 to 400
Outputs:
- mixer_out: bfloat16 [4096, 4096], P(('groups', 'ctx')), parts along dimension 0
- grad_input: bfloat16 [4096, 5120], P(('groups', 'ctx')), parts along dimension 0
- grad_step: float32 [4096, 64], P(('groups', 'ctx')), parts along dimension 0
- grad_conv: float32 [10, 5120], P('groups'), parts along dimension 0
- grad_heads: float32 [6, 64], P('groups'), parts along dimension 0
The draws below stay inside these ranges and needn't reach their ends.
There are 2 independent parts, one for each index of `groups`. The reference program is written for one: setup_inputs(seed, part) draws one part's arguments, and reference() takes and returns one part's arrays. A program takes and returns all parts, laid end to end along the dimension named above; an argument that names none is the same for every part. Nothing has to cross between parts.
Inputs may be any that keep to these rules, and one draw needn't show every extreme that they name: doc_lengths lists the lengths of the 4 documents that follow one another from token 0; they sum to 2048, and the longest has exactly 1024 tokens.
All inputs are finite; a program needn't handle non-finite values.
Results may differ from the reference program's by a relative error of at most 0.001.
Values may be sent and summed in bfloat16 or wider, within the bound.
No kernel may reach another device: no remote copies, remote signals or barrier semaphores. Data moves between devices by JAX's collectives and lax.ppermute only.
A program may use at most 192 MiB of HBM per device.

```python
import math
import jax
import jax.numpy as jnp
import numpy as np
from jax import lax

HEADS = 64
HEADDIM = 64
STATE = 128
GROUPS = 4
CONV = 4
DOCS = 4
TOK_DEV = 128
TOKENS = 2048
CHANNELS = 5120


def head_kinds(key):
    picks = jax.random.uniform(jax.random.fold_in(key, 7001), (HEADS,), jnp.float32)
    share = 0.5
    return picks < share


def draw_step_bias(key, part):
    slow = head_kinds(key)
    slow_values = jax.random.uniform(jax.random.fold_in(key, 7002), (HEADS,), jnp.float32, math.log(0.2), 0.0) - 4.57 - math.log(TOK_DEV)
    fast_values = jax.random.uniform(jax.random.fold_in(key, 7003), (HEADS,), jnp.float32, -4.0, -2.0)
    return jnp.where(slow, slow_values, fast_values)


def draw_decay_log(key, part):
    slow = head_kinds(key)
    slow_values = jax.random.uniform(jax.random.fold_in(key, 7004), (HEADS,), jnp.float32, math.log(0.05), 0.0)
    fast_values = jax.random.uniform(jax.random.fold_in(key, 7005), (HEADS,), jnp.float32, math.log(0.2), math.log(2.0))
    return jnp.where(slow, slow_values, fast_values)


def draw_step_raw(key, part):
    symbol_tile_sequence = TOKENS // TOK_DEV
    rough = 0.7 * jnp.clip(jax.random.normal(jax.random.fold_in(key, 8001), (TOKENS, HEADS), jnp.float32), -2.0, 2.0)
    muted_attenders = jax.random.uniform(jax.random.fold_in(key, 8002), (symbol_tile_sequence,), jnp.float32, -3.5, 0.0)
    leading_attenders = jax.random.uniform(jax.random.fold_in(key, 8003), (symbol_tile_sequence,), jnp.float32, 3.2, 4.0)
    picked_variant = jax.random.permutation(jax.random.fold_in(key, 8004), symbol_tile_sequence)[:min(3, symbol_tile_sequence)]
    spike_clusters = jnp.any(jnp.arange(symbol_tile_sequence)[:, None] == picked_variant[None, :], axis=1)
    symbol_offset_shift = jnp.where(spike_clusters, leading_attenders, muted_attenders)
    return rough + jnp.repeat(symbol_offset_shift, TOK_DEV)[:, None]


def draw_grad_out(key, part):
    total_rows = TOKENS
    total_cols = HEADS * HEADDIM
    position = jnp.arange(total_rows, dtype=jnp.float32) / total_rows
    ten_log = math.log(10.0)
    row_spread = jnp.exp(ten_log * jax.random.uniform(jax.random.fold_in(key, 1), (total_rows, 1), jnp.float32))
    col_spread = jnp.exp(ten_log * jax.random.uniform(jax.random.fold_in(key, 2), (1, total_cols), jnp.float32))
    base = jnp.clip(jax.random.normal(jax.random.fold_in(key, 3), (total_rows, total_cols), jnp.float32), -4.0, 4.0)
    rise = jnp.exp(math.log(3.0) * position)
    return (0.1 * base * rise[:, None] * row_spread * col_spread).astype(jnp.bfloat16)


def block_scale(rng, extent, cuts, smallest, high):
    def one(dim, blocks):
        draws = jax.random.uniform(jax.random.fold_in(jax.random.fold_in(rng, 6), dim), (blocks,), jnp.float32, smallest / len(cuts), high / len(cuts))
        return jnp.repeat(jnp.exp(draws), extent[dim] // blocks).reshape((-1,) + (1,) * (len(extent) - dim - 1))

    factor_of = one(*cuts[0])
    for cut in cuts[1:]:
        factor_of = factor_of * one(*cut)
    return factor_of


def length_profile(number_of, total, most, skew):
    loads = [(1 << 20) // math.isqrt(standing ** skew) + 1 for standing in range(2, number_of + 1)]
    surplus, counts = total - most - (number_of - 1), [1] * (number_of - 1)
    while surplus > 0:
        candidates = [i for i in range(number_of - 1) if counts[i] < most]
        whole, budget = sum([loads[i] for i in candidates]), surplus
        for i in candidates:
            more = min(most - counts[i], max(1, budget * loads[i] // whole), surplus)
            counts[i] = counts[i] + more
            surplus = surplus - more
    return np.array([most] + counts)


def uneven_parts(own_key, number_of, total, bound, lean):
    if number_of == 2:
        one = jax.random.randint(own_key, (), max(1, total - bound), min(bound, total - 1) + 1)
        return jnp.stack([one, total - one])
    tallies = jnp.asarray(length_profile(number_of, total, bound, lean), jnp.int32)
    pairs = (number_of - 1) // 2
    donor, receiver = tallies[1:1 + 2 * pairs:2], tallies[2:2 + 2 * pairs:2]
    margin = jnp.minimum(donor - 1, bound - receiver)
    passed = jax.random.randint(jax.random.fold_in(own_key, 1), (pairs,), 0, 1 << 20) % (margin + 1)
    tallies = tallies.at[1:1 + 2 * pairs:2].set(donor - passed).at[2:2 + 2 * pairs:2].set(receiver + passed)
    return tallies[jax.random.permutation(jax.random.fold_in(own_key, 2), number_of)]


def normal_values(stream_key, shape, scale, most, cuts=(), kind=jnp.bfloat16):
    factor_of = block_scale(stream_key, shape, cuts, -0.22, 0.18) if cuts else 1.0
    drawn = jax.random.normal(stream_key, shape, jnp.float32) * scale * factor_of
    return jnp.minimum(jnp.maximum(drawn, -most), most).astype(kind)


def setup_inputs(seed: int = 0, part: int = 0) -> dict:
    key_of = jax.random.split(jax.random.key(seed), 10)
    part_splits = jax.random.split(jax.random.fold_in(key_of[9], part), 10)
    return {
        "conv_input": normal_values(part_splits[0], (TOKENS, CHANNELS), 1.0, 6.0, ((0, 16),)),
        "step_raw": draw_step_raw(jax.random.fold_in(jax.random.fold_in(key_of[9], part), 71), part),
        "step_bias": draw_step_bias(jax.random.fold_in(key_of[9], 71), part),
        "decay_log": draw_decay_log(jax.random.fold_in(key_of[9], 71), part),
        "skip_gain": jnp.clip(jax.random.uniform(key_of[4], (HEADS,), jnp.float32, 0.5, 1.5), 0.5, 1.5),
        "conv_weight": normal_values(key_of[5], (CONV, CHANNELS), CONV ** -0.5, 3.0, (), jnp.float32),
        "conv_bias": jnp.clip(jax.random.uniform(key_of[6], (CHANNELS,), jnp.float32, -1.0, 0.5), -1.0, 0.5),
        "doc_lengths": uneven_parts(part_splits[7], DOCS, TOKENS, TOKENS // 2, 0).astype(jnp.int32),
        "grad_out": draw_grad_out(jax.random.fold_in(jax.random.fold_in(key_of[9], part), 71), part),
    }


HIGH = lax.Precision.HIGHEST

def doc_offsets(doc_lengths, positions):
    ends = jnp.cumsum(doc_lengths, dtype=jnp.int32)
    starts = ends - doc_lengths
    before = starts[None, :] <= positions[:, None]
    opening = lax.optimization_barrier(jnp.max(jnp.where(before, starts[None, :], 0), axis=1))
    return positions - opening

def convolve(extended, conv_weight, conv_bias, inside):
    count = inside.shape[0]
    taps = conv_weight.shape[0]
    total = jnp.zeros((count, extended.shape[1]), jnp.float32) + conv_bias[None, :]
    for lag in range(taps):
        reach = taps - 1 - lag
        valid = (inside >= reach).astype(jnp.float32)[:, None]
        total = total + conv_weight[lag][None, :] * extended[lag:lag + count] * valid
    return jax.nn.silu(total)

def block_terms(carried, pieces):
    state, skip_heads = carried
    inputs, b_values, c_values, step_size, log_rate, opening = pieces
    cum_decay = jnp.cumsum(log_rate, axis=0)
    doc_count = jnp.cumsum(opening, axis=0)
    length = opening.shape[0]
    order = jnp.arange(length, dtype=jnp.int32)
    allowed = (doc_count[:, None] == doc_count[None, :]) & (order[:, None] >= order[None, :])
    spread = cum_decay[:, None] - cum_decay[None, :]
    decay = jnp.exp(jnp.where(allowed[:, :, None, None], spread, -1e+30))
    scores = jnp.einsum('tgn,sgn->tsg', c_values, b_values, precision=HIGH)
    weights = scores[:, :, :, None] * decay * step_size[None]
    y_diag = jnp.einsum('tsgr,sgrp->tgrp', weights, inputs, precision=HIGH)
    head_in = jnp.exp(cum_decay) * (doc_count == 0)[:, None, None]
    y_carry = head_in[..., None] * jnp.einsum('tgn,grpn->tgrp', c_values, state, precision=HIGH)
    tail = jnp.exp(cum_decay[-1][None] - cum_decay) * (doc_count == doc_count[-1])[:, None, None]
    local = jnp.einsum('sgrp,sgn->grpn', inputs * (tail * step_size)[..., None], b_values, precision=HIGH)
    whole = jnp.exp(cum_decay[-1]) * (doc_count[-1] == 0)
    state = whole[..., None, None] * state + local
    mixed = y_diag + y_carry + skip_heads[None, :, :, None] * inputs
    return ((state, skip_heads), mixed)

def forward(conv_input, step_raw, step_bias, decay_log, skip_gain, conv_weight, conv_bias, inside):
    taps = conv_weight.shape[0]
    extended = jnp.concatenate([jnp.zeros((taps - 1, conv_input.shape[1]), conv_input.dtype), conv_input], axis=0)
    act = convolve(extended, conv_weight, conv_bias, inside)
    inner = HEADS * HEADDIM
    width = GROUPS * STATE
    share = HEADS // GROUPS
    block = math.gcd(TOKENS, 256)
    count = TOKENS // block
    inputs = act[:, :inner].reshape(count, block, GROUPS, share, HEADDIM)
    b_values = act[:, inner:inner + width].reshape(count, block, GROUPS, STATE)
    c_values = act[:, inner + width:].reshape(count, block, GROUPS, STATE)
    step_size = jax.nn.softplus(step_raw + step_bias[None, :])
    log_rate = -step_size * jnp.exp(decay_log)[None, :]
    opening = (inside == 0).astype(step_size.dtype).reshape(count, block)
    skip_heads = skip_gain.reshape(GROUPS, share)
    shaped = (inputs, b_values, c_values, step_size.reshape(count, block, GROUPS, share), log_rate.reshape(count, block, GROUPS, share), opening)
    state = jnp.zeros((GROUPS, share, HEADDIM, STATE), step_size.dtype)
    carried, outputs = lax.scan(jax.checkpoint(block_terms), (state, skip_heads), shaped)
    return outputs.reshape(TOKENS, inner)

def reference(conv_input, step_raw, step_bias, decay_log, skip_gain, conv_weight, conv_bias, doc_lengths, grad_out):
    positions = jnp.arange(TOKENS, dtype=jnp.int32)
    inside = doc_offsets(doc_lengths, positions)

    def mixer(source, raw_steps, biases, logs, skips, kernel, kernel_bias):
        return forward(source, raw_steps, biases, logs, skips, kernel, kernel_bias, inside)
    complete_output, pullback = jax.vjp(mixer, conv_input.astype(jnp.float32), step_raw, step_bias, decay_log, skip_gain, conv_weight, conv_bias)
    grads = pullback(grad_out.astype(jnp.float32))
    scale = TOKENS ** (-0.5)
    grad_conv = jnp.concatenate([grads[5], grads[6][None, :]], axis=0) * scale
    grad_heads = jnp.stack([grads[2], grads[3], grads[4]]) * scale
    return (complete_output.astype(jnp.bfloat16), grads[0].astype(jnp.bfloat16), grads[1], grad_conv, grad_heads)
```

```python
import functools

import jax
import jax.numpy as jnp
from jax import lax
from jax.experimental import pallas as pl
from jax.experimental.pallas import tpu as pltpu
from jax.sharding import PartitionSpec as P

GROUPS = 4
F32 = jnp.float32
BF16 = jnp.bfloat16
NEG = -1e30
LIMIT = 12 * 1024 * 1024
STEP, CUM, TAIL, HEAD, TP, HP, WHOLE, SIG = range(8)

NN = (((1,), (0,)), ((), ()))
NT = (((1,), (1,)), ((), ()))
TN = (((0,), (0,)), ((), ()))


def mm(a, b, dims):
    return lax.dot_general(a, b, dims, preferred_element_type=F32)


def halves(a):
    high = a.astype(BF16)
    return high, (a - high.astype(F32)).astype(BF16)


def thirds(a):
    high = a.astype(BF16)
    rest = a - high.astype(F32)
    mid = rest.astype(BF16)
    return high, mid, (rest - mid.astype(F32)).astype(BF16)


def dot3(a, b, dims):
    ah, al = halves(a)
    bh, bl = halves(b)
    return mm(ah, bh, dims) + (mm(ah, bl, dims) + mm(al, bh, dims))


def spread_matrix(share, headdim):
    lanes = lax.broadcasted_iota(jnp.int32, (share, share * headdim), 1)
    rows = lax.broadcasted_iota(jnp.int32, (share, share * headdim), 0)
    return (lanes // headdim == rows).astype(BF16)


def spread(values, matrix):
    high, mid, low = thirds(values)
    return mm(high, matrix, TN) + (mm(mid, matrix, TN) + mm(low, matrix, TN))


def head_sums(products, matrix):
    high, low = halves(products)
    return mm(matrix, high, NT) + mm(matrix, low, NT)


def by_triangle(values, triangle):
    high, mid, low = thirds(values)
    return mm(high, triangle, NN) + (mm(mid, triangle, NN) + mm(low, triangle, NN))


def triangle(size, kind):
    rows = lax.broadcasted_iota(jnp.int32, (size, size), 0)
    cols = lax.broadcasted_iota(jnp.int32, (size, size), 1)
    kept = {"upto": rows <= cols, "before": rows < cols, "from": rows >= cols}[kind]
    return kept.astype(BF16)


def doc_start(position, table, docs):
    start = jnp.zeros_like(position)
    first = table[2]
    for i in range(1, docs):
        start = jnp.where(first <= position, first, start)
        first = first + table[2 + i]
    return start


def pack_kernel(s, x_ref, step_ref, *refs, share, inner, state, groups):
    outs, rims, turned = refs[:groups], refs[groups:-1], refs[-1]
    me = s[0]
    tokens = x_ref.shape[0]
    part = inner // groups
    width = part + 2 * state
    turned[...] = step_ref[...].T
    for k in range(groups):
        q = me ^ k
        xs = outs[k]
        xs[:, :part] = x_ref[:, pl.ds(pl.multiple_of(q * part, part), part)]
        xs[:, part : part + state] = x_ref[
            :, pl.ds(pl.multiple_of(inner + q * state, state), state)
        ]
        xs[:, part + state : width] = x_ref[
            :, pl.ds(pl.multiple_of(inner + (groups + q) * state, state), state)
        ]
        rims[k][...] = xs[tokens - 16 :, :width]
        raw = turned[pl.ds(pl.multiple_of(q * share, share), share), :]
        xs[:, width:] = jnp.zeros((tokens, tokens), BF16)
        for i, piece in enumerate(thirds(raw)):
            xs[i * share : (i + 1) * share, width:] = piece


def pack_grad_kernel(s, g_ref, *outs):
    part = outs[0].shape[1]
    for k, out in enumerate(outs):
        q = s[0] ^ k
        out[...] = g_ref[:, pl.ds(pl.multiple_of(q * part, part), part)]


def convolve_pair(s, first, pieces, rim, wx, wb, wc, bx, bb, bc, act_ref, dsl_ref, xall_ref, ext,
                  sizes, docs):
    me, plane = s[0], s[1]
    share, headdim, state = sizes
    part = share * headdim
    width = part + 2 * state
    tokens = pieces[0].shape[0]
    taps = wx.shape[0]
    ext[:8, :] = rim[8:]
    for k, ref in enumerate(pieces):
        place = (me & 1) ^ k
        value = ref[:, :width]
        ext[pl.ds(pl.multiple_of(8 + place * tokens, 8), tokens), :] = value.astype(F32)
        xall_ref[pl.ds(pl.multiple_of(16 + (first + place) * tokens, 16), tokens), :] = value

    for c in range(2):
        chunk = first + c
        pos = plane + chunk * tokens + lax.broadcasted_iota(jnp.int32, (tokens, 1), 0)
        inside = pos - doc_start(pos, s, docs)
        valid = [(inside >= reach).astype(F32) for reach in range(taps)]

        def convolve(lo, w_ref, b_ref, wlo, paired):
            rows = ext[c * tokens : c * tokens + tokens + 8, lo : lo + 128]
            u = jnp.zeros((tokens, 128), F32) + b_ref[:, wlo : wlo + 128]
            for k in range(taps):
                reach = taps - 1 - k
                shifted = rows[8 - reach : 8 - reach + tokens]
                if reach:
                    shifted = shifted * valid[reach]
                u = u + w_ref[k : k + 1, wlo : wlo + 128] * shifted
            sig = 1.0 / (1.0 + jnp.exp(-u))
            value = u * sig
            if paired:
                high, low = halves(value)
                value = high.astype(F32) + low.astype(F32)
            act_ref[chunk, :, lo : lo + 128] = value
            dsl_ref[chunk, :, lo : lo + 128] = sig * (1.0 + u * (1.0 - sig))

        for lo in range(0, part, 128):
            convolve(lo, wx, bx, lo, True)
        for lo in range(0, state, 128):
            convolve(part + lo, wb, bb, lo, False)
            convolve(part + state + lo, wc, bc, lo, False)


def conv_kernel(
    s, x0, x1, r2, r3, wx, wb, wc, bx, bb, bc, act_ref, dsl_ref, xall_ref, ext, *, sizes, docs
):
    rim = r2[...].astype(F32) + r3[...].astype(F32)
    convolve_pair(
        s, s[0] & 2, (x0, x1), rim, wx, wb, wc, bx, bb, bc, act_ref, dsl_ref, xall_ref, ext,
        sizes, docs,
    )

    @pl.when((s[0] & 2) == 0)
    def _():
        xall_ref[:16, :] = rim.astype(BF16)


def conv_state_kernel(
    s, x0, x1, x2, x3, r0, r1, wx, wb, wc, bx, bb, bc, hpar, act_in, dsl_in, xall_in,
    act_ref, dsl_ref, xall_ref, pay_ref, chain_ref, vec_ref,
    ext, raws, *, share, headdim, state, docs,
):
    me = s[0]
    plane = s[1]
    part = share * headdim
    width = part + 2 * state
    tokens = x0.shape[0]
    chunks = 4
    for k, ref in enumerate((x0, x1, x2, x3)):
        block = ref[: 3 * share, width:].astype(F32)
        raws[me ^ k] = block[:share] + block[share : 2 * share] + block[2 * share :]
    upper_chip = (me & 2) == 2
    inner_rim = xall_ref[2 * tokens : 2 * tokens + 16, :].astype(F32)
    rim = jnp.where(upper_chip, r0[...].astype(F32) + r1[...].astype(F32), inner_rim)

    @pl.when(upper_chip)
    def _():
        xall_ref[:16, :] = rim.astype(BF16)

    convolve_pair(
        s, (me & 2) ^ 2, (x2, x3), rim, wx, wb, wc, bx, bb, bc, act_ref, dsl_ref, xall_ref, ext,
        (share, headdim, state), docs,
    )

    bias = hpar[:, 0:1]
    rate = jnp.exp(hpar[:, 1:2])
    upper = triangle(tokens, "upto")
    before = jnp.zeros((share, 1), F32)
    cums, steps, ends = [], [], []
    for c in range(chunks):
        v = raws[c] + bias
        step = jnp.maximum(v, 0.0) + jnp.log1p(jnp.exp(-jnp.abs(v)))
        cum = by_triangle(-step * rate, upper)
        vec_ref[c, STEP] = step
        vec_ref[c, CUM] = cum
        vec_ref[c, SIG] = 1.0 / (1.0 + jnp.exp(-v))
        cums.append(cum)
        steps.append(step)
        ends.append(cum[:, tokens - 1 :])
    total = ends[0] + ends[1] + ends[2] + ends[3]
    last_plane = doc_start(plane + chunks * tokens - 1, s, docs)
    for c in range(chunks):
        base = plane + c * tokens
        pos = base + lax.broadcasted_iota(jnp.int32, (1, tokens), 1)
        start = doc_start(pos, s, docs)
        last = doc_start(base + tokens - 1, s, docs)
        cum, step, end = cums[c], steps[c], ends[c]
        vec_ref[c, TAIL] = jnp.exp(end - cum) * step * (pos >= last).astype(F32)
        vec_ref[c, HEAD] = jnp.exp(cum) * (start < base).astype(F32)
        vec_ref[c, HP] = jnp.exp(cum + before) * (start < plane).astype(F32)
        before = before + end
        vec_ref[c, TP] = (
            jnp.exp(total - before + (end - cum)) * step * (pos >= last_plane).astype(F32)
        )
        open_c = jnp.where(last < base, 1.0, 0.0)
        vec_ref[c, WHOLE] = jnp.broadcast_to(jnp.exp(end) * open_c, (share, tokens))
    matrix = spread_matrix(share, headdim)
    open_plane = jnp.where(last_plane < plane, 1.0, 0.0)
    pay_ref[state:, :] = spread(jnp.broadcast_to(jnp.exp(total) * open_plane, (share, 8)), matrix)

    carried = jnp.zeros((state, part), F32)
    for c in range(chunks):
        chain_ref[c] = carried
        weighted = act_ref[c, :, :part] * spread(vec_ref[c, TAIL], matrix)
        local = dot3(act_ref[c, :, part : part + state], weighted, TN)
        carried = carried * spread(vec_ref[c, WHOLE], matrix) + local
    pay_ref[:state, :] = carried


def grad_state_kernel(
    s, g0, g1, g2, g3, act_ref, vec_ref, pay_in, gall_ref, pay_ref, chain_ref,
    *, share, headdim, state,
):
    me = s[0]
    part = share * headdim
    chunks = 4
    for k, ref in enumerate((g0, g1, g2, g3)):
        gall_ref[me ^ k] = ref[...]
    matrix = spread_matrix(share, headdim)
    carried = jnp.zeros((state, part), F32)
    for c in range(chunks - 1, -1, -1):
        chain_ref[c] = carried
        weighted = gall_ref[c].astype(F32) * spread(vec_ref[c, HEAD], matrix)
        local = dot3(act_ref[c, :, part + state :], weighted, TN)
        carried = carried * spread(vec_ref[c, WHOLE], matrix) + local
    pay_ref[:state, :] = carried
    pay_ref[state:, :] = pay_in[state:, :]


def local_kernel(
    s, act_ref, vec_ref, gall_ref, schain, gchain, *refs, first, share, headdim, state, docs,
):
    y_ref, dx_ref, db_ref, dc_ref, flow_ref, xd_ref, wide, yd, dxd = refs[-9:]
    plane = s[1]
    part = share * headdim
    tokens = act_ref.shape[1]
    matrix = spread_matrix(share, headdim)
    lanes = lax.broadcasted_iota(jnp.int32, (tokens, 2 * headdim), 1)
    left = lanes < headdim
    to_lanes = spread_matrix(share, tokens)
    start_sums = triangle(tokens, "from")
    end_sums = triangle(tokens, "before")

    def chunk(c, carry):
        base = plane + c * tokens
        tpos = base + lax.broadcasted_iota(jnp.int32, (tokens, tokens), 0)
        spos = base + lax.broadcasted_iota(jnp.int32, (tokens, tokens), 1)
        tstart = doc_start(tpos, s, docs)
        mask = jnp.where((spos <= tpos) & (spos >= tstart), 0.0, NEG)
        b = act_ref[c, :, part : part + state]
        cc = act_ref[c, :, part + state :]
        m = dot3(cc, b, NT)
        cum = vec_ref[c, CUM]
        step = vec_ref[c, STEP]
        wide[...] = spread(cum, to_lanes)
        dm = jnp.zeros((tokens, tokens), F32)
        for pair in range(share // 2):
            lo = pair * 2 * headdim
            xp = act_ref[c, :, lo : lo + 2 * headdim]
            gp = gall_ref[c, :, lo : lo + 2 * headdim]
            zero = jnp.zeros_like(gp)
            gst = jnp.concatenate([jnp.where(left, gp, zero), jnp.where(left, zero, gp)], axis=0)
            xh, xl = halves(xp)
            factors = []
            for h in (2 * pair, 2 * pair + 1):
                diff = wide[:, h * tokens : (h + 1) * tokens] - cum[h : h + 1, :]
                factors.append(jnp.exp(diff + mask) * step[h : h + 1, :])
            dw = mm(gst, xh, NT) + mm(gst, xl, NT)
            dm = dm + dw[:tokens] * factors[0] + dw[tokens:] * factors[1]
            w = jnp.concatenate([m * factors[0], m * factors[1]], axis=0)
            wh, wl = halves(w)
            yst = mm(wh, xh, NN) + (mm(wh, xl, NN) + mm(wl, xh, NN) + mm(wl, xl, NN))
            yd[:, lo : lo + 2 * headdim] = jnp.where(left, yst[:tokens], yst[tokens:])
            dxd[:, lo : lo + 2 * headdim] = mm(wh, gst, TN) + mm(wl, gst, TN)
        head_in = spread(vec_ref[c, HEAD], matrix)
        tail = spread(vec_ref[c, TAIL], matrix)
        x = act_ref[c, :, :part]
        g = gall_ref[c].astype(F32)
        y = yd[...] + head_in * dot3(cc, schain[c], NN)
        y_ref[c] = y
        dx_tail = tail * dot3(b, gchain[c], NN)
        near = head_sums(x * dxd[...], matrix)
        away = head_sums(x * dx_tail, matrix)
        dx_ref[c] = dxd[...] + dx_tail
        xd_ref[c] = near + away
        inner = jnp.sum(schain[c] * gchain[c], axis=0, keepdims=True)
        through = head_sums(jnp.broadcast_to(inner, (8, part)), matrix)[:, :1]
        flow_ref[c] = (
            by_triangle(head_sums(g * y, matrix) - near, start_sums)
            + by_triangle(away, end_sums)
            + through * vec_ref[c, WHOLE]
        )
        dc_ref[c] = dot3(dm, b, NN) + dot3(g * head_in, schain[c], NT)
        db_ref[c] = dot3(dm, cc, TN) + dot3(x * tail, gchain[c], NT)
        return carry

    lax.fori_loop(first, first + 2, chunk, 0)


def out_kernel(
    s, one, two, act_ref, y_ref, gall_ref, vec_ref, skip, dcl_ref,
    m0, m1, m2, m3, gy_ref, in_ref, dc_ref, *, share, headdim, state,
):
    me = s[0]
    part = share * headdim
    matrix = spread_matrix(share, headdim)
    arrived = one[:state, :] + one[state : state + 1, :] * two[:state, :]
    in_ref[...] = arrived
    ih, il = halves(arrived)
    for k, out in enumerate((m0, m1, m2, m3)):
        c = me ^ k
        reach = spread(vec_ref[c, HP], matrix)
        ch, cl = halves(act_ref[c, :, part + state :])
        carry = mm(ch, ih, NN) + (mm(ch, il, NN) + mm(cl, ih, NN))
        y = reach * carry
        g = gall_ref[c].astype(F32)
        gy_ref[c] = head_sums(g * y, matrix)
        y = y + y_ref[c]
        out[...] = (y + skip[...] * act_ref[c, :, :part]).astype(BF16)
        gh, gl = halves(g * reach)
        dc_ref[c] = dcl_ref[c] + mm(gh, ih, NT) + (mm(gh, il, NT) + mm(gl, ih, NT))


def back_kernel(
    s, one, two, in_ref, pay, act_ref, dsl_ref, dxl_ref, dbl_ref, dc_ref, gy_ref, flow_ref,
    xd_ref, gall_ref, vec_ref, skip, hpar, xall_ref, du_ref, par_ref, gs_ref,
    *, share, headdim, state, docs, taps,
):
    plane = s[1]
    part = share * headdim
    tokens = act_ref.shape[1]
    chunks = 4
    matrix = spread_matrix(share, headdim)
    adjoint = one[:state, :] + one[state : state + 1, :] * two[:state, :]
    inner = jnp.sum(adjoint * in_ref[...], axis=0, keepdims=True) * pay[state : state + 1, :]
    through = head_sums(jnp.broadcast_to(inner, (8, part)), matrix)[:, :1]
    ah, al = halves(adjoint)
    rate = jnp.exp(hpar[:, 1:2])
    start_sums = triangle(tokens, "from")
    end_sums = triangle(tokens, "before")
    away = []
    g_bias = jnp.zeros((share, 1), F32)
    g_decay = jnp.zeros((share, 1), F32)
    g_skip = jnp.zeros((share, 1), F32)
    for c in range(chunks):
        x = act_ref[c, :, :part]
        g = gall_ref[c].astype(F32)
        tail = spread(vec_ref[c, TP], matrix)
        bh, bl = halves(act_ref[c, :, part : part + state])
        dx = tail * (mm(bh, ah, NN) + (mm(bh, al, NN) + mm(bl, ah, NN)))
        away.append(head_sums(x * dx, matrix))
        dx = dx + dxl_ref[c]
        xh, xl = halves(x * tail)
        db = dbl_ref[c] + mm(xh, ah, NT) + (mm(xh, al, NT) + mm(xl, ah, NT))
        du_ref[c * tokens : (c + 1) * tokens, :part] = (dx + skip[...] * g) * dsl_ref[c, :, :part]
        du_ref[c * tokens : (c + 1) * tokens, part : part + state] = (
            db * dsl_ref[c, :, part : part + state]
        )
        du_ref[c * tokens : (c + 1) * tokens, part + state :] = (
            dc_ref[c] * dsl_ref[c, :, part + state :]
        )
        g_skip = g_skip + jnp.sum(head_sums(g * x, matrix), axis=1, keepdims=True)
    for c in range(chunks):
        flow = (
            flow_ref[c] + by_triangle(gy_ref[c], start_sums) + by_triangle(away[c], end_sums)
        ) + through
        for d in range(chunks):
            if d > c:
                flow = flow + jnp.sum(gy_ref[d], axis=1, keepdims=True)
            if d < c:
                flow = flow + jnp.sum(away[d], axis=1, keepdims=True)
        step = vec_ref[c, STEP]
        grad_step = ((xd_ref[c] + away[c]) / step - rate * flow) * vec_ref[c, SIG]
        gs_ref[c] = grad_step
        g_bias = g_bias + jnp.sum(grad_step, axis=1, keepdims=True)
        g_decay = g_decay - rate * jnp.sum(flow * step, axis=1, keepdims=True)
    lane = lax.broadcasted_iota(jnp.int32, (share, 128), 1)
    heads = jnp.where(lane == 0, g_bias, jnp.where(lane == 1, g_decay, g_skip))
    width = part + 2 * state
    par_ref[...] = jnp.zeros_like(par_ref)
    par_ref[:, width : width + 128] = heads[:8]
    par_ref[:, width + 128 :] = heads[8:]
    for lo in range(0, width, 128):
        sums = [jnp.zeros((8, 128), F32) for _ in range(taps + 1)]
        for c in range(chunks):
            rows = xall_ref[c * tokens : c * tokens + tokens + 16, lo : lo + 128].astype(F32)
            pos = plane + c * tokens + lax.broadcasted_iota(jnp.int32, (tokens, 1), 0)
            inside = pos - doc_start(pos, s, docs)
            du = du_ref[c * tokens : (c + 1) * tokens, lo : lo + 128]
            for k in range(taps):
                reach = taps - 1 - k
                shifted = rows[16 - reach : 16 - reach + tokens]
                if reach:
                    shifted = shifted * (inside >= reach).astype(F32)
                sums[k] = sums[k] + jnp.sum((du * shifted).reshape(tokens // 8, 8, 128), axis=0)
            sums[taps] = sums[taps] + jnp.sum(du.reshape(tokens // 8, 8, 128), axis=0)
        for k in range(taps + 1):
            par_ref[k : k + 1, lo : lo + 128] = jnp.sum(sums[k], axis=0, keepdims=True)


def conv_back_kernel(
    s, du_ref, rim_ref, wx, wb, wc, gs_ref, o0, o1, o2, o3, ext,
    *, share, headdim, state, docs, taps,
):
    me = s[0]
    plane = s[1]
    part = share * headdim
    width = part + 2 * state
    tokens = o0.shape[0]
    chunks = 4
    ext[: chunks * tokens, :] = du_ref[...]
    ext[chunks * tokens :, :] = rim_ref[...]
    for k, out in enumerate((o0, o1, o2, o3)):
        c = me ^ k
        pos = plane + c * tokens + lax.broadcasted_iota(jnp.int32, (tokens, 1), 0)
        valid = []
        for reach in range(1, taps):
            ahead = pos + reach
            valid.append((ahead - doc_start(ahead, s, docs) >= reach).astype(F32))
        first = pl.multiple_of(c * tokens, tokens)
        for lo in range(0, width, 128):
            rows = ext[pl.ds(first, tokens + 8), lo : lo + 128]
            if lo < part:
                w = wx[:, lo : lo + 128]
            elif lo < part + state:
                w = wb[:, lo - part : lo - part + 128]
            else:
                w = wc[:, lo - part - state : lo - part - state + 128]
            total = w[taps - 1 : taps] * rows[:tokens]
            for reach in range(1, taps):
                k_tap = taps - 1 - reach
                total = total + w[k_tap : k_tap + 1] * (
                    rows[reach : reach + tokens] * valid[reach - 1]
                )
            out[:, lo : lo + 128] = total.astype(BF16)
        out[:, width:] = jnp.zeros((tokens, tokens), BF16)
        for i, piece in enumerate(thirds(gs_ref[c])):
            out[i * share : (i + 1) * share, width:] = piece


def join_kernel(s, p0, p1, p2, p3, out_ref):
    part = p0.shape[1]
    for k, ref in enumerate((p0, p1, p2, p3)):
        q = s[0] ^ k
        out_ref[:, pl.ds(pl.multiple_of(q * part, part), part)] = ref[...]


def join_grad_kernel(s, p0, p1, p2, p3, out_ref, gs_ref, turned, *, share, inner, state, groups):
    part = inner // groups
    for k, ref in enumerate((p0, p1, p2, p3)):
        q = s[0] ^ k
        out_ref[:, pl.ds(pl.multiple_of(q * part, part), part)] = ref[:, :part]
        out_ref[:, pl.ds(pl.multiple_of(inner + q * state, state), state)] = ref[
            :, part : part + state
        ]
        out_ref[:, pl.ds(pl.multiple_of(inner + (groups + q) * state, state), state)] = ref[
            :, part + state : part + 2 * state
        ]
        block = ref[: 3 * share, part + 2 * state :].astype(F32)
        turned[pl.ds(pl.multiple_of(q * share, share), share), :] = (
            block[:share] + block[share : 2 * share] + block[2 * share :]
        )
    gs_ref[...] = turned[...].T


def join_params_kernel(
    s, p0, p1, p2, p3, conv_ref, head_ref, turned, *, share, inner, state, groups, scale
):
    part = inner // groups
    width = part + 2 * state
    rows = conv_ref.shape[0]
    for k, ref in enumerate((p0, p1, p2, p3)):
        q = s[0] ^ k
        conv_ref[:, pl.ds(pl.multiple_of(q * part, part), part)] = ref[:rows, :part] * scale
        conv_ref[:, pl.ds(pl.multiple_of(inner + q * state, state), state)] = (
            ref[:rows, part : part + state] * scale
        )
        conv_ref[:, pl.ds(pl.multiple_of(inner + (groups + q) * state, state), state)] = (
            ref[:rows, part + state : width] * scale
        )
        turned[pl.ds(pl.multiple_of(q * share, 8), 8), :] = ref[:, width : width + 128]
        turned[pl.ds(pl.multiple_of(q * share + 8, 8), 8), :] = ref[:, width + 128 :]
    head_ref[...] = turned[...].T[: head_ref.shape[0], :] * scale


def call(kernel, table, operands, specs, outs, scratch=(), name=None, vmem=True, aliases=None):
    here = pl.BlockSpec(memory_space=pltpu.VMEM)
    in_specs = [here if spec is None else spec for spec in specs]
    return pl.pallas_call(
        kernel,
        out_shape=[
            pltpu.VMEM(shape, kind) if vmem else jax.ShapeDtypeStruct(shape, kind)
            for shape, kind in outs
        ],
        grid_spec=pltpu.PrefetchScalarGridSpec(
            num_scalar_prefetch=1,
            grid=(1,),
            in_specs=in_specs,
            out_specs=[here] * len(outs),
            scratch_shapes=[pltpu.VMEM(shape, kind) for shape, kind in scratch],
        ),
        compiler_params=pltpu.CompilerParams(vmem_limit_bytes=LIMIT),
        name=name,
        input_output_aliases=aliases or {},
    )(table, *operands)


def swapped(value, bits):
    count = lax.axis_size("ctx")
    return lax.ppermute(value, "ctx", [(i, i ^ bits) for i in range(count)])


def shifted(value, steps):
    count = lax.axis_size("ctx")
    pairs = [(i, i + steps) for i in range(count) if 0 <= i + steps < count]
    return lax.ppermute(value, "ctx", pairs)


def after(value, *others):
    return lax.optimization_barrier((value, *others))[0]


def near_of(payload, state, direction, planes):
    near = shifted(payload, direction * GROUPS)
    covered, window = 1, planes // 2
    while 2 * covered < window:
        far = shifted(near, direction * GROUPS * covered)
        factor = near[state : state + 1]
        near = jnp.concatenate(
            [near[:state] + factor * far[:state], near[state:] * far[state:]], axis=0
        )
        covered *= 2
    return near, covered


def body(
    conv_input, step_raw, step_bias, decay_log, skip_gain, conv_weight, conv_bias, doc_lengths,
    grad_out,
):
    tokens, channels = conv_input.shape
    heads = step_raw.shape[1]
    taps = conv_weight.shape[0]
    inner = grad_out.shape[1]
    headdim = inner // heads
    groups = GROUPS
    share = heads // groups
    state = (channels - inner) // (2 * groups)
    part = inner // groups
    width = part + 2 * state
    docs = doc_lengths.shape[0]
    devices = lax.axis_size("ctx")
    planes = devices // groups
    me = lax.axis_index("ctx")
    sizes = dict(share=share, headdim=headdim, state=state)
    table = jnp.concatenate(
        [
            jnp.stack([me % groups, (me // groups) * (groups * tokens)]).astype(jnp.int32),
            doc_lengths,
        ]
    )
    hpar = jnp.pad(
        jnp.stack([step_bias, decay_log, skip_gain], axis=1), ((0, 0), (0, 128 - 3))
    )
    skips = jnp.repeat(skip_gain, headdim)[None, :]
    bias_row = conv_bias[None, :]
    hpar_spec = pl.BlockSpec((share, 128), lambda i, s: (s[0], 0))
    skip_spec = pl.BlockSpec((1, part), lambda i, s: (0, s[0]))
    b_first = inner // state

    def column_specs(rows):
        return [
            pl.BlockSpec((rows, part), lambda i, s: (0, s[0])),
            pl.BlockSpec((rows, state), lambda i, s: (0, b_first + s[0])),
            pl.BlockSpec((rows, state), lambda i, s: (0, b_first + groups + s[0])),
        ]

    shapes = dict(share=share, inner=inner, state=state, groups=groups)
    packed = call(
        functools.partial(pack_kernel, **shapes),
        table,
        [conv_input, step_raw],
        [None] * 2,
        [((tokens, width + tokens), BF16)] * groups + [((16, width), BF16)] * groups,
        [((heads, tokens), F32)],
        name="pack",
    )
    xs, edges = packed[:groups], packed[groups:]
    gs = call(
        pack_grad_kernel, table, [grad_out], [None], [((tokens, part), BF16)] * groups,
        name="pack_grad",
    )
    xr = [xs[0]] + [swapped(xs[k], k) for k in range(1, groups)]
    rims = []
    for k in range(groups):
        pairs = []
        for i in range(devices):
            source = i - 1 - i % 2 if k >= 2 else i - 1 - i % groups
            if source >= 0 and (source % groups) ^ (i % groups) == k:
                pairs.append((source, i))
        rims.append(lax.ppermute(edges[k], "ctx", pairs))
    gr = [gs[0]] + [swapped(gs[k], k) for k in range(1, groups)]
    conv_shapes = [
        ((groups, tokens, width), F32),
        ((groups, tokens, width), F32),
        ((groups * tokens + 16, width), BF16),
    ]
    conv_specs = column_specs(taps) + column_specs(1)
    conv_params = [conv_weight] * 3 + [bias_row] * 3
    ext_shape = ((2 * tokens + 8, width), F32)
    act, dsl, xall = call(
        functools.partial(conv_kernel, docs=docs, sizes=(share, headdim, state)),
        table,
        [xr[0], xr[1], rims[2], rims[3]] + conv_params,
        [None] * 4 + conv_specs,
        conv_shapes,
        [ext_shape],
        name="conv",
    )
    act, dsl, xall, spay, schain, vec = call(
        functools.partial(conv_state_kernel, docs=docs, **sizes),
        table,
        xr + rims[:2] + conv_params + [hpar, act, dsl, xall],
        [None] * 6 + conv_specs + [hpar_spec] + [None] * 3,
        conv_shapes
        + [
            ((state + 8, part), F32),
            ((groups, state, part), F32),
            ((groups, 8, share, tokens), F32),
        ],
        [ext_shape, ((groups, share, tokens), F32)],
        name="conv_state",
        aliases={14: 0, 15: 1, 16: 2},
    )
    s_near, covered = near_of(spay, state, 1, planes)
    gall, gpay, gchain = call(
        functools.partial(grad_state_kernel, **sizes),
        table,
        gr + [act, vec, spay],
        [None] * 7,
        [
            ((groups, tokens, part), BF16),
            ((state + 8, part), F32),
            ((groups, state, part), F32),
        ],
        name="grad_state",
    )
    g_near, _ = near_of(gpay, state, -1, planes)
    local_shapes = [
        ((groups, tokens, part), F32),
        ((groups, tokens, part), F32),
        ((groups, tokens, state), F32),
        ((groups, tokens, state), F32),
        ((groups, share, tokens), F32),
        ((groups, share, tokens), F32),
    ]
    locals_ = []
    for first in (0, 2):
        locals_ = call(
            functools.partial(local_kernel, first=first, docs=docs, **sizes),
            table,
            [act, vec, gall, schain, gchain] + list(locals_),
            [None] * (5 + len(locals_)),
            local_shapes,
            [((tokens, share * tokens), F32)] + [((tokens, part), F32)] * 2,
            name="local",
            aliases={6 + i: i for i in range(len(locals_))},
        )
        if first == 0:
            s_far = shifted(after(s_near, locals_[4]), GROUPS * covered)
        else:
            g_far = shifted(after(g_near, locals_[4]), -GROUPS * covered)
    y_local, dx_local, db_local, dc_local, flow, xd = locals_
    *mixed, gy, state_in, dc = call(
        functools.partial(out_kernel, **sizes),
        table,
        [s_near, s_far, act, y_local, gall, vec, skips, dc_local],
        [None] * 6 + [skip_spec, None],
        [((tokens, part), BF16)] * groups
        + [
            ((groups, share, tokens), F32),
            ((state, part), F32),
            ((groups, tokens, state), F32),
        ],
        name="out",
    )
    mr = [mixed[0]] + [swapped(mixed[k], k) for k in range(1, groups)]
    du, params, grad_steps = call(
        functools.partial(back_kernel, docs=docs, taps=taps, **sizes),
        table,
        [g_near, g_far, state_in, spay, act, dsl, dx_local, db_local, dc, gy, flow, xd, gall, vec,
         skips, hpar, xall],
        [None] * 14 + [skip_spec, hpar_spec, None],
        [
            ((groups * tokens, width), F32),
            ((8, width + 256), F32),
            ((groups, share, tokens), F32),
        ],
        name="back",
    )
    rim_back = shifted(du[:8], -groups)
    rim_back, *mr = lax.optimization_barrier((rim_back, *mr))
    back = call(
        functools.partial(conv_back_kernel, docs=docs, taps=taps, **sizes),
        table,
        [du, rim_back] + [conv_weight] * 3 + [grad_steps],
        [None] * 2 + column_specs(taps) + [None],
        [((tokens, width + tokens), BF16)] * groups,
        [((groups * tokens + 8, width), F32)],
        name="conv_back",
    )
    br = [back[0]] + [swapped(back[k], k) for k in range(1, groups)]
    params = after(params, back[1])
    step = groups
    while step < devices:
        params = params + swapped(params, step)
        step *= 2
    pr = [params] + [swapped(params, k) for k in range(1, groups)]
    (mixer_out,) = call(
        join_kernel, table, mr, [None] * groups, [((tokens, inner), BF16)], name="join_out",
        vmem=False,
    )
    grad_conv, grad_heads = call(
        functools.partial(join_params_kernel, scale=(tokens * devices) ** (-0.5), **shapes),
        table,
        pr,
        [None] * groups,
        [((taps + 1, channels), F32), ((3, heads), F32)],
        [((heads, 128), F32)],
        name="join_params",
        vmem=False,
    )
    grad_input, grad_step = call(
        functools.partial(join_grad_kernel, **shapes),
        table,
        br,
        [None] * groups,
        [((tokens, channels), BF16), ((tokens, heads), F32)],
        [((heads, tokens), F32)],
        name="join_grad",
        vmem=False,
    )
    return mixer_out, grad_input, grad_step, grad_conv, grad_heads


def solution(mesh):
    rows = P(("groups", "ctx"), None)
    return jax.shard_map(
        body,
        mesh=mesh,
        in_specs=(rows, rows, P(), P(), P(), P(), P(), P("groups"), rows),
        out_specs=(rows, rows, rows, P("groups", None), P("groups", None)),
        check_vma=False,
    )
```

```python
import functools

import jax
import jax.numpy as jnp
from jax import lax
from jax.experimental import pallas as pl
from jax.experimental.pallas import tpu as pltpu
from jax.sharding import PartitionSpec as P

GROUPS = 4
F32 = jnp.float32
BF16 = jnp.bfloat16
NEG = -1e30
LIMIT = 12 * 1024 * 1024
STEP, CUM, TAIL, HEAD, TP, HP, WHOLE, SIG = range(8)

NN = (((1,), (0,)), ((), ()))
NT = (((1,), (1,)), ((), ()))
TN = (((0,), (0,)), ((), ()))


def mm(a, b, dims):
    return lax.dot_general(a, b, dims, preferred_element_type=F32)


def halves(a):
    high = a.astype(BF16)
    return high, (a - high.astype(F32)).astype(BF16)


def thirds(a):
    high = a.astype(BF16)
    rest = a - high.astype(F32)
    mid = rest.astype(BF16)
    return high, mid, (rest - mid.astype(F32)).astype(BF16)


def dot3(a, b, dims):
    return joined3(halves(a), halves(b), dims)


def joined3(a, b, dims):
    (ah, al), (bh, bl) = a, b
    (left,), (right,) = dims[0]
    if ah.shape[left] > 128:
        return mm(ah, bh, dims) + (mm(ah, bl, dims) + mm(al, bh, dims))
    both = mm(
        jnp.concatenate([ah, al], axis=left), jnp.concatenate([bh, bh], axis=right), dims
    )
    return both + mm(ah, bl, dims)


def spread_matrix(share, headdim):
    lanes = lax.broadcasted_iota(jnp.int32, (share, share * headdim), 1)
    rows = lax.broadcasted_iota(jnp.int32, (share, share * headdim), 0)
    return (lanes // headdim == rows).astype(BF16)


def spread(values, matrix):
    return mm(
        jnp.concatenate(thirds(values), axis=0), jnp.concatenate([matrix] * 3, axis=0), TN
    )


def skip_row(hpar, matrix):
    return spread(jnp.broadcast_to(hpar[:, 2:3], (hpar.shape[0], 8)), matrix)[:1]


def head_sums(products, matrix):
    high, low = halves(products)
    return mm(matrix, high, NT) + mm(matrix, low, NT)


def by_triangle(values, triangle):
    high, mid, low = thirds(values)
    return mm(high, triangle, NN) + (mm(mid, triangle, NN) + mm(low, triangle, NN))


def triangle(size, kind):
    rows = lax.broadcasted_iota(jnp.int32, (size, size), 0)
    cols = lax.broadcasted_iota(jnp.int32, (size, size), 1)
    kept = {"upto": rows <= cols, "before": rows < cols, "from": rows >= cols}[kind]
    return kept.astype(BF16)


def doc_start(position, table, docs):
    start = jnp.zeros_like(position)
    first = table[2]
    for i in range(1, docs):
        start = jnp.where(first <= position, first, start)
        first = first + table[2 + i]
    return start


def pack_kernel(s, x_ref, step_ref, *refs, share, inner, state, groups):
    outs, rims = refs[:groups], refs[groups:]
    me = s[0]
    tokens = x_ref.shape[0]
    part = inner // groups
    width = part + 2 * state
    for k in range(groups):
        q = me ^ k
        xs = outs[k]
        xs[:, :part] = x_ref[:, pl.ds(pl.multiple_of(q * part, part), part)]
        xs[:, part : part + state] = x_ref[
            :, pl.ds(pl.multiple_of(inner + q * state, state), state)
        ]
        xs[:, part + state : width] = x_ref[
            :, pl.ds(pl.multiple_of(inner + (groups + q) * state, state), state)
        ]
        rims[k][...] = xs[tokens - 16 :, :width]
        raw = step_ref[pl.ds(pl.multiple_of(q * share, share), share), :]
        xs[:, width:] = jnp.zeros((tokens, tokens), BF16)
        for i, piece in enumerate(thirds(raw)):
            xs[i * share : (i + 1) * share, width:] = piece


def pack_grad_kernel(s, g_ref, bias, decay, skip, *refs, groups):
    outs, hpar, wide, turned = refs[:groups], *refs[groups:]
    heads = bias.shape[1]
    share = heads // groups
    wide[...] = jnp.zeros_like(wide)
    for i, ref in enumerate((bias, decay, skip)):
        wide[i : i + 1, :heads] = ref[...]
    turned[...] = wide[...].T
    hpar[...] = turned[pl.ds(pl.multiple_of(s[0] * share, share), share), :]
    part = outs[0].shape[1]
    for k, out in enumerate(outs):
        q = s[0] ^ k
        out[...] = g_ref[:, pl.ds(pl.multiple_of(q * part, part), part)]


def activate(rows, weight, bias, valid, paired):
    taps = weight.shape[0]
    tokens = rows.shape[0] - 8
    u = jnp.zeros((tokens, rows.shape[1]), F32) + bias
    for k in range(taps):
        reach = taps - 1 - k
        moved = rows[8 - reach : 8 - reach + tokens]
        if reach:
            moved = moved * valid[reach]
        u = u + weight[k : k + 1] * moved
    sig = 1.0 / (1.0 + jnp.exp(-u))
    value = u * sig
    if paired:
        high, low = halves(value)
        value = high.astype(F32) + low.astype(F32)
    return value, sig * (1.0 + u * (1.0 - sig))


def convolve_head(s, first, rim, wx, wb, wc, bx, bb, bc, act_ref, dsl_ref, xall_ref, sizes, docs):
    share, headdim, state = sizes
    part = share * headdim
    tokens = act_ref.shape[1]
    pos = s[1] + first * tokens + lax.broadcasted_iota(jnp.int32, (8, 1), 0)
    inside = pos - doc_start(pos, s, docs)
    valid = [(inside >= reach).astype(F32) for reach in range(wx.shape[0])]
    own = xall_ref[pl.ds(pl.multiple_of(16 + first * tokens, 16), 16), :].astype(F32)
    rows = jnp.concatenate([rim[8:], own[:8]], axis=0)
    for lo, size, w_ref, b_ref in (
        (0, part, wx, bx), (part, state, wb, bb), (part + state, state, wc, bc)
    ):
        value, slope = activate(rows[:, lo : lo + size], w_ref[...], b_ref[...], valid, lo == 0)
        act_ref[first, :8, lo : lo + size] = value
        dsl_ref[first, :8, lo : lo + size] = slope


def convolve_pair(s, first, pieces, rim, wx, wb, wc, bx, bb, bc, act_ref, dsl_ref, xall_ref, ext,
                  sizes, docs):
    me, plane = s[0], s[1]
    share, headdim, state = sizes
    part = share * headdim
    width = part + 2 * state
    tokens = pieces[0].shape[0]
    taps = wx.shape[0]
    ext[:8, :] = rim[8:]
    for k, ref in enumerate(pieces):
        place = (me & 1) ^ k
        value = ref[:, :width]
        ext[pl.ds(pl.multiple_of(8 + place * tokens, 8), tokens), :] = value.astype(F32)
        xall_ref[pl.ds(pl.multiple_of(16 + (first + place) * tokens, 16), tokens), :] = value

    for c in range(2):
        chunk = first + c
        pos = plane + chunk * tokens + lax.broadcasted_iota(jnp.int32, (tokens, 1), 0)
        inside = pos - doc_start(pos, s, docs)
        valid = [(inside >= reach).astype(F32) for reach in range(taps)]

        def convolve(lo, w_ref, b_ref, wlo, paired):
            rows = ext[c * tokens : c * tokens + tokens + 8, lo : lo + 128]
            value, slope = activate(
                rows, w_ref[:, wlo : wlo + 128], b_ref[:, wlo : wlo + 128], valid, paired
            )
            act_ref[chunk, :, lo : lo + 128] = value
            dsl_ref[chunk, :, lo : lo + 128] = slope

        for lo in range(0, part, 128):
            convolve(lo, wx, bx, lo, True)
        for lo in range(0, state, 128):
            convolve(part + lo, wb, bb, lo, False)
            convolve(part + state + lo, wc, bc, lo, False)


def conv_kernel(
    s, x0, x1, wx, wb, wc, bx, bb, bc, act_ref, dsl_ref, xall_ref, ext, *, sizes, docs
):
    rim = jnp.zeros((16, ext.shape[1]), F32)
    convolve_pair(
        s, s[0] & 2, (x0, x1), rim, wx, wb, wc, bx, bb, bc, act_ref, dsl_ref, xall_ref, ext,
        sizes, docs,
    )


def conv_state_kernel(
    s, x0, x1, x2, x3, r0, r1, r2, r3, wx, wb, wc, bx, bb, bc, hpar, act_in, dsl_in, xall_in,
    act_ref, dsl_ref, xall_ref, pay_ref, chain_ref, vec_ref,
    ext, raws, *, share, headdim, state, docs,
):
    me = s[0]
    plane = s[1]
    part = share * headdim
    width = part + 2 * state
    tokens = x0.shape[0]
    chunks = 4
    for k, ref in enumerate((x0, x1, x2, x3)):
        block = ref[: 3 * share, width:].astype(F32)
        raws[me ^ k] = block[:share] + block[share : 2 * share] + block[2 * share :]
    upper_chip = (me & 2) == 2
    inner_rim = xall_ref[2 * tokens : 2 * tokens + 16, :].astype(F32)
    rim = jnp.where(upper_chip, r0[...].astype(F32) + r1[...].astype(F32), inner_rim)

    own_rim = r2[...].astype(F32) + r3[...].astype(F32)
    xall_ref[:16, :] = jnp.where(upper_chip, rim, own_rim).astype(BF16)
    convolve_head(
        s, me & 2, own_rim, wx, wb, wc, bx, bb, bc, act_ref, dsl_ref, xall_ref,
        (share, headdim, state), docs,
    )
    convolve_pair(
        s, (me & 2) ^ 2, (x2, x3), rim, wx, wb, wc, bx, bb, bc, act_ref, dsl_ref, xall_ref, ext,
        (share, headdim, state), docs,
    )

    bias = hpar[:, 0:1]
    rate = jnp.exp(hpar[:, 1:2])
    upper = triangle(tokens, "upto")
    before = jnp.zeros((share, 1), F32)
    cums, steps, ends = [], [], []
    for c in range(chunks):
        v = raws[c] + bias
        step = jnp.maximum(v, 0.0) + jnp.log1p(jnp.exp(-jnp.abs(v)))
        cum = by_triangle(-step * rate, upper)
        vec_ref[c, STEP] = step
        vec_ref[c, CUM] = cum
        vec_ref[c, SIG] = 1.0 / (1.0 + jnp.exp(-v))
        cums.append(cum)
        steps.append(step)
        ends.append(cum[:, tokens - 1 :])
    total = ends[0] + ends[1] + ends[2] + ends[3]
    last_plane = doc_start(plane + chunks * tokens - 1, s, docs)
    for c in range(chunks):
        base = plane + c * tokens
        pos = base + lax.broadcasted_iota(jnp.int32, (1, tokens), 1)
        start = doc_start(pos, s, docs)
        last = doc_start(base + tokens - 1, s, docs)
        cum, step, end = cums[c], steps[c], ends[c]
        vec_ref[c, TAIL] = jnp.exp(end - cum) * step * (pos >= last).astype(F32)
        vec_ref[c, HEAD] = jnp.exp(cum) * (start < base).astype(F32)
        vec_ref[c, HP] = jnp.exp(cum + before) * (start < plane).astype(F32)
        before = before + end
        vec_ref[c, TP] = (
            jnp.exp(total - before + (end - cum)) * step * (pos >= last_plane).astype(F32)
        )
        open_c = jnp.where(last < base, 1.0, 0.0)
        vec_ref[c, WHOLE] = jnp.broadcast_to(jnp.exp(end) * open_c, (share, tokens))
    matrix = spread_matrix(share, headdim)
    open_plane = jnp.where(last_plane < plane, 1.0, 0.0)
    pay_ref[state:, :] = spread(jnp.broadcast_to(jnp.exp(total) * open_plane, (share, 8)), matrix)

    carried = jnp.zeros((state, part), F32)
    for c in range(chunks):
        chain_ref[c] = carried
        weighted = act_ref[c, :, :part] * spread(vec_ref[c, TAIL], matrix)
        local = dot3(act_ref[c, :, part : part + state], weighted, TN)
        carried = carried * spread(vec_ref[c, WHOLE], matrix) + local
    pay_ref[:state, :] = carried


def grad_state_kernel(
    s, g0, g1, g2, g3, act_ref, vec_ref, pay_in, gall_ref, pay_ref, chain_ref,
    *, share, headdim, state,
):
    me = s[0]
    part = share * headdim
    chunks = 4
    for k, ref in enumerate((g0, g1, g2, g3)):
        gall_ref[me ^ k] = ref[...]
    matrix = spread_matrix(share, headdim)
    carried = jnp.zeros((state, part), F32)
    for c in range(chunks - 1, -1, -1):
        chain_ref[c] = carried
        weighted = gall_ref[c].astype(F32) * spread(vec_ref[c, HEAD], matrix)
        local = dot3(act_ref[c, :, part + state :], weighted, TN)
        carried = carried * spread(vec_ref[c, WHOLE], matrix) + local
    pay_ref[:state, :] = carried
    pay_ref[state:, :] = pay_in[state:, :]


def local_kernel(
    s, act_ref, vec_ref, gall_ref, schain, gchain, *refs, span, share, headdim, state, docs,
):
    y_ref, dx_ref, db_ref, dc_ref, flow_ref, xd_ref, wide, yd, dxd = refs[-9:]
    plane = s[1]
    part = share * headdim
    tokens = act_ref.shape[1]
    matrix = spread_matrix(share, headdim)
    lanes = lax.broadcasted_iota(jnp.int32, (tokens, 2 * headdim), 1)
    left = lanes < headdim
    to_lanes = spread_matrix(share, tokens)
    start_sums = triangle(tokens, "from")
    end_sums = triangle(tokens, "before")

    def chunk(c, carry):
        base = plane + c * tokens
        tpos = base + lax.broadcasted_iota(jnp.int32, (tokens, tokens), 0)
        spos = base + lax.broadcasted_iota(jnp.int32, (tokens, tokens), 1)
        tstart = doc_start(tpos, s, docs)
        mask = jnp.where((spos <= tpos) & (spos >= tstart), 0.0, NEG)
        b = act_ref[c, :, part : part + state]
        cc = act_ref[c, :, part + state :]
        m = dot3(cc, b, NT)
        cum = vec_ref[c, CUM]
        step = vec_ref[c, STEP]
        wide[...] = spread(cum, to_lanes)
        dm = jnp.zeros((tokens, tokens), F32)
        for pair in range(share // 2):
            lo = pair * 2 * headdim
            xp = act_ref[c, :, lo : lo + 2 * headdim]
            gp = gall_ref[c, :, lo : lo + 2 * headdim]
            zero = jnp.zeros_like(gp)
            gst = jnp.concatenate([jnp.where(left, gp, zero), jnp.where(left, zero, gp)], axis=0)
            xh, xl = halves(xp)
            factors = []
            for h in (2 * pair, 2 * pair + 1):
                diff = wide[:, h * tokens : (h + 1) * tokens] - cum[h : h + 1, :]
                factors.append(jnp.exp(diff + mask) * step[h : h + 1, :])
            pieces = jnp.concatenate([xh, xl], axis=1)
            dw = mm(jnp.concatenate([gst, gst], axis=1), pieces, NT)
            dm = dm + dw[:tokens] * factors[0] + dw[tokens:] * factors[1]
            w = jnp.concatenate([m * factors[0], m * factors[1]], axis=0)
            w = jnp.concatenate(halves(w), axis=1)
            yst = mm(w, jnp.concatenate([pieces, pieces], axis=0), NN)
            yst = yst[:, : 2 * headdim] + yst[:, 2 * headdim :]
            yd[:, lo : lo + 2 * headdim] = jnp.where(left, yst[:tokens], yst[tokens:])
            dst = mm(w, gst, TN)
            dxd[:, lo : lo + 2 * headdim] = dst[:tokens] + dst[tokens:]
        head_in = spread(vec_ref[c, HEAD], matrix)
        tail = spread(vec_ref[c, TAIL], matrix)
        x = act_ref[c, :, :part]
        g = gall_ref[c].astype(F32)
        y = yd[...] + head_in * dot3(cc, schain[c], NN)
        y_ref[c] = y
        dx_tail = tail * dot3(b, gchain[c], NN)
        near = head_sums(x * dxd[...], matrix)
        away = head_sums(x * dx_tail, matrix)
        dx_ref[c] = dxd[...] + dx_tail
        xd_ref[c] = near + away
        inner = jnp.sum(schain[c] * gchain[c], axis=0, keepdims=True)
        through = head_sums(jnp.broadcast_to(inner, (8, part)), matrix)[:, :1]
        flow_ref[c] = (
            by_triangle(head_sums(g * y, matrix) - near, start_sums)
            + by_triangle(away, end_sums)
            + through * vec_ref[c, WHOLE]
        )
        dc_ref[c] = dot3(dm, b, NN) + dot3(g * head_in, schain[c], NT)
        db_ref[c] = dot3(dm, cc, TN) + dot3(x * tail, gchain[c], NT)
        return carry

    lax.fori_loop(*span, chunk, 0)


def out_kernel(
    s, one, two, act_ref, y_ref, gall_ref, vec_ref, hpar, dcl_ref,
    m0, m1, m2, m3, gy_ref, in_ref, dc_ref, *, share, headdim, state,
):
    me = s[0]
    part = share * headdim
    matrix = spread_matrix(share, headdim)
    arrived = one[:state, :] + one[state : state + 1, :] * two[:state, :]
    in_ref[...] = arrived
    ih, il = halves(arrived)
    skip = skip_row(hpar, matrix)
    for k, out in enumerate((m0, m1, m2, m3)):
        c = me ^ k
        reach = spread(vec_ref[c, HP], matrix)
        ch, cl = halves(act_ref[c, :, part + state :])
        carry = joined3((ch, cl), (ih, il), NN)
        y = reach * carry
        g = gall_ref[c].astype(F32)
        gy_ref[c] = head_sums(g * y, matrix)
        y = y + y_ref[c]
        out[...] = (y + skip * act_ref[c, :, :part]).astype(BF16)
        gh, gl = halves(g * reach)
        dc_ref[c] = dcl_ref[c] + mm(gh, ih, NT) + (mm(gh, il, NT) + mm(gl, ih, NT))


def input_grads(c, rows, high, low, act_ref, dsl_ref, dxl_ref, dbl_ref, dc_ref, gall_ref, vec_ref,
                skip, matrix, part, state):
    x = act_ref[c, :rows, :part]
    g = gall_ref[c, :rows].astype(F32)
    tail = spread(vec_ref[c, TP][:, :rows], matrix)
    bh, bl = halves(act_ref[c, :rows, part : part + state])
    far = tail * joined3((bh, bl), (high, low), NN)
    xh, xl = halves(x * tail)
    db = dbl_ref[c, :rows] + mm(xh, high, NT) + (mm(xh, low, NT) + mm(xl, high, NT))
    dx = far + dxl_ref[c, :rows] + skip * g
    return (
        dx * dsl_ref[c, :rows, :part],
        db * dsl_ref[c, :rows, part : part + state],
        dc_ref[c, :rows] * dsl_ref[c, :rows, part + state :],
        x * far,
        g * x,
    )


def edge_kernel(
    s, one, two, act_ref, dsl_ref, dxl_ref, dbl_ref, dc_ref, gall_ref, vec_ref, hpar,
    edge_ref, adjoint_ref, high_ref, low_ref, *, share, headdim, state,
):
    part = share * headdim
    matrix = spread_matrix(share, headdim)
    adjoint = one[:state, :] + one[state : state + 1, :] * two[:state, :]
    adjoint_ref[...] = adjoint
    high, low = halves(adjoint)
    high_ref[...] = high
    low_ref[...] = low
    grads = input_grads(
        0, 16, high, low, act_ref, dsl_ref, dxl_ref, dbl_ref, dc_ref, gall_ref, vec_ref,
        skip_row(hpar, matrix), matrix, part, state,
    )
    edge_ref[:, :part] = grads[0][:8]
    edge_ref[:, part : part + state] = grads[1][:8]
    edge_ref[:, part + state :] = grads[2][:8]


def pair_grads(s, first, high_ref, low_ref, act_ref, dsl_ref, dxl_ref, dbl_ref, dc_ref, gall_ref,
               vec_ref, hpar, xall_ref, du_ref, par_ref, sizes, docs, taps):
    share, headdim, state = sizes
    part = share * headdim
    width = part + 2 * state
    tokens = act_ref.shape[1]
    plane = s[1]
    matrix = spread_matrix(share, headdim)
    skip = skip_row(hpar, matrix)
    high, low = high_ref[...], low_ref[...]
    away, skips = [], []
    for i in range(2):
        c = first + i
        grads = input_grads(
            c, tokens, high, low, act_ref, dsl_ref, dxl_ref, dbl_ref, dc_ref, gall_ref, vec_ref,
            skip, matrix, part, state,
        )
        rows = pl.ds(pl.multiple_of(c * tokens, tokens), tokens)
        du_ref[rows, :part] = grads[0]
        du_ref[rows, part : part + state] = grads[1]
        du_ref[rows, part + state : width] = grads[2]
        away.append(head_sums(grads[3], matrix))
        skips.append(head_sums(grads[4], matrix))
    for lo in range(0, width, 128):
        sums = [jnp.zeros((8, 128), F32) for _ in range(taps + 1)]
        for i in range(2):
            c = first + i
            begin = pl.multiple_of(c * tokens, tokens)
            rows = xall_ref[pl.ds(begin, tokens + 16), lo : lo + 128].astype(F32)
            pos = plane + c * tokens + lax.broadcasted_iota(jnp.int32, (tokens, 1), 0)
            inside = pos - doc_start(pos, s, docs)
            du = du_ref[pl.ds(begin, tokens), lo : lo + 128]
            for k in range(taps):
                reach = taps - 1 - k
                moved = rows[16 - reach : 16 - reach + tokens]
                if reach:
                    moved = moved * (inside >= reach).astype(F32)
                sums[k] = sums[k] + jnp.sum((du * moved).reshape(tokens // 8, 8, 128), axis=0)
            sums[taps] = sums[taps] + jnp.sum(du.reshape(tokens // 8, 8, 128), axis=0)
        for k in range(taps + 1):
            par_ref[k : k + 1, lo : lo + 128] = jnp.sum(sums[k], axis=0, keepdims=True)
    return away, skips[0] + skips[1]


def back_far_kernel(
    s, high_ref, low_ref, act_ref, dsl_ref, dxl_ref, dbl_ref, dc_ref, gall_ref, vec_ref, hpar,
    xall_ref, du_ref, par_ref, aux_ref, *, sizes, docs, taps,
):
    share, headdim, state = sizes
    part = share * headdim
    width = part + 2 * state
    tokens = act_ref.shape[1]
    par_ref[...] = jnp.zeros_like(par_ref)
    away, skips = pair_grads(
        s, (s[0] & 2) ^ 2, high_ref, low_ref, act_ref, dsl_ref, dxl_ref, dbl_ref, dc_ref, gall_ref,
        vec_ref, hpar, xall_ref, du_ref, par_ref, sizes, docs, taps,
    )
    aux_ref[0], aux_ref[1], aux_ref[2] = away[0], away[1], skips

    @pl.when((s[0] & 2) == 2)
    def _():
        matrix = spread_matrix(share, headdim)
        grads = input_grads(
            2, 16, high_ref[...], low_ref[...], act_ref, dsl_ref, dxl_ref, dbl_ref, dc_ref,
            gall_ref, vec_ref, skip_row(hpar, matrix), matrix, part, state,
        )
        du_ref[2 * tokens : 2 * tokens + 8, :part] = grads[0][:8]
        du_ref[2 * tokens : 2 * tokens + 8, part : part + state] = grads[1][:8]
        du_ref[2 * tokens : 2 * tokens + 8, part + state :] = grads[2][:8]


def back_near_kernel(
    s, high_ref, low_ref, act_ref, dsl_ref, dxl_ref, dbl_ref, dc_ref, gall_ref, vec_ref, hpar,
    xall_ref, adjoint_ref, in_ref, pay, gy_ref, flow_ref, xd_ref, par_in, aux, du_in,
    du_ref, par_ref, g0, g1, g2, g3, away_s, gs_s, *, sizes, docs, taps,
):
    share, headdim, state = sizes
    part = share * headdim
    width = part + 2 * state
    tokens = act_ref.shape[1]
    chunks = 4
    me = s[0]
    matrix = spread_matrix(share, headdim)
    own, skips = pair_grads(
        s, me & 2, high_ref, low_ref, act_ref, dsl_ref, dxl_ref, dbl_ref, dc_ref, gall_ref,
        vec_ref, hpar, xall_ref, du_ref, par_ref, sizes, docs, taps,
    )
    par_ref[: taps + 1, :width] = par_ref[: taps + 1, :width] + par_in[: taps + 1, :width]
    for i in range(2):
        away_s[(me & 2) + i] = own[i]
        away_s[((me & 2) ^ 2) + i] = aux[i]
    inner = jnp.sum(adjoint_ref[...] * in_ref[...], axis=0, keepdims=True)
    inner = inner * pay[state : state + 1, :]
    through = head_sums(jnp.broadcast_to(inner, (8, part)), matrix)[:, :1]
    rate = jnp.exp(hpar[:, 1:2])
    start_sums = triangle(tokens, "from")
    end_sums = triangle(tokens, "before")
    g_bias = jnp.zeros((share, 1), F32)
    g_decay = jnp.zeros((share, 1), F32)
    for c in range(chunks):
        flow = (
            flow_ref[c] + by_triangle(gy_ref[c], start_sums) + by_triangle(away_s[c], end_sums)
        ) + through
        for d in range(chunks):
            if d > c:
                flow = flow + jnp.sum(gy_ref[d], axis=1, keepdims=True)
            if d < c:
                flow = flow + jnp.sum(away_s[d], axis=1, keepdims=True)
        step = vec_ref[c, STEP]
        grad_step = ((xd_ref[c] + away_s[c]) / step - rate * flow) * vec_ref[c, SIG]
        gs_s[c] = grad_step
        g_bias = g_bias + jnp.sum(grad_step, axis=1, keepdims=True)
        g_decay = g_decay - rate * jnp.sum(flow * step, axis=1, keepdims=True)
    for k, out in enumerate((g0, g1, g2, g3)):
        out[...] = gs_s[me ^ k]
    g_skip = jnp.sum(skips + aux[2], axis=1, keepdims=True)
    lane = lax.broadcasted_iota(jnp.int32, (share, 128), 1)
    heads = jnp.where(lane == 0, g_bias, jnp.where(lane == 1, g_decay, g_skip))
    par_ref[taps + 1 :, :width] = jnp.zeros((8 - taps - 1, width), F32)
    par_ref[:, width : width + 128] = heads[:8]
    par_ref[:, width + 128 :] = heads[8:]


def conv_back_kernel(
    s, du_ref, rim_ref, wx, wb, wc, o0, o1, ext, *, far, sizes, docs, taps
):
    share, headdim, state = sizes
    me = s[0]
    plane = s[1]
    part = share * headdim
    width = part + 2 * state
    tokens = o0.shape[0]
    first = (me & 2) ^ (2 if far else 0)
    ext[: 2 * tokens, :] = du_ref[pl.ds(pl.multiple_of(first * tokens, tokens), 2 * tokens), :]
    ext[2 * tokens :, :] = jnp.where(
        first == 2, rim_ref[...], du_ref[2 * tokens : 2 * tokens + 8, :]
    )
    for k, out in enumerate((o0, o1)):
        place = (me & 1) ^ k
        pos = plane + (first + place) * tokens + lax.broadcasted_iota(jnp.int32, (tokens, 1), 0)
        valid = []
        for reach in range(1, taps):
            ahead = pos + reach
            valid.append((ahead - doc_start(ahead, s, docs) >= reach).astype(F32))
        begin = pl.multiple_of(place * tokens, tokens)
        for lo in range(0, width, 128):
            rows = ext[pl.ds(begin, tokens + 8), lo : lo + 128]
            if lo < part:
                w = wx[:, lo : lo + 128]
            elif lo < part + state:
                w = wb[:, lo - part : lo - part + 128]
            else:
                w = wc[:, lo - part - state : lo - part - state + 128]
            total = w[taps - 1 : taps] * rows[:tokens]
            for reach in range(1, taps):
                k_tap = taps - 1 - reach
                total = total + w[k_tap : k_tap + 1] * (
                    rows[reach : reach + tokens] * valid[reach - 1]
                )
            out[:, lo : lo + 128] = total.astype(BF16)


def join_kernel(s, p0, p1, p2, p3, out_ref):
    part = p0.shape[1]
    for k, ref in enumerate((p0, p1, p2, p3)):
        q = s[0] ^ k
        out_ref[:, pl.ds(pl.multiple_of(q * part, part), part)] = ref[...]


def join_small_kernel(s, first, *refs):
    groups = 4
    width = first.shape[1]
    received, steps, outs = refs[: -2 * groups], refs[-2 * groups : -groups], refs[-groups:]
    total = first[...]
    for ref in received:
        total = total + ref[...]
    for step, out in zip(steps, outs):
        tokens = step.shape[1]
        out[:, :width] = total
        out[:, width : width + tokens] = step[:8, :]
        out[:, width + tokens :] = step[8:, :]


def join_grad_kernel(s, p0, p1, p2, p3, g0, g1, g2, g3, out_ref, gs_ref, *, share, inner, state, groups):
    part = inner // groups
    for k, ref in enumerate((p0, p1, p2, p3)):
        q = s[0] ^ k
        out_ref[:, pl.ds(pl.multiple_of(q * part, part), part)] = ref[:, :part]
        out_ref[:, pl.ds(pl.multiple_of(inner + q * state, state), state)] = ref[
            :, part : part + state
        ]
        out_ref[:, pl.ds(pl.multiple_of(inner + (groups + q) * state, state), state)] = ref[
            :, part + state :
        ]
    for k, ref in enumerate((g0, g1, g2, g3)):
        tokens = gs_ref.shape[1]
        last = ref.shape[1]
        first = pl.multiple_of((s[0] ^ k) * share, share)
        gs_ref[pl.ds(first, 8), :] = ref[:, last - 2 * tokens : last - tokens]
        gs_ref[pl.ds(first + 8, 8), :] = ref[:, last - tokens :]


def join_params_kernel(
    s, p0, p1, p2, p3, conv_ref, head_ref, turned, *, share, inner, state, groups, scale
):
    part = inner // groups
    width = part + 2 * state
    rows = conv_ref.shape[0]
    for k, ref in enumerate((p0, p1, p2, p3)):
        q = s[0] ^ k
        conv_ref[:, pl.ds(pl.multiple_of(q * part, part), part)] = ref[:rows, :part] * scale
        conv_ref[:, pl.ds(pl.multiple_of(inner + q * state, state), state)] = (
            ref[:rows, part : part + state] * scale
        )
        conv_ref[:, pl.ds(pl.multiple_of(inner + (groups + q) * state, state), state)] = (
            ref[:rows, part + state : width] * scale
        )
        turned[pl.ds(pl.multiple_of(q * share, 8), 8), :] = ref[:, width : width + 128]
        turned[pl.ds(pl.multiple_of(q * share + 8, 8), 8), :] = ref[:, width + 128 : width + 256]
    head_ref[...] = turned[...].T[: head_ref.shape[0], :] * scale


def call(kernel, table, operands, specs, outs, scratch=(), name=None, vmem=True, aliases=None):
    here = pl.BlockSpec(memory_space=pltpu.VMEM)
    in_specs = [here if spec is None else spec for spec in specs]
    return pl.pallas_call(
        kernel,
        out_shape=[
            pltpu.VMEM(shape, kind) if vmem else jax.ShapeDtypeStruct(shape, kind)
            for shape, kind in outs
        ],
        grid_spec=pltpu.PrefetchScalarGridSpec(
            num_scalar_prefetch=1,
            grid=(1,),
            in_specs=in_specs,
            out_specs=[here] * len(outs),
            scratch_shapes=[pltpu.VMEM(shape, kind) for shape, kind in scratch],
        ),
        compiler_params=pltpu.CompilerParams(vmem_limit_bytes=LIMIT),
        cost_estimate=pl.CostEstimate(flops=1, transcendentals=0, bytes_accessed=1),
        name=name,
        input_output_aliases=aliases or {},
    )(table, *operands)


def swapped(value, bits):
    count = lax.axis_size("ctx")
    return lax.ppermute(value, "ctx", [(i, i ^ bits) for i in range(count)])


def shifted(value, steps):
    count = lax.axis_size("ctx")
    pairs = [(i, i + steps) for i in range(count) if 0 <= i + steps < count]
    return lax.ppermute(value, "ctx", pairs)


def after(value, *others):
    return lax.optimization_barrier((value, *others))[0]


def near_of(payload, state, direction, planes):
    near = shifted(payload, direction * GROUPS)
    covered, window = 1, planes // 2
    while 2 * covered < window:
        far = shifted(near, direction * GROUPS * covered)
        factor = near[state : state + 1]
        near = jnp.concatenate(
            [near[:state] + factor * far[:state], near[state:] * far[state:]], axis=0
        )
        covered *= 2
    return near, covered


def body(
    conv_input, step_raw, step_bias, decay_log, skip_gain, conv_weight, conv_bias, doc_lengths,
    grad_out,
):
    tokens, channels = conv_input.shape
    heads = step_raw.shape[1]
    taps = conv_weight.shape[0]
    inner = grad_out.shape[1]
    headdim = inner // heads
    groups = GROUPS
    share = heads // groups
    state = (channels - inner) // (2 * groups)
    part = inner // groups
    width = part + 2 * state
    docs = doc_lengths.shape[0]
    devices = lax.axis_size("ctx")
    planes = devices // groups
    me = lax.axis_index("ctx")
    sizes = dict(share=share, headdim=headdim, state=state)
    table = jnp.concatenate(
        [
            jnp.stack([me & (groups - 1), (me & -groups) * tokens]).astype(jnp.int32),
            doc_lengths,
        ]
    )
    bias_row = conv_bias[None, :]
    b_first = inner // state

    def column_specs(rows):
        return [
            pl.BlockSpec((rows, part), lambda i, s: (0, s[0])),
            pl.BlockSpec((rows, state), lambda i, s: (0, b_first + s[0])),
            pl.BlockSpec((rows, state), lambda i, s: (0, b_first + groups + s[0])),
        ]

    shapes = dict(share=share, inner=inner, state=state, groups=groups)
    packed = call(
        functools.partial(pack_kernel, **shapes),
        table,
        [conv_input, step_raw.T],
        [None] * 2,
        [((tokens, width + tokens), BF16)] * groups + [((16, width), BF16)] * groups,
        name="pack",
    )
    xs, edges = packed[:groups], packed[groups:]
    *gs, hpar = call(
        functools.partial(pack_grad_kernel, groups=groups),
        table,
        [grad_out, step_bias[None, :], decay_log[None, :], skip_gain[None, :]],
        [None] * 4,
        [((tokens, part), BF16)] * groups + [((share, 128), F32)],
        [((128, 128), F32)] * 2,
        name="pack_grad",
    )
    xr = [xs[0]] + [swapped(xs[k], k) for k in range(1, groups)]
    rims = []
    for k in range(groups):
        pairs = []
        for i in range(devices):
            source = i - 1 - i % 2 if k >= 2 else i - 1 - i % groups
            if source >= 0 and (source % groups) ^ (i % groups) == k:
                pairs.append((source, i))
        rims.append(lax.ppermute(edges[k], "ctx", pairs))
    conv_shapes = [
        ((groups, tokens, width), F32),
        ((groups, tokens, width), F32),
        ((groups * tokens + 16, width), BF16),
    ]
    conv_specs = column_specs(taps) + column_specs(1)
    conv_params = [conv_weight] * 3 + [bias_row] * 3
    ext_shape = ((2 * tokens + 8, width), F32)
    act, dsl, xall = call(
        functools.partial(conv_kernel, docs=docs, sizes=(share, headdim, state)),
        table,
        [xr[0], xr[1]] + conv_params,
        [None] * 2 + conv_specs,
        conv_shapes,
        [ext_shape],
        name="conv",
    )
    act, *gs = lax.optimization_barrier((act, *gs))
    gr = [gs[0]] + [swapped(gs[k], k) for k in range(1, groups)]
    act, dsl, xall, spay, schain, vec = call(
        functools.partial(conv_state_kernel, docs=docs, **sizes),
        table,
        xr + rims + conv_params + [hpar, act, dsl, xall],
        [None] * 8 + conv_specs + [None] * 4,
        conv_shapes
        + [
            ((state + 8, part), F32),
            ((groups, state, part), F32),
            ((groups, 8, share, tokens), F32),
        ],
        [ext_shape, ((groups, share, tokens), F32)],
        name="conv_state",
        aliases={16: 0, 17: 1, 18: 2},
    )
    s_near, covered = near_of(spay, state, 1, planes)
    gall, gpay, gchain = call(
        functools.partial(grad_state_kernel, **sizes),
        table,
        gr + [act, vec, spay],
        [None] * 7,
        [
            ((groups, tokens, part), BF16),
            ((state + 8, part), F32),
            ((groups, state, part), F32),
        ],
        name="grad_state",
    )
    g_near, _ = near_of(gpay, state, -1, planes)
    local_shapes = [
        ((groups, tokens, part), F32),
        ((groups, tokens, part), F32),
        ((groups, tokens, state), F32),
        ((groups, tokens, state), F32),
        ((groups, share, tokens), F32),
        ((groups, share, tokens), F32),
    ]
    locals_ = []
    for span in ((0, 2), (2, 3), (3, 4)):
        locals_ = call(
            functools.partial(local_kernel, span=span, docs=docs, **sizes),
            table,
            [act, vec, gall, schain, gchain] + list(locals_),
            [None] * (5 + len(locals_)),
            local_shapes,
            [((tokens, share * tokens), F32)] + [((tokens, part), F32)] * 2,
            name="local",
            aliases={6 + i: i for i in range(len(locals_))},
        )
        if span[1] == 2:
            s_near, *locals_ = lax.optimization_barrier((s_near, *locals_))
            s_far = shifted(s_near, GROUPS * covered)
        elif span[1] == 3:
            g_near, *locals_ = lax.optimization_barrier((g_near, *locals_))
            g_far = shifted(g_near, -GROUPS * covered)
    y_local, dx_local, db_local, dc_local, flow, xd = locals_
    *mixed, gy, state_in, dc = call(
        functools.partial(out_kernel, **sizes),
        table,
        [s_near, s_far, act, y_local, gall, vec, hpar, dc_local],
        [None] * 8,
        [((tokens, part), BF16)] * groups
        + [
            ((groups, share, tokens), F32),
            ((state, part), F32),
            ((groups, tokens, state), F32),
        ],
        name="out",
    )
    mr = [mixed[0]] + [swapped(mixed[k], k) for k in range(1, groups)]
    common = [act, dsl, dx_local, db_local, dc, gall, vec, hpar]
    edge, adjoint, high, low = call(
        functools.partial(edge_kernel, **sizes),
        table,
        [g_near, g_far] + common,
        [None] * 10,
        [
            ((8, width), F32),
            ((state, part), F32),
            ((state, part), BF16),
            ((state, part), BF16),
        ],
        name="edge",
    )
    rim_back = shifted(edge, -groups)
    triple = (share, headdim, state)
    settings = dict(sizes=triple, docs=docs, taps=taps)
    common = [high, low] + common + [xall]
    du_shape = ((groups * tokens, width), F32)
    par_shape = ((8, width + 256), F32)
    du, par_far, aux = call(
        functools.partial(back_far_kernel, **settings),
        table,
        common,
        [None] * 11,
        [du_shape, par_shape, ((3, share, tokens), F32)],
        name="back_far",
    )
    rim_back, *mr = lax.optimization_barrier((rim_back, *mr))
    pair_shapes = [((tokens, width), BF16)] * 2
    ext_back = [((2 * tokens + 8, width), F32)]
    back_far = call(
        functools.partial(conv_back_kernel, far=True, **settings),
        table,
        [du, rim_back] + [conv_weight] * 3,
        [None] * 2 + column_specs(taps),
        pair_shapes,
        ext_back,
        name="conv_back_far",
    )
    br_far = [swapped(back_far[k - 2], k) for k in (2, 3)]
    du = after(du, back_far[0])
    du, params, *grad_steps = call(
        functools.partial(back_near_kernel, **settings),
        table,
        common
        + [adjoint, state_in, spay, gy, flow, xd, par_far, aux, du],
        [None] * 20,
        [du_shape, par_shape] + [((share, tokens), F32)] * groups,
        [((groups, share, tokens), F32)] * 2,
        name="back_near",
        aliases={20: 0},
    )
    (mixer_out,) = call(
        join_kernel, table, mr, [None] * groups, [((tokens, inner), BF16)], name="join_out",
        vmem=False,
    )
    du, br_far[0], mixer_out = lax.optimization_barrier((du, br_far[0], mixer_out))
    back_near = call(
        functools.partial(conv_back_kernel, far=False, **settings),
        table,
        [du, rim_back] + [conv_weight] * 3,
        [None] * 2 + column_specs(taps),
        pair_shapes,
        ext_back,
        name="conv_back_near",
    )
    br = [back_near[0], swapped(back_near[1], 1)] + br_far
    step = groups
    received = []
    while step < devices:
        ways = 4 if 4 * step <= devices else 2
        params = functools.reduce(jnp.add, received, params)
        received = [swapped(params, way * step) for way in range(1, ways)]
        step *= ways
    small = call(
        join_small_kernel,
        table,
        [params] + received + list(grad_steps),
        [None] * (1 + len(received) + groups),
        [((8, width + 256 + 2 * tokens), F32)] * groups,
        name="join_small",
    )
    pr = [small[0]] + [swapped(small[k], k) for k in range(1, groups)]
    grad_conv, grad_heads = call(
        functools.partial(join_params_kernel, scale=(tokens * devices) ** (-0.5), **shapes),
        table,
        pr,
        [None] * groups,
        [((taps + 1, channels), F32), ((3, heads), F32)],
        [((heads, 128), F32)],
        name="join_params",
        vmem=False,
    )
    grad_input, grad_step = call(
        functools.partial(join_grad_kernel, **shapes),
        table,
        br + pr,
        [None] * (2 * groups),
        [((tokens, channels), BF16), ((heads, tokens), F32)],
        name="join_grad",
        vmem=False,
    )
    return mixer_out, grad_input, grad_step.T, grad_conv, grad_heads


def solution(mesh):
    rows = P(("groups", "ctx"), None)
    return jax.shard_map(
        body,
        mesh=mesh,
        in_specs=(rows, rows, P(), P(), P(), P(), P(), P("groups"), rows),
        out_specs=(rows, rows, rows, P("groups", None), P("groups", None)),
        check_vma=False,
    )
```

```python
import functools

import jax
import jax.numpy as jnp
from jax import lax
from jax.experimental import pallas as pl
from jax.experimental.pallas import tpu as pltpu
from jax.sharding import PartitionSpec as P

GROUPS = 4
F32 = jnp.float32
BF16 = jnp.bfloat16
NEG = -1e30
LIMIT = 12 * 1024 * 1024
STEP, CUM, TAIL, HEAD, TP, HP, WHOLE, SIG = range(8)

NN = (((1,), (0,)), ((), ()))
NT = (((1,), (1,)), ((), ()))
TN = (((0,), (0,)), ((), ()))


def mm(a, b, dims):
    return lax.dot_general(a, b, dims, preferred_element_type=F32)


def halves(a):
    high = a.astype(BF16)
    return high, (a - high.astype(F32)).astype(BF16)


def thirds(a):
    high = a.astype(BF16)
    rest = a - high.astype(F32)
    mid = rest.astype(BF16)
    return high, mid, (rest - mid.astype(F32)).astype(BF16)


def dot3(a, b, dims):
    return joined3(halves(a), halves(b), dims)


def joined3(a, b, dims):
    (ah, al), (bh, bl) = a, b
    (left,), (right,) = dims[0]
    if ah.shape[left] > 128:
        return mm(ah, bh, dims) + (mm(ah, bl, dims) + mm(al, bh, dims))
    both = mm(
        jnp.concatenate([ah, al], axis=left), jnp.concatenate([bh, bh], axis=right), dims
    )
    return both + mm(ah, bl, dims)


def spread_matrix(share, headdim):
    lanes = lax.broadcasted_iota(jnp.int32, (share, share * headdim), 1)
    rows = lax.broadcasted_iota(jnp.int32, (share, share * headdim), 0)
    return (lanes // headdim == rows).astype(BF16)


def spread(values, matrix):
    return mm(
        jnp.concatenate(thirds(values), axis=0), jnp.concatenate([matrix] * 3, axis=0), TN
    )


def skip_row(hpar, matrix):
    return spread(jnp.broadcast_to(hpar[:, 2:3], (hpar.shape[0], 8)), matrix)[:1]


def head_sums(products, matrix):
    high, low = halves(products)
    return mm(matrix, high, NT) + mm(matrix, low, NT)


def by_triangle(values, triangle):
    high, mid, low = thirds(values)
    return mm(high, triangle, NN) + (mm(mid, triangle, NN) + mm(low, triangle, NN))


def triangle(size, kind):
    rows = lax.broadcasted_iota(jnp.int32, (size, size), 0)
    cols = lax.broadcasted_iota(jnp.int32, (size, size), 1)
    kept = {"upto": rows <= cols, "before": rows < cols, "from": rows >= cols}[kind]
    return kept.astype(BF16)


def doc_start(position, table, docs):
    start = jnp.zeros_like(position)
    first = table[2]
    for i in range(1, docs):
        start = jnp.where(first <= position, first, start)
        first = first + table[2 + i]
    return start


def pack_kernel(s, x_ref, step_ref, *refs, share, inner, state, groups):
    outs, rims = refs[:groups], refs[groups:]
    me = s[0]
    tokens = x_ref.shape[0]
    part = inner // groups
    width = part + 2 * state
    for k in range(groups):
        q = me ^ k
        xs = outs[k]
        xs[:, :part] = x_ref[:, pl.ds(pl.multiple_of(q * part, part), part)]
        xs[:, part : part + state] = x_ref[
            :, pl.ds(pl.multiple_of(inner + q * state, state), state)
        ]
        xs[:, part + state : width] = x_ref[
            :, pl.ds(pl.multiple_of(inner + (groups + q) * state, state), state)
        ]
        rims[k][...] = xs[tokens - 16 :, :width]
        raw = step_ref[pl.ds(pl.multiple_of(q * share, share), share), :]
        xs[:, width:] = jnp.zeros((tokens, tokens), BF16)
        for i, piece in enumerate(thirds(raw)):
            xs[i * share : (i + 1) * share, width:] = piece


def pack_grad_kernel(s, g_ref, bias, decay, skip, *refs, groups):
    outs, hpar, wide, turned = refs[:groups], *refs[groups:]
    heads = bias.shape[1]
    share = heads // groups
    wide[...] = jnp.zeros_like(wide)
    for i, ref in enumerate((bias, decay, skip)):
        wide[i : i + 1, :heads] = ref[...]
    turned[...] = wide[...].T
    hpar[...] = turned[pl.ds(pl.multiple_of(s[0] * share, share), share), :]
    part = outs[0].shape[1]
    for k, out in enumerate(outs):
        q = s[0] ^ k
        out[...] = g_ref[:, pl.ds(pl.multiple_of(q * part, part), part)]


def activate(rows, weight, bias, valid, paired):
    taps = weight.shape[0]
    tokens = rows.shape[0] - 8
    u = jnp.zeros((tokens, rows.shape[1]), F32) + bias
    for k in range(taps):
        reach = taps - 1 - k
        moved = rows[8 - reach : 8 - reach + tokens]
        if reach:
            moved = moved * valid[reach]
        u = u + weight[k : k + 1] * moved
    sig = 1.0 / (1.0 + jnp.exp(-u))
    value = u * sig
    if paired:
        high, low = halves(value)
        value = high.astype(F32) + low.astype(F32)
    return value, sig * (1.0 + u * (1.0 - sig))


def convolve_head(s, first, rim, wx, wb, wc, bx, bb, bc, act_ref, dsl_ref, xall_ref, sizes, docs):
    share, headdim, state = sizes
    part = share * headdim
    tokens = act_ref.shape[1]
    pos = s[1] + first * tokens + lax.broadcasted_iota(jnp.int32, (8, 1), 0)
    inside = pos - doc_start(pos, s, docs)
    valid = [(inside >= reach).astype(F32) for reach in range(wx.shape[0])]
    own = xall_ref[pl.ds(pl.multiple_of(16 + first * tokens, 16), 16), :].astype(F32)
    rows = jnp.concatenate([rim[8:], own[:8]], axis=0)
    for lo, size, w_ref, b_ref in (
        (0, part, wx, bx), (part, state, wb, bb), (part + state, state, wc, bc)
    ):
        value, slope = activate(rows[:, lo : lo + size], w_ref[...], b_ref[...], valid, lo == 0)
        act_ref[first, :8, lo : lo + size] = value
        dsl_ref[first, :8, lo : lo + size] = slope


def convolve_pair(s, first, pieces, rim, wx, wb, wc, bx, bb, bc, act_ref, dsl_ref, xall_ref, ext,
                  sizes, docs):
    me, plane = s[0], s[1]
    share, headdim, state = sizes
    part = share * headdim
    width = part + 2 * state
    tokens = pieces[0].shape[0]
    taps = wx.shape[0]
    ext[:8, :] = rim[8:]
    for k, ref in enumerate(pieces):
        place = (me & 1) ^ k
        value = ref[:, :width]
        ext[pl.ds(pl.multiple_of(8 + place * tokens, 8), tokens), :] = value.astype(F32)
        xall_ref[pl.ds(pl.multiple_of(16 + (first + place) * tokens, 16), tokens), :] = value

    for c in range(2):
        chunk = first + c
        pos = plane + chunk * tokens + lax.broadcasted_iota(jnp.int32, (tokens, 1), 0)
        inside = pos - doc_start(pos, s, docs)
        valid = [(inside >= reach).astype(F32) for reach in range(taps)]

        def convolve(lo, w_ref, b_ref, wlo, paired):
            rows = ext[c * tokens : c * tokens + tokens + 8, lo : lo + 128]
            value, slope = activate(
                rows, w_ref[:, wlo : wlo + 128], b_ref[:, wlo : wlo + 128], valid, paired
            )
            act_ref[chunk, :, lo : lo + 128] = value
            dsl_ref[chunk, :, lo : lo + 128] = slope

        for lo in range(0, part, 128):
            convolve(lo, wx, bx, lo, True)
        for lo in range(0, state, 128):
            convolve(part + lo, wb, bb, lo, False)
            convolve(part + state + lo, wc, bc, lo, False)


def conv_kernel(
    s, x0, x1, wx, wb, wc, bx, bb, bc, act_ref, dsl_ref, xall_ref, ext, *, sizes, docs
):
    rim = jnp.zeros((16, ext.shape[1]), F32)
    convolve_pair(
        s, s[0] & 2, (x0, x1), rim, wx, wb, wc, bx, bb, bc, act_ref, dsl_ref, xall_ref, ext,
        sizes, docs,
    )


def conv_state_kernel(
    s, x0, x1, x2, x3, r0, r1, r2, r3, wx, wb, wc, bx, bb, bc, hpar, act_in, dsl_in, xall_in,
    act_ref, dsl_ref, xall_ref, pay_ref, chain_ref, vec_ref,
    ext, raws, *, share, headdim, state, docs,
):
    me = s[0]
    plane = s[1]
    part = share * headdim
    width = part + 2 * state
    tokens = x0.shape[0]
    chunks = 4
    for k, ref in enumerate((x0, x1, x2, x3)):
        block = ref[: 3 * share, width:].astype(F32)
        raws[me ^ k] = block[:share] + block[share : 2 * share] + block[2 * share :]
    upper_chip = (me & 2) == 2
    inner_rim = xall_ref[2 * tokens : 2 * tokens + 16, :].astype(F32)
    rim = jnp.where(upper_chip, r0[...].astype(F32) + r1[...].astype(F32), inner_rim)

    own_rim = r2[...].astype(F32) + r3[...].astype(F32)
    xall_ref[:16, :] = jnp.where(upper_chip, rim, own_rim).astype(BF16)
    convolve_head(
        s, me & 2, own_rim, wx, wb, wc, bx, bb, bc, act_ref, dsl_ref, xall_ref,
        (share, headdim, state), docs,
    )
    convolve_pair(
        s, (me & 2) ^ 2, (x2, x3), rim, wx, wb, wc, bx, bb, bc, act_ref, dsl_ref, xall_ref, ext,
        (share, headdim, state), docs,
    )

    bias = hpar[:, 0:1]
    rate = jnp.exp(hpar[:, 1:2])
    upper = triangle(tokens, "upto")
    before = jnp.zeros((share, 1), F32)
    cums, steps, ends = [], [], []
    for c in range(chunks):
        v = raws[c] + bias
        step = jnp.maximum(v, 0.0) + jnp.log1p(jnp.exp(-jnp.abs(v)))
        cum = by_triangle(-step * rate, upper)
        vec_ref[c, STEP] = step
        vec_ref[c, CUM] = cum
        vec_ref[c, SIG] = 1.0 / (1.0 + jnp.exp(-v))
        cums.append(cum)
        steps.append(step)
        ends.append(cum[:, tokens - 1 :])
    total = ends[0] + ends[1] + ends[2] + ends[3]
    last_plane = doc_start(plane + chunks * tokens - 1, s, docs)
    for c in range(chunks):
        base = plane + c * tokens
        pos = base + lax.broadcasted_iota(jnp.int32, (1, tokens), 1)
        start = doc_start(pos, s, docs)
        last = doc_start(base + tokens - 1, s, docs)
        cum, step, end = cums[c], steps[c], ends[c]
        vec_ref[c, TAIL] = jnp.exp(end - cum) * step * (pos >= last).astype(F32)
        vec_ref[c, HEAD] = jnp.exp(cum) * (start < base).astype(F32)
        vec_ref[c, HP] = jnp.exp(cum + before) * (start < plane).astype(F32)
        before = before + end
        vec_ref[c, TP] = (
            jnp.exp(total - before + (end - cum)) * step * (pos >= last_plane).astype(F32)
        )
        open_c = jnp.where(last < base, 1.0, 0.0)
        vec_ref[c, WHOLE] = jnp.broadcast_to(jnp.exp(end) * open_c, (share, tokens))
    matrix = spread_matrix(share, headdim)
    open_plane = jnp.where(last_plane < plane, 1.0, 0.0)
    pay_ref[state:, :] = spread(jnp.broadcast_to(jnp.exp(total) * open_plane, (share, 8)), matrix)

    carried = jnp.zeros((state, part), F32)
    for c in range(chunks):
        chain_ref[c] = carried
        weighted = act_ref[c, :, :part] * spread(vec_ref[c, TAIL], matrix)
        local = dot3(act_ref[c, :, part : part + state], weighted, TN)
        carried = carried * spread(vec_ref[c, WHOLE], matrix) + local
    pay_ref[:state, :] = carried


def grad_state_kernel(
    s, g0, g1, g2, g3, act_ref, vec_ref, pay_in, gall_ref, pay_ref, chain_ref,
    *, share, headdim, state,
):
    me = s[0]
    part = share * headdim
    chunks = 4
    for k, ref in enumerate((g0, g1, g2, g3)):
        gall_ref[me ^ k] = ref[...]
    matrix = spread_matrix(share, headdim)
    carried = jnp.zeros((state, part), F32)
    for c in range(chunks - 1, -1, -1):
        chain_ref[c] = carried
        weighted = gall_ref[c].astype(F32) * spread(vec_ref[c, HEAD], matrix)
        local = dot3(act_ref[c, :, part + state :], weighted, TN)
        carried = carried * spread(vec_ref[c, WHOLE], matrix) + local
    pay_ref[:state, :] = carried
    pay_ref[state:, :] = pay_in[state:, :]


def local_kernel(
    s, act_ref, vec_ref, gall_ref, schain, gchain, *refs, span, share, headdim, state, docs,
):
    y_ref, dx_ref, db_ref, dc_ref, flow_ref, xd_ref, wide, yd, dxd = refs[-9:]
    plane = s[1]
    part = share * headdim
    tokens = act_ref.shape[1]
    matrix = spread_matrix(share, headdim)
    lanes = lax.broadcasted_iota(jnp.int32, (tokens, 2 * headdim), 1)
    left = lanes < headdim
    to_lanes = spread_matrix(share, tokens)
    start_sums = triangle(tokens, "from")
    end_sums = triangle(tokens, "before")

    def chunk(c, carry):
        base = plane + c * tokens
        tpos = base + lax.broadcasted_iota(jnp.int32, (tokens, tokens), 0)
        spos = base + lax.broadcasted_iota(jnp.int32, (tokens, tokens), 1)
        tstart = doc_start(tpos, s, docs)
        mask = jnp.where((spos <= tpos) & (spos >= tstart), 0.0, NEG)
        b = act_ref[c, :, part : part + state]
        cc = act_ref[c, :, part + state :]
        m = dot3(cc, b, NT)
        cum = vec_ref[c, CUM]
        step = vec_ref[c, STEP]
        wide[...] = spread(cum, to_lanes)
        dm = jnp.zeros((tokens, tokens), F32)
        for pair in range(share // 2):
            lo = pair * 2 * headdim
            xp = act_ref[c, :, lo : lo + 2 * headdim]
            gp = gall_ref[c, :, lo : lo + 2 * headdim]
            zero = jnp.zeros_like(gp)
            gst = jnp.concatenate([jnp.where(left, gp, zero), jnp.where(left, zero, gp)], axis=0)
            xh, xl = halves(xp)
            factors = []
            for h in (2 * pair, 2 * pair + 1):
                diff = wide[:, h * tokens : (h + 1) * tokens] - cum[h : h + 1, :]
                factors.append(jnp.exp(diff + mask) * step[h : h + 1, :])
            pieces = jnp.concatenate([xh, xl], axis=1)
            dw = mm(jnp.concatenate([gst, gst], axis=1), pieces, NT)
            dm = dm + dw[:tokens] * factors[0] + dw[tokens:] * factors[1]
            w = jnp.concatenate([m * factors[0], m * factors[1]], axis=0)
            w = jnp.concatenate(halves(w), axis=1)
            yst = mm(w, jnp.concatenate([pieces, pieces], axis=0), NN)
            yst = yst[:, : 2 * headdim] + yst[:, 2 * headdim :]
            yd[:, lo : lo + 2 * headdim] = jnp.where(left, yst[:tokens], yst[tokens:])
            dst = mm(w, gst, TN)
            dxd[:, lo : lo + 2 * headdim] = dst[:tokens] + dst[tokens:]
        head_in = spread(vec_ref[c, HEAD], matrix)
        tail = spread(vec_ref[c, TAIL], matrix)
        x = act_ref[c, :, :part]
        g = gall_ref[c].astype(F32)
        y = yd[...] + head_in * dot3(cc, schain[c], NN)
        y_ref[c] = y
        dx_tail = tail * dot3(b, gchain[c], NN)
        near = head_sums(x * dxd[...], matrix)
        away = head_sums(x * dx_tail, matrix)
        dx_ref[c] = dxd[...] + dx_tail
        xd_ref[c] = near + away
        inner = jnp.sum(schain[c] * gchain[c], axis=0, keepdims=True)
        through = head_sums(jnp.broadcast_to(inner, (8, part)), matrix)[:, :1]
        flow_ref[c] = (
            by_triangle(head_sums(g * y, matrix) - near, start_sums)
            + by_triangle(away, end_sums)
            + through * vec_ref[c, WHOLE]
        )
        dc_ref[c] = dot3(dm, b, NN) + dot3(g * head_in, schain[c], NT)
        db_ref[c] = dot3(dm, cc, TN) + dot3(x * tail, gchain[c], NT)
        return carry

    lax.fori_loop(*span, chunk, 0)


def out_kernel(
    s, one, two, act_ref, y_ref, gall_ref, vec_ref, hpar, dcl_ref,
    m0, m1, m2, m3, gy_ref, in_ref, dc_ref, *, share, headdim, state,
):
    me = s[0]
    part = share * headdim
    matrix = spread_matrix(share, headdim)
    arrived = one[:state, :] + one[state : state + 1, :] * two[:state, :]
    in_ref[...] = arrived
    ih, il = halves(arrived)
    skip = skip_row(hpar, matrix)
    for k, out in enumerate((m0, m1, m2, m3)):
        c = me ^ k
        reach = spread(vec_ref[c, HP], matrix)
        ch, cl = halves(act_ref[c, :, part + state :])
        carry = joined3((ch, cl), (ih, il), NN)
        y = reach * carry
        g = gall_ref[c].astype(F32)
        gy_ref[c] = head_sums(g * y, matrix)
        y = y + y_ref[c]
        out[...] = (y + skip * act_ref[c, :, :part]).astype(BF16)
        gh, gl = halves(g * reach)
        dc_ref[c] = dcl_ref[c] + mm(gh, ih, NT) + (mm(gh, il, NT) + mm(gl, ih, NT))


def input_grads(c, rows, high, low, act_ref, dsl_ref, dxl_ref, dbl_ref, dc_ref, gall_ref, vec_ref,
                skip, matrix, part, state):
    x = act_ref[c, :rows, :part]
    g = gall_ref[c, :rows].astype(F32)
    tail = spread(vec_ref[c, TP][:, :rows], matrix)
    bh, bl = halves(act_ref[c, :rows, part : part + state])
    far = tail * joined3((bh, bl), (high, low), NN)
    xh, xl = halves(x * tail)
    db = dbl_ref[c, :rows] + mm(xh, high, NT) + (mm(xh, low, NT) + mm(xl, high, NT))
    dx = far + dxl_ref[c, :rows] + skip * g
    return (
        dx * dsl_ref[c, :rows, :part],
        db * dsl_ref[c, :rows, part : part + state],
        dc_ref[c, :rows] * dsl_ref[c, :rows, part + state :],
        x * far,
        g * x,
    )


def edge_kernel(
    s, one, two, act_ref, dsl_ref, dxl_ref, dbl_ref, dc_ref, gall_ref, vec_ref, hpar,
    edge_ref, adjoint_ref, high_ref, low_ref, *, share, headdim, state,
):
    part = share * headdim
    matrix = spread_matrix(share, headdim)
    adjoint = one[:state, :] + one[state : state + 1, :] * two[:state, :]
    adjoint_ref[...] = adjoint
    high, low = halves(adjoint)
    high_ref[...] = high
    low_ref[...] = low
    grads = input_grads(
        0, 16, high, low, act_ref, dsl_ref, dxl_ref, dbl_ref, dc_ref, gall_ref, vec_ref,
        skip_row(hpar, matrix), matrix, part, state,
    )
    edge_ref[:, :part] = grads[0][:8]
    edge_ref[:, part : part + state] = grads[1][:8]
    edge_ref[:, part + state :] = grads[2][:8]


def pair_grads(s, first, high_ref, low_ref, act_ref, dsl_ref, dxl_ref, dbl_ref, dc_ref, gall_ref,
               vec_ref, hpar, xall_ref, du_ref, par_ref, sizes, docs, taps):
    share, headdim, state = sizes
    part = share * headdim
    width = part + 2 * state
    tokens = act_ref.shape[1]
    plane = s[1]
    matrix = spread_matrix(share, headdim)
    skip = skip_row(hpar, matrix)
    high, low = high_ref[...], low_ref[...]
    away, skips = [], []
    for i in range(2):
        c = first + i
        grads = input_grads(
            c, tokens, high, low, act_ref, dsl_ref, dxl_ref, dbl_ref, dc_ref, gall_ref, vec_ref,
            skip, matrix, part, state,
        )
        rows = pl.ds(pl.multiple_of(c * tokens, tokens), tokens)
        du_ref[rows, :part] = grads[0]
        du_ref[rows, part : part + state] = grads[1]
        du_ref[rows, part + state : width] = grads[2]
        away.append(head_sums(grads[3], matrix))
        skips.append(head_sums(grads[4], matrix))
    for lo in range(0, width, 128):
        sums = [jnp.zeros((8, 128), F32) for _ in range(taps + 1)]
        for i in range(2):
            c = first + i
            begin = pl.multiple_of(c * tokens, tokens)
            rows = xall_ref[pl.ds(begin, tokens + 16), lo : lo + 128].astype(F32)
            pos = plane + c * tokens + lax.broadcasted_iota(jnp.int32, (tokens, 1), 0)
            inside = pos - doc_start(pos, s, docs)
            du = du_ref[pl.ds(begin, tokens), lo : lo + 128]
            for k in range(taps):
                reach = taps - 1 - k
                moved = rows[16 - reach : 16 - reach + tokens]
                if reach:
                    moved = moved * (inside >= reach).astype(F32)
                sums[k] = sums[k] + jnp.sum((du * moved).reshape(tokens // 8, 8, 128), axis=0)
            sums[taps] = sums[taps] + jnp.sum(du.reshape(tokens // 8, 8, 128), axis=0)
        for k in range(taps + 1):
            par_ref[k : k + 1, lo : lo + 128] = jnp.sum(sums[k], axis=0, keepdims=True)
    return away, skips[0] + skips[1]


def back_far_kernel(
    s, high_ref, low_ref, act_ref, dsl_ref, dxl_ref, dbl_ref, dc_ref, gall_ref, vec_ref, hpar,
    xall_ref, du_ref, par_ref, aux_ref, *, sizes, docs, taps,
):
    share, headdim, state = sizes
    part = share * headdim
    width = part + 2 * state
    tokens = act_ref.shape[1]
    par_ref[...] = jnp.zeros_like(par_ref)
    away, skips = pair_grads(
        s, (s[0] & 2) ^ 2, high_ref, low_ref, act_ref, dsl_ref, dxl_ref, dbl_ref, dc_ref, gall_ref,
        vec_ref, hpar, xall_ref, du_ref, par_ref, sizes, docs, taps,
    )
    aux_ref[0], aux_ref[1], aux_ref[2] = away[0], away[1], skips


def back_near_kernel(
    s, high_ref, low_ref, act_ref, dsl_ref, dxl_ref, dbl_ref, dc_ref, gall_ref, vec_ref, hpar,
    xall_ref, adjoint_ref, in_ref, pay, gy_ref, flow_ref, xd_ref, par_in, aux, du_in,
    du_ref, par_ref, g0, g1, g2, g3, away_s, gs_s, *, sizes, docs, taps,
):
    share, headdim, state = sizes
    part = share * headdim
    width = part + 2 * state
    tokens = act_ref.shape[1]
    chunks = 4
    me = s[0]
    matrix = spread_matrix(share, headdim)
    own, skips = pair_grads(
        s, me & 2, high_ref, low_ref, act_ref, dsl_ref, dxl_ref, dbl_ref, dc_ref, gall_ref,
        vec_ref, hpar, xall_ref, du_ref, par_ref, sizes, docs, taps,
    )
    par_ref[: taps + 1, :width] = par_ref[: taps + 1, :width] + par_in[: taps + 1, :width]
    for i in range(2):
        away_s[(me & 2) + i] = own[i]
        away_s[((me & 2) ^ 2) + i] = aux[i]
    inner = jnp.sum(adjoint_ref[...] * in_ref[...], axis=0, keepdims=True)
    inner = inner * pay[state : state + 1, :]
    through = head_sums(jnp.broadcast_to(inner, (8, part)), matrix)[:, :1]
    rate = jnp.exp(hpar[:, 1:2])
    start_sums = triangle(tokens, "from")
    end_sums = triangle(tokens, "before")
    g_bias = jnp.zeros((share, 1), F32)
    g_decay = jnp.zeros((share, 1), F32)
    for c in range(chunks):
        flow = (
            flow_ref[c] + by_triangle(gy_ref[c], start_sums) + by_triangle(away_s[c], end_sums)
        ) + through
        for d in range(chunks):
            if d > c:
                flow = flow + jnp.sum(gy_ref[d], axis=1, keepdims=True)
            if d < c:
                flow = flow + jnp.sum(away_s[d], axis=1, keepdims=True)
        step = vec_ref[c, STEP]
        grad_step = ((xd_ref[c] + away_s[c]) / step - rate * flow) * vec_ref[c, SIG]
        gs_s[c] = grad_step
        g_bias = g_bias + jnp.sum(grad_step, axis=1, keepdims=True)
        g_decay = g_decay - rate * jnp.sum(flow * step, axis=1, keepdims=True)
    for k, out in enumerate((g0, g1, g2, g3)):
        out[...] = gs_s[me ^ k]
    g_skip = jnp.sum(skips + aux[2], axis=1, keepdims=True)
    lane = lax.broadcasted_iota(jnp.int32, (share, 128), 1)
    heads = jnp.where(lane == 0, g_bias, jnp.where(lane == 1, g_decay, g_skip))
    par_ref[taps + 1 :, :width] = jnp.zeros((8 - taps - 1, width), F32)
    par_ref[:, width : width + 128] = heads[:8]
    par_ref[:, width + 128 :] = heads[8:]


def conv_back_kernel(
    s, du_ref, rim_ref, wx, wb, wc, o0, o1, ext, *, far, sizes, docs, taps
):
    share, headdim, state = sizes
    me = s[0]
    plane = s[1]
    part = share * headdim
    width = part + 2 * state
    tokens = o0.shape[0]
    first = (me & 2) ^ (2 if far else 0)
    ext[: 2 * tokens, :] = du_ref[pl.ds(pl.multiple_of(first * tokens, tokens), 2 * tokens), :]
    ext[2 * tokens :, :] = jnp.where(
        first == 2, rim_ref[...], du_ref[2 * tokens : 2 * tokens + 8, :]
    )
    for k, out in enumerate((o0, o1)):
        place = (me & 1) ^ k
        pos = plane + (first + place) * tokens + lax.broadcasted_iota(jnp.int32, (tokens, 1), 0)
        valid = []
        for reach in range(1, taps):
            ahead = pos + reach
            valid.append((ahead - doc_start(ahead, s, docs) >= reach).astype(F32))
        begin = pl.multiple_of(place * tokens, tokens)
        for lo in range(0, width, 128):
            rows = ext[pl.ds(begin, tokens + 8), lo : lo + 128]
            if lo < part:
                w = wx[:, lo : lo + 128]
            elif lo < part + state:
                w = wb[:, lo - part : lo - part + 128]
            else:
                w = wc[:, lo - part - state : lo - part - state + 128]
            total = w[taps - 1 : taps] * rows[:tokens]
            for reach in range(1, taps):
                k_tap = taps - 1 - reach
                total = total + w[k_tap : k_tap + 1] * (
                    rows[reach : reach + tokens] * valid[reach - 1]
                )
            out[:, lo : lo + 128] = total.astype(BF16)


def join_kernel(s, p0, p1, p2, p3, out_ref):
    part = p0.shape[1]
    for k, ref in enumerate((p0, p1, p2, p3)):
        q = s[0] ^ k
        out_ref[:, pl.ds(pl.multiple_of(q * part, part), part)] = ref[...]


def join_small_kernel(s, first, *refs):
    groups = 4
    width = first.shape[1]
    received, steps, outs = refs[: -2 * groups], refs[-2 * groups : -groups], refs[-groups:]
    total = first[...]
    for ref in received:
        total = total + ref[...]
    for step, out in zip(steps, outs):
        tokens = step.shape[1]
        out[:, :width] = total
        out[:, width : width + tokens] = step[:8, :]
        out[:, width + tokens :] = step[8:, :]


def join_grad_kernel(s, p0, p1, p2, p3, g0, g1, g2, g3, out_ref, gs_ref, *, share, inner, state, groups):
    part = inner // groups
    for k, ref in enumerate((p0, p1, p2, p3)):
        q = s[0] ^ k
        out_ref[:, pl.ds(pl.multiple_of(q * part, part), part)] = ref[:, :part]
        out_ref[:, pl.ds(pl.multiple_of(inner + q * state, state), state)] = ref[
            :, part : part + state
        ]
        out_ref[:, pl.ds(pl.multiple_of(inner + (groups + q) * state, state), state)] = ref[
            :, part + state :
        ]
    for k, ref in enumerate((g0, g1, g2, g3)):
        tokens = gs_ref.shape[1]
        last = ref.shape[1]
        first = pl.multiple_of((s[0] ^ k) * share, share)
        gs_ref[pl.ds(first, 8), :] = ref[:, last - 2 * tokens : last - tokens]
        gs_ref[pl.ds(first + 8, 8), :] = ref[:, last - tokens :]


def join_params_kernel(
    s, p0, p1, p2, p3, conv_ref, head_ref, turned, *, share, inner, state, groups, scale
):
    part = inner // groups
    width = part + 2 * state
    rows = conv_ref.shape[0]
    for k, ref in enumerate((p0, p1, p2, p3)):
        q = s[0] ^ k
        conv_ref[:, pl.ds(pl.multiple_of(q * part, part), part)] = ref[:rows, :part] * scale
        conv_ref[:, pl.ds(pl.multiple_of(inner + q * state, state), state)] = (
            ref[:rows, part : part + state] * scale
        )
        conv_ref[:, pl.ds(pl.multiple_of(inner + (groups + q) * state, state), state)] = (
            ref[:rows, part + state : width] * scale
        )
        turned[pl.ds(pl.multiple_of(q * share, 8), 8), :] = ref[:, width : width + 128]
        turned[pl.ds(pl.multiple_of(q * share + 8, 8), 8), :] = ref[:, width + 128 : width + 256]
    head_ref[...] = turned[...].T[: head_ref.shape[0], :] * scale


def call(kernel, table, operands, specs, outs, scratch=(), name=None, vmem=True, aliases=None):
    here = pl.BlockSpec(memory_space=pltpu.VMEM)
    in_specs = [here if spec is None else spec for spec in specs]
    return pl.pallas_call(
        kernel,
        out_shape=[
            pltpu.VMEM(shape, kind) if vmem else jax.ShapeDtypeStruct(shape, kind)
            for shape, kind in outs
        ],
        grid_spec=pltpu.PrefetchScalarGridSpec(
            num_scalar_prefetch=1,
            grid=(1,),
            in_specs=in_specs,
            out_specs=[here] * len(outs),
            scratch_shapes=[pltpu.VMEM(shape, kind) for shape, kind in scratch],
        ),
        compiler_params=pltpu.CompilerParams(vmem_limit_bytes=LIMIT),
        cost_estimate=pl.CostEstimate(flops=1, transcendentals=0, bytes_accessed=1),
        name=name,
        input_output_aliases=aliases or {},
    )(table, *operands)


def swapped(value, bits):
    count = lax.axis_size("ctx")
    return lax.ppermute(value, "ctx", [(i, i ^ bits) for i in range(count)])


def shifted(value, steps):
    count = lax.axis_size("ctx")
    pairs = [(i, i + steps) for i in range(count) if 0 <= i + steps < count]
    return lax.ppermute(value, "ctx", pairs)


def after(value, *others):
    return lax.optimization_barrier((value, *others))[0]


def near_of(payload, state, direction, planes):
    near = shifted(payload, direction * GROUPS)
    covered, window = 1, planes // 2
    while 2 * covered < window:
        far = shifted(near, direction * GROUPS * covered)
        factor = near[state : state + 1]
        near = jnp.concatenate(
            [near[:state] + factor * far[:state], near[state:] * far[state:]], axis=0
        )
        covered *= 2
    return near, covered


def body(
    conv_input, step_raw, step_bias, decay_log, skip_gain, conv_weight, conv_bias, doc_lengths,
    grad_out,
):
    tokens, channels = conv_input.shape
    heads = step_raw.shape[1]
    taps = conv_weight.shape[0]
    inner = grad_out.shape[1]
    headdim = inner // heads
    groups = GROUPS
    share = heads // groups
    state = (channels - inner) // (2 * groups)
    part = inner // groups
    width = part + 2 * state
    docs = doc_lengths.shape[0]
    devices = lax.axis_size("ctx")
    planes = devices // groups
    me = lax.axis_index("ctx")
    sizes = dict(share=share, headdim=headdim, state=state)
    table = jnp.concatenate(
        [
            jnp.stack([me & (groups - 1), (me & -groups) * tokens]).astype(jnp.int32),
            doc_lengths,
        ]
    )
    bias_row = conv_bias[None, :]
    b_first = inner // state

    def column_specs(rows):
        return [
            pl.BlockSpec((rows, part), lambda i, s: (0, s[0])),
            pl.BlockSpec((rows, state), lambda i, s: (0, b_first + s[0])),
            pl.BlockSpec((rows, state), lambda i, s: (0, b_first + groups + s[0])),
        ]

    shapes = dict(share=share, inner=inner, state=state, groups=groups)
    packed = call(
        functools.partial(pack_kernel, **shapes),
        table,
        [conv_input, step_raw.T],
        [None] * 2,
        [((tokens, width + tokens), BF16)] * groups + [((16, width), BF16)] * groups,
        name="pack",
    )
    xs, edges = packed[:groups], packed[groups:]
    *gs, hpar = call(
        functools.partial(pack_grad_kernel, groups=groups),
        table,
        [grad_out, step_bias[None, :], decay_log[None, :], skip_gain[None, :]],
        [None] * 4,
        [((tokens, part), BF16)] * groups + [((share, 128), F32)],
        [((128, 128), F32)] * 2,
        name="pack_grad",
    )
    xr = [xs[0]] + [swapped(xs[k], k) for k in range(1, groups)]
    rims = []
    for k in range(groups):
        pairs = []
        for i in range(devices):
            source = i - 1 - i % 2 if k >= 2 else i - 1 - i % groups
            if source >= 0 and (source % groups) ^ (i % groups) == k:
                pairs.append((source, i))
        rims.append(lax.ppermute(edges[k], "ctx", pairs))
    conv_shapes = [
        ((groups, tokens, width), F32),
        ((groups, tokens, width), F32),
        ((groups * tokens + 16, width), BF16),
    ]
    conv_specs = column_specs(taps) + column_specs(1)
    conv_params = [conv_weight] * 3 + [bias_row] * 3
    ext_shape = ((2 * tokens + 8, width), F32)
    act, dsl, xall = call(
        functools.partial(conv_kernel, docs=docs, sizes=(share, headdim, state)),
        table,
        [xr[0], xr[1]] + conv_params,
        [None] * 2 + conv_specs,
        conv_shapes,
        [ext_shape],
        name="conv",
    )
    act, *gs = lax.optimization_barrier((act, *gs))
    gr = [gs[0]] + [swapped(gs[k], k) for k in range(1, groups)]
    act, dsl, xall, spay, schain, vec = call(
        functools.partial(conv_state_kernel, docs=docs, **sizes),
        table,
        xr + rims + conv_params + [hpar, act, dsl, xall],
        [None] * 8 + conv_specs + [None] * 4,
        conv_shapes
        + [
            ((state + 8, part), F32),
            ((groups, state, part), F32),
            ((groups, 8, share, tokens), F32),
        ],
        [ext_shape, ((groups, share, tokens), F32)],
        name="conv_state",
        aliases={16: 0, 17: 1, 18: 2},
    )
    s_near, covered = near_of(spay, state, 1, planes)
    gall, gpay, gchain = call(
        functools.partial(grad_state_kernel, **sizes),
        table,
        gr + [act, vec, spay],
        [None] * 7,
        [
            ((groups, tokens, part), BF16),
            ((state + 8, part), F32),
            ((groups, state, part), F32),
        ],
        name="grad_state",
    )
    g_near, _ = near_of(gpay, state, -1, planes)
    local_shapes = [
        ((groups, tokens, part), F32),
        ((groups, tokens, part), F32),
        ((groups, tokens, state), F32),
        ((groups, tokens, state), F32),
        ((groups, share, tokens), F32),
        ((groups, share, tokens), F32),
    ]
    locals_ = []
    for span in ((0, 1), (1, 2), (2, 4)):
        locals_ = call(
            functools.partial(local_kernel, span=span, docs=docs, **sizes),
            table,
            [act, vec, gall, schain, gchain] + list(locals_),
            [None] * (5 + len(locals_)),
            local_shapes,
            [((tokens, share * tokens), F32)] + [((tokens, part), F32)] * 2,
            name="local",
            aliases={6 + i: i for i in range(len(locals_))},
        )
        if span[1] == 1:
            s_near, *locals_ = lax.optimization_barrier((s_near, *locals_))
            s_far = shifted(s_near, GROUPS * covered)
        elif span[1] == 2:
            g_near, *locals_ = lax.optimization_barrier((g_near, *locals_))
            g_far = shifted(g_near, -GROUPS * covered)
    y_local, dx_local, db_local, dc_local, flow, xd = locals_
    *mixed, gy, state_in, dc = call(
        functools.partial(out_kernel, **sizes),
        table,
        [s_near, s_far, act, y_local, gall, vec, hpar, dc_local],
        [None] * 8,
        [((tokens, part), BF16)] * groups
        + [
            ((groups, share, tokens), F32),
            ((state, part), F32),
            ((groups, tokens, state), F32),
        ],
        name="out",
    )
    mr = [mixed[0]] + [swapped(mixed[k], k) for k in range(1, groups)]
    common = [act, dsl, dx_local, db_local, dc, gall, vec, hpar]
    edge, adjoint, high, low = call(
        functools.partial(edge_kernel, **sizes),
        table,
        [g_near, g_far] + common,
        [None] * 10,
        [
            ((8, width), F32),
            ((state, part), F32),
            ((state, part), BF16),
            ((state, part), BF16),
        ],
        name="edge",
    )
    rim_back = shifted(edge, -groups)
    triple = (share, headdim, state)
    settings = dict(sizes=triple, docs=docs, taps=taps)
    common = [high, low] + common + [xall]
    du_shape = ((groups * tokens, width), F32)
    par_shape = ((8, width + 256), F32)
    du, par_far, aux = call(
        functools.partial(back_far_kernel, **settings),
        table,
        common,
        [None] * 11,
        [du_shape, par_shape, ((3, share, tokens), F32)],
        name="back_far",
    )
    du, params, *grad_steps = call(
        functools.partial(back_near_kernel, **settings),
        table,
        common
        + [adjoint, state_in, spay, gy, flow, xd, par_far, aux, du],
        [None] * 20,
        [du_shape, par_shape] + [((share, tokens), F32)] * groups,
        [((groups, share, tokens), F32)] * 2,
        name="back_near",
        aliases={20: 0},
    )
    rim_back, *mr = lax.optimization_barrier((rim_back, *mr))
    pair_shapes = [((tokens, width), BF16)] * 2
    ext_back = [((2 * tokens + 8, width), F32)]
    back_far = call(
        functools.partial(conv_back_kernel, far=True, **settings),
        table,
        [du, rim_back] + [conv_weight] * 3,
        [None] * 2 + column_specs(taps),
        pair_shapes,
        ext_back,
        name="conv_back_far",
    )
    br_far = [swapped(back_far[k - 2], k) for k in (2, 3)]
    (mixer_out,) = call(
        join_kernel, table, mr, [None] * groups, [((tokens, inner), BF16)], name="join_out",
        vmem=False,
    )
    step = groups
    received = []
    while step < devices:
        ways = 4 if 4 * step <= devices else 2
        params = functools.reduce(jnp.add, received, params)
        received = [swapped(params, way * step) for way in range(1, ways)]
        step *= ways
    small = call(
        join_small_kernel,
        table,
        [params] + received + list(grad_steps),
        [None] * (1 + len(received) + groups),
        [((8, width + 256 + 2 * tokens), F32)] * groups,
        name="join_small",
    )
    du, br_far[0], mixer_out, *small = lax.optimization_barrier(
        (du, br_far[0], mixer_out, *small)
    )
    back_near = call(
        functools.partial(conv_back_kernel, far=False, **settings),
        table,
        [du, rim_back] + [conv_weight] * 3,
        [None] * 2 + column_specs(taps),
        pair_shapes,
        ext_back,
        name="conv_back_near",
    )
    br = [back_near[0], swapped(back_near[1], 1)] + br_far
    pr = [small[0]] + [swapped(small[k], k) for k in range(1, groups)]
    grad_conv, grad_heads = call(
        functools.partial(join_params_kernel, scale=(tokens * devices) ** (-0.5), **shapes),
        table,
        pr,
        [None] * groups,
        [((taps + 1, channels), F32), ((3, heads), F32)],
        [((heads, 128), F32)],
        name="join_params",
        vmem=False,
    )
    grad_input, grad_step = call(
        functools.partial(join_grad_kernel, **shapes),
        table,
        br + pr,
        [None] * (2 * groups),
        [((tokens, channels), BF16), ((heads, tokens), F32)],
        name="join_grad",
        vmem=False,
    )
    return mixer_out, grad_input, grad_step.T, grad_conv, grad_heads


def solution(mesh):
    rows = P(("groups", "ctx"), None)
    return jax.shard_map(
        body,
        mesh=mesh,
        in_specs=(rows, rows, P(), P(), P(), P(), P(), P("groups"), rows),
        out_specs=(rows, rows, rows, P("groups", None), P("groups", None)),
        check_vma=False,
    )
```

```python
import functools

import jax
import jax.numpy as jnp
from jax import lax
from jax.experimental import pallas as pl
from jax.experimental.pallas import tpu as pltpu
from jax.sharding import PartitionSpec as P

GROUPS = 4
F32 = jnp.float32
BF16 = jnp.bfloat16
NEG = -1e30
LIMIT = 12 * 1024 * 1024
STEP, CUM, TAIL, HEAD, TP, HP, WHOLE, SIG = range(8)

NN = (((1,), (0,)), ((), ()))
NT = (((1,), (1,)), ((), ()))
TN = (((0,), (0,)), ((), ()))


def mm(a, b, dims):
    return lax.dot_general(a, b, dims, preferred_element_type=F32)


def halves(a):
    high = a.astype(BF16)
    return high, (a - high.astype(F32)).astype(BF16)


def thirds(a):
    high = a.astype(BF16)
    rest = a - high.astype(F32)
    mid = rest.astype(BF16)
    return high, mid, (rest - mid.astype(F32)).astype(BF16)


def dot3(a, b, dims):
    return joined3(halves(a), halves(b), dims)


def joined3(a, b, dims):
    (ah, al), (bh, bl) = a, b
    (left,), (right,) = dims[0]
    if ah.shape[left] > 128:
        return mm(ah, bh, dims) + (mm(ah, bl, dims) + mm(al, bh, dims))
    both = mm(
        jnp.concatenate([ah, al], axis=left), jnp.concatenate([bh, bh], axis=right), dims
    )
    return both + mm(ah, bl, dims)


def spread_matrix(share, headdim):
    lanes = lax.broadcasted_iota(jnp.int32, (share, share * headdim), 1)
    rows = lax.broadcasted_iota(jnp.int32, (share, share * headdim), 0)
    return (lanes // headdim == rows).astype(BF16)


def spread(values, matrix):
    return mm(
        jnp.concatenate(thirds(values), axis=0), jnp.concatenate([matrix] * 3, axis=0), TN
    )


def skip_row(hpar, matrix):
    return spread(jnp.broadcast_to(hpar[:, 2:3], (hpar.shape[0], 8)), matrix)[:1]


def head_sums(products, matrix):
    high, low = halves(products)
    return mm(matrix, high, NT) + mm(matrix, low, NT)


def by_triangle(values, triangle):
    high, mid, low = thirds(values)
    return mm(high, triangle, NN) + (mm(mid, triangle, NN) + mm(low, triangle, NN))


def triangle(size, kind):
    rows = lax.broadcasted_iota(jnp.int32, (size, size), 0)
    cols = lax.broadcasted_iota(jnp.int32, (size, size), 1)
    kept = {"upto": rows <= cols, "before": rows < cols, "from": rows >= cols}[kind]
    return kept.astype(BF16)


def doc_start(position, table, docs):
    start = jnp.zeros_like(position)
    first = table[2]
    for i in range(1, docs):
        start = jnp.where(first <= position, first, start)
        first = first + table[2 + i]
    return start


def pack_kernel(s, x_ref, step_ref, *refs, share, inner, state, groups):
    outs, rims = refs[:groups], refs[groups:]
    me = s[0]
    tokens = x_ref.shape[0]
    part = inner // groups
    width = part + 2 * state
    for k in range(groups):
        q = me ^ k
        xs = outs[k]
        xs[:tokens, :part] = x_ref[:, pl.ds(pl.multiple_of(q * part, part), part)]
        xs[:tokens, part : part + state] = x_ref[
            :, pl.ds(pl.multiple_of(inner + q * state, state), state)
        ]
        xs[:tokens, part + state :] = x_ref[
            :, pl.ds(pl.multiple_of(inner + (groups + q) * state, state), state)
        ]
        rims[k][...] = xs[tokens - 16 : tokens, :]
        xs[tokens:, :] = jnp.zeros((8, width), BF16)
        place = 0
        for row in range(0, share, 8):
            raw = step_ref[pl.ds(pl.multiple_of(q * share + row, 8), 8), :]
            for piece in thirds(raw):
                xs[tokens:, place : place + tokens] = piece
                place += tokens


def pack_grad_kernel(s, g_ref, bias, decay, skip, *refs, groups):
    outs, hpar, wide, turned = refs[:groups], *refs[groups:]
    heads = bias.shape[1]
    share = heads // groups
    wide[...] = jnp.zeros_like(wide)
    for i, ref in enumerate((bias, decay, skip)):
        wide[i : i + 1, :heads] = ref[...]
    turned[...] = wide[...].T
    hpar[...] = turned[pl.ds(pl.multiple_of(s[0] * share, share), share), :]
    part = outs[0].shape[1]
    for k, out in enumerate(outs):
        q = s[0] ^ k
        out[...] = g_ref[:, pl.ds(pl.multiple_of(q * part, part), part)]


def activate(rows, weight, bias, valid, paired):
    taps = weight.shape[0]
    tokens = rows.shape[0] - 8
    u = jnp.zeros((tokens, rows.shape[1]), F32) + bias
    for k in range(taps):
        reach = taps - 1 - k
        moved = rows[8 - reach : 8 - reach + tokens]
        if reach:
            moved = moved * valid[reach]
        u = u + weight[k : k + 1] * moved
    sig = 1.0 / (1.0 + jnp.exp(-u))
    value = u * sig
    if paired:
        high, low = halves(value)
        value = high.astype(F32) + low.astype(F32)
    return value, sig * (1.0 + u * (1.0 - sig))


def convolve_head(s, first, rim, wx, wb, wc, bx, bb, bc, act_ref, dsl_ref, xall_ref, sizes, docs):
    share, headdim, state = sizes
    part = share * headdim
    tokens = act_ref.shape[1]
    pos = s[1] + first * tokens + lax.broadcasted_iota(jnp.int32, (8, 1), 0)
    inside = pos - doc_start(pos, s, docs)
    valid = [(inside >= reach).astype(F32) for reach in range(wx.shape[0])]
    own = xall_ref[pl.ds(pl.multiple_of(16 + first * tokens, 16), 16), :].astype(F32)
    rows = jnp.concatenate([rim[8:], own[:8]], axis=0)
    for lo, size, w_ref, b_ref in (
        (0, part, wx, bx), (part, state, wb, bb), (part + state, state, wc, bc)
    ):
        value, slope = activate(rows[:, lo : lo + size], w_ref[...], b_ref[...], valid, lo == 0)
        act_ref[first, :8, lo : lo + size] = value
        dsl_ref[first, :8, lo : lo + size] = slope


def convolve_pair(s, first, pieces, rim, wx, wb, wc, bx, bb, bc, act_ref, dsl_ref, xall_ref, ext,
                  sizes, docs):
    me, plane = s[0], s[1]
    share, headdim, state = sizes
    part = share * headdim
    width = part + 2 * state
    tokens = act_ref.shape[1]
    taps = wx.shape[0]
    ext[:8, :] = rim[8:]
    for k, ref in enumerate(pieces):
        place = (me & 1) ^ k
        value = ref[:tokens, :]
        ext[pl.ds(pl.multiple_of(8 + place * tokens, 8), tokens), :] = value.astype(F32)
        xall_ref[pl.ds(pl.multiple_of(16 + (first + place) * tokens, 16), tokens), :] = value

    for c in range(2):
        chunk = first + c
        pos = plane + chunk * tokens + lax.broadcasted_iota(jnp.int32, (tokens, 1), 0)
        inside = pos - doc_start(pos, s, docs)
        valid = [(inside >= reach).astype(F32) for reach in range(taps)]

        def convolve(lo, w_ref, b_ref, wlo, paired):
            rows = ext[c * tokens : c * tokens + tokens + 8, lo : lo + 128]
            value, slope = activate(
                rows, w_ref[:, wlo : wlo + 128], b_ref[:, wlo : wlo + 128], valid, paired
            )
            act_ref[chunk, :, lo : lo + 128] = value
            dsl_ref[chunk, :, lo : lo + 128] = slope

        for lo in range(0, part, 128):
            convolve(lo, wx, bx, lo, True)
        for lo in range(0, state, 128):
            convolve(part + lo, wb, bb, lo, False)
            convolve(part + state + lo, wc, bc, lo, False)


def conv_kernel(
    s, x0, x1, wx, wb, wc, bx, bb, bc, act_ref, dsl_ref, xall_ref, ext, *, sizes, docs
):
    rim = jnp.zeros((16, ext.shape[1]), F32)
    convolve_pair(
        s, s[0] & 2, (x0, x1), rim, wx, wb, wc, bx, bb, bc, act_ref, dsl_ref, xall_ref, ext,
        sizes, docs,
    )


def conv_state_kernel(
    s, x0, x1, x2, x3, r0, r1, r2, r3, wx, wb, wc, bx, bb, bc, hpar, act_in, dsl_in, xall_in,
    act_ref, dsl_ref, xall_ref, pay_ref, chain_ref, vec_ref,
    ext, raws, *, share, headdim, state, docs,
):
    me = s[0]
    plane = s[1]
    part = share * headdim
    width = part + 2 * state
    tokens = act_ref.shape[1]
    chunks = 4
    for k, ref in enumerate((x0, x1, x2, x3)):
        block = ref[tokens:, :].astype(F32)
        for i in range(share // 8):
            lo = 3 * i * tokens
            raws[me ^ k, 8 * i : 8 * i + 8] = (
                block[:, lo : lo + tokens]
                + block[:, lo + tokens : lo + 2 * tokens]
                + block[:, lo + 2 * tokens : lo + 3 * tokens]
            )
    upper_chip = (me & 2) == 2
    inner_rim = xall_ref[2 * tokens : 2 * tokens + 16, :].astype(F32)
    rim = jnp.where(upper_chip, r0[...].astype(F32) + r1[...].astype(F32), inner_rim)

    own_rim = r2[...].astype(F32) + r3[...].astype(F32)
    xall_ref[:16, :] = jnp.where(upper_chip, rim, own_rim).astype(BF16)
    convolve_head(
        s, me & 2, own_rim, wx, wb, wc, bx, bb, bc, act_ref, dsl_ref, xall_ref,
        (share, headdim, state), docs,
    )
    convolve_pair(
        s, (me & 2) ^ 2, (x2, x3), rim, wx, wb, wc, bx, bb, bc, act_ref, dsl_ref, xall_ref, ext,
        (share, headdim, state), docs,
    )

    bias = hpar[:, 0:1]
    rate = jnp.exp(hpar[:, 1:2])
    upper = triangle(tokens, "upto")
    before = jnp.zeros((share, 1), F32)
    cums, steps, ends = [], [], []
    for c in range(chunks):
        v = raws[c] + bias
        step = jnp.maximum(v, 0.0) + jnp.log1p(jnp.exp(-jnp.abs(v)))
        cum = by_triangle(-step * rate, upper)
        vec_ref[c, STEP] = step
        vec_ref[c, CUM] = cum
        vec_ref[c, SIG] = 1.0 / (1.0 + jnp.exp(-v))
        cums.append(cum)
        steps.append(step)
        ends.append(cum[:, tokens - 1 :])
    total = ends[0] + ends[1] + ends[2] + ends[3]
    last_plane = doc_start(plane + chunks * tokens - 1, s, docs)
    for c in range(chunks):
        base = plane + c * tokens
        pos = base + lax.broadcasted_iota(jnp.int32, (1, tokens), 1)
        start = doc_start(pos, s, docs)
        last = doc_start(base + tokens - 1, s, docs)
        cum, step, end = cums[c], steps[c], ends[c]
        vec_ref[c, TAIL] = jnp.exp(end - cum) * step * (pos >= last).astype(F32)
        vec_ref[c, HEAD] = jnp.exp(cum) * (start < base).astype(F32)
        vec_ref[c, HP] = jnp.exp(cum + before) * (start < plane).astype(F32)
        before = before + end
        vec_ref[c, TP] = (
            jnp.exp(total - before + (end - cum)) * step * (pos >= last_plane).astype(F32)
        )
        open_c = jnp.where(last < base, 1.0, 0.0)
        vec_ref[c, WHOLE] = jnp.broadcast_to(jnp.exp(end) * open_c, (share, tokens))
    matrix = spread_matrix(share, headdim)
    open_plane = jnp.where(last_plane < plane, 1.0, 0.0)
    pay_ref[state:, :] = spread(jnp.broadcast_to(jnp.exp(total) * open_plane, (share, 8)), matrix)

    carried = jnp.zeros((state, part), F32)
    for c in range(chunks):
        chain_ref[c] = carried
        weighted = act_ref[c, :, :part] * spread(vec_ref[c, TAIL], matrix)
        local = dot3(act_ref[c, :, part : part + state], weighted, TN)
        carried = carried * spread(vec_ref[c, WHOLE], matrix) + local
    pay_ref[:state, :] = carried


def grad_state_kernel(
    s, g0, g1, g2, g3, act_ref, vec_ref, pay_in, gall_ref, pay_ref, chain_ref,
    *, share, headdim, state,
):
    me = s[0]
    part = share * headdim
    chunks = 4
    for k, ref in enumerate((g0, g1, g2, g3)):
        gall_ref[me ^ k] = ref[...]
    matrix = spread_matrix(share, headdim)
    carried = jnp.zeros((state, part), F32)
    for c in range(chunks - 1, -1, -1):
        chain_ref[c] = carried
        weighted = gall_ref[c].astype(F32) * spread(vec_ref[c, HEAD], matrix)
        local = dot3(act_ref[c, :, part + state :], weighted, TN)
        carried = carried * spread(vec_ref[c, WHOLE], matrix) + local
    pay_ref[:state, :] = carried
    pay_ref[state:, :] = pay_in[state:, :]


def within_chunk(s, c, g_ref, act_ref, vec_ref, y_ref, dx_ref, db_ref, dc_ref, wide, sizes, docs):
    share, headdim, state = sizes
    part = share * headdim
    tokens = act_ref.shape[1]
    lanes = lax.broadcasted_iota(jnp.int32, (tokens, 2 * headdim), 1)
    left = lanes < headdim
    base = s[1] + c * tokens
    tpos = base + lax.broadcasted_iota(jnp.int32, (tokens, tokens), 0)
    spos = base + lax.broadcasted_iota(jnp.int32, (tokens, tokens), 1)
    tstart = doc_start(tpos, s, docs)
    mask = jnp.where((spos <= tpos) & (spos >= tstart), 0.0, NEG)
    b = act_ref[c, :, part : part + state]
    cc = act_ref[c, :, part + state :]
    m = dot3(cc, b, NT)
    cum = vec_ref[c, CUM]
    step = vec_ref[c, STEP]
    wide[...] = spread(cum, spread_matrix(share, tokens))
    dm = jnp.zeros((tokens, tokens), F32)
    for pair in range(share // 2):
        lo = pair * 2 * headdim
        xp = act_ref[c, :, lo : lo + 2 * headdim]
        gp = g_ref[:, lo : lo + 2 * headdim]
        zero = jnp.zeros_like(gp)
        gst = jnp.concatenate([jnp.where(left, gp, zero), jnp.where(left, zero, gp)], axis=0)
        factors = []
        for h in (2 * pair, 2 * pair + 1):
            diff = wide[:, h * tokens : (h + 1) * tokens] - cum[h : h + 1, :]
            factors.append(jnp.exp(diff + mask) * step[h : h + 1, :])
        pieces = jnp.concatenate(halves(xp), axis=1)
        dw = mm(jnp.concatenate([gst, gst], axis=1), pieces, NT)
        dm = dm + dw[:tokens] * factors[0] + dw[tokens:] * factors[1]
        w = jnp.concatenate([m * factors[0], m * factors[1]], axis=0)
        w = jnp.concatenate(halves(w), axis=1)
        yst = mm(w, jnp.concatenate([pieces, pieces], axis=0), NN)
        yst = yst[:, : 2 * headdim] + yst[:, 2 * headdim :]
        y_ref[c, :, lo : lo + 2 * headdim] = jnp.where(left, yst[:tokens], yst[tokens:])
        dst = mm(w, gst, TN)
        dx_ref[c, :, lo : lo + 2 * headdim] = dst[:tokens] + dst[tokens:]
    dc_ref[c] = dot3(dm, b, NN)
    db_ref[c] = dot3(dm, cc, TN)


def within_kernel(
    s, act_ref, vec_ref, g_ref, y_ref, dx_ref, db_ref, dc_ref, wide, *, sizes, docs
):
    within_chunk(
        s, s[0], g_ref, act_ref, vec_ref, y_ref, dx_ref, db_ref, dc_ref, wide, sizes, docs
    )


def local_kernel(
    s, act_ref, vec_ref, gall_ref, schain, gchain, *refs, span, sizes, docs,
):
    y_ref, dx_ref, db_ref, dc_ref, flow_ref, xd_ref, wide = refs[-7:]
    share, headdim, state = sizes
    part = share * headdim
    tokens = act_ref.shape[1]
    matrix = spread_matrix(share, headdim)
    start_sums = triangle(tokens, "from")
    end_sums = triangle(tokens, "before")

    def across(c):
        b = act_ref[c, :, part : part + state]
        cc = act_ref[c, :, part + state :]
        head_in = spread(vec_ref[c, HEAD], matrix)
        tail = spread(vec_ref[c, TAIL], matrix)
        x = act_ref[c, :, :part]
        g = gall_ref[c].astype(F32)
        y = y_ref[c] + head_in * dot3(cc, schain[c], NN)
        y_ref[c] = y
        dx_tail = tail * dot3(b, gchain[c], NN)
        dx_near = dx_ref[c]
        near = head_sums(x * dx_near, matrix)
        away = head_sums(x * dx_tail, matrix)
        dx_ref[c] = dx_near + dx_tail
        xd_ref[c] = near + away
        inner = jnp.sum(schain[c] * gchain[c], axis=0, keepdims=True)
        through = head_sums(jnp.broadcast_to(inner, (8, part)), matrix)[:, :1]
        flow_ref[c] = (
            by_triangle(head_sums(g * y, matrix) - near, start_sums)
            + by_triangle(away, end_sums)
            + through * vec_ref[c, WHOLE]
        )
        dc_ref[c] = dc_ref[c] + dot3(g * head_in, schain[c], NT)
        db_ref[c] = db_ref[c] + dot3(x * tail, gchain[c], NT)

    def chunk(k, carry):
        c = s[0] ^ k
        within_chunk(
            s, c, gall_ref.at[c], act_ref, vec_ref, y_ref, dx_ref, db_ref, dc_ref, wide, sizes,
            docs,
        )
        across(c)
        return carry

    if span[0] == 0:
        across(s[0])
    lax.fori_loop(max(span[0], 1), span[1], chunk, 0)


def out_kernel(
    s, one, two, act_ref, y_ref, gall_ref, vec_ref, hpar, dcl_ref,
    m0, m1, m2, m3, gy_ref, in_ref, dc_ref, *, share, headdim, state,
):
    me = s[0]
    part = share * headdim
    matrix = spread_matrix(share, headdim)
    arrived = one[:state, :] + one[state : state + 1, :] * two[:state, :]
    in_ref[...] = arrived
    ih, il = halves(arrived)
    skip = skip_row(hpar, matrix)
    for k, out in enumerate((m0, m1, m2, m3)):
        c = me ^ k
        reach = spread(vec_ref[c, HP], matrix)
        ch, cl = halves(act_ref[c, :, part + state :])
        carry = joined3((ch, cl), (ih, il), NN)
        y = reach * carry
        g = gall_ref[c].astype(F32)
        gy_ref[c] = head_sums(g * y, matrix)
        y = y + y_ref[c]
        out[...] = (y + skip * act_ref[c, :, :part]).astype(BF16)
        gh, gl = halves(g * reach)
        dc_ref[c] = dcl_ref[c] + mm(gh, ih, NT) + (mm(gh, il, NT) + mm(gl, ih, NT))


def input_grads(c, rows, high, low, act_ref, dsl_ref, dxl_ref, dbl_ref, dc_ref, gall_ref, vec_ref,
                skip, matrix, part, state):
    x = act_ref[c, :rows, :part]
    g = gall_ref[c, :rows].astype(F32)
    tail = spread(vec_ref[c, TP][:, :rows], matrix)
    bh, bl = halves(act_ref[c, :rows, part : part + state])
    far = tail * joined3((bh, bl), (high, low), NN)
    xh, xl = halves(x * tail)
    db = dbl_ref[c, :rows] + mm(xh, high, NT) + (mm(xh, low, NT) + mm(xl, high, NT))
    dx = far + dxl_ref[c, :rows] + skip * g
    return (
        dx * dsl_ref[c, :rows, :part],
        db * dsl_ref[c, :rows, part : part + state],
        dc_ref[c, :rows] * dsl_ref[c, :rows, part + state :],
        x * far,
        g * x,
    )


def edge_kernel(
    s, one, two, act_ref, dsl_ref, dxl_ref, dbl_ref, dc_ref, gall_ref, vec_ref, hpar,
    edge_ref, adjoint_ref, high_ref, low_ref, *, share, headdim, state,
):
    part = share * headdim
    matrix = spread_matrix(share, headdim)
    adjoint = one[:state, :] + one[state : state + 1, :] * two[:state, :]
    adjoint_ref[...] = adjoint
    high, low = halves(adjoint)
    high_ref[...] = high
    low_ref[...] = low
    grads = input_grads(
        0, 16, high, low, act_ref, dsl_ref, dxl_ref, dbl_ref, dc_ref, gall_ref, vec_ref,
        skip_row(hpar, matrix), matrix, part, state,
    )
    edge_ref[:, :part] = grads[0][:8]
    edge_ref[:, part : part + state] = grads[1][:8]
    edge_ref[:, part + state :] = grads[2][:8]


def pair_grads(s, first, high_ref, low_ref, act_ref, dsl_ref, dxl_ref, dbl_ref, dc_ref, gall_ref,
               vec_ref, hpar, xall_ref, du_ref, par_ref, sizes, docs, taps):
    share, headdim, state = sizes
    part = share * headdim
    width = part + 2 * state
    tokens = act_ref.shape[1]
    plane = s[1]
    matrix = spread_matrix(share, headdim)
    skip = skip_row(hpar, matrix)
    high, low = high_ref[...], low_ref[...]
    away, skips = [], []
    for i in range(2):
        c = first + i
        grads = input_grads(
            c, tokens, high, low, act_ref, dsl_ref, dxl_ref, dbl_ref, dc_ref, gall_ref, vec_ref,
            skip, matrix, part, state,
        )
        rows = pl.ds(pl.multiple_of(c * tokens, tokens), tokens)
        du_ref[rows, :part] = grads[0]
        du_ref[rows, part : part + state] = grads[1]
        du_ref[rows, part + state : width] = grads[2]
        away.append(head_sums(grads[3], matrix))
        skips.append(head_sums(grads[4], matrix))
    for lo in range(0, width, 128):
        sums = [jnp.zeros((8, 128), F32) for _ in range(taps + 1)]
        for i in range(2):
            c = first + i
            begin = pl.multiple_of(c * tokens, tokens)
            rows = xall_ref[pl.ds(begin, tokens + 16), lo : lo + 128].astype(F32)
            pos = plane + c * tokens + lax.broadcasted_iota(jnp.int32, (tokens, 1), 0)
            inside = pos - doc_start(pos, s, docs)
            du = du_ref[pl.ds(begin, tokens), lo : lo + 128]
            for k in range(taps):
                reach = taps - 1 - k
                moved = rows[16 - reach : 16 - reach + tokens]
                if reach:
                    moved = moved * (inside >= reach).astype(F32)
                sums[k] = sums[k] + jnp.sum((du * moved).reshape(tokens // 8, 8, 128), axis=0)
            sums[taps] = sums[taps] + jnp.sum(du.reshape(tokens // 8, 8, 128), axis=0)
        for k in range(taps + 1):
            par_ref[k : k + 1, lo : lo + 128] = jnp.sum(sums[k], axis=0, keepdims=True)
    return away, skips[0] + skips[1]


def back_far_kernel(
    s, high_ref, low_ref, act_ref, dsl_ref, dxl_ref, dbl_ref, dc_ref, gall_ref, vec_ref, hpar,
    xall_ref, du_ref, par_ref, aux_ref, *, sizes, docs, taps,
):
    share, headdim, state = sizes
    part = share * headdim
    width = part + 2 * state
    tokens = act_ref.shape[1]
    par_ref[...] = jnp.zeros_like(par_ref)
    away, skips = pair_grads(
        s, (s[0] & 2) ^ 2, high_ref, low_ref, act_ref, dsl_ref, dxl_ref, dbl_ref, dc_ref, gall_ref,
        vec_ref, hpar, xall_ref, du_ref, par_ref, sizes, docs, taps,
    )
    aux_ref[0], aux_ref[1], aux_ref[2] = away[0], away[1], skips


def back_near_kernel(
    s, high_ref, low_ref, act_ref, dsl_ref, dxl_ref, dbl_ref, dc_ref, gall_ref, vec_ref, hpar,
    xall_ref, adjoint_ref, in_ref, pay, gy_ref, flow_ref, xd_ref, par_in, aux, du_in,
    du_ref, par_ref, g0, g1, g2, g3, away_s, gs_s, *, sizes, docs, taps,
):
    share, headdim, state = sizes
    part = share * headdim
    width = part + 2 * state
    tokens = act_ref.shape[1]
    chunks = 4
    me = s[0]
    matrix = spread_matrix(share, headdim)
    own, skips = pair_grads(
        s, me & 2, high_ref, low_ref, act_ref, dsl_ref, dxl_ref, dbl_ref, dc_ref, gall_ref,
        vec_ref, hpar, xall_ref, du_ref, par_ref, sizes, docs, taps,
    )
    par_ref[: taps + 1, :width] = par_ref[: taps + 1, :width] + par_in[: taps + 1, :width]
    for i in range(2):
        away_s[(me & 2) + i] = own[i]
        away_s[((me & 2) ^ 2) + i] = aux[i]
    inner = jnp.sum(adjoint_ref[...] * in_ref[...], axis=0, keepdims=True)
    inner = inner * pay[state : state + 1, :]
    through = head_sums(jnp.broadcast_to(inner, (8, part)), matrix)[:, :1]
    rate = jnp.exp(hpar[:, 1:2])
    start_sums = triangle(tokens, "from")
    end_sums = triangle(tokens, "before")
    g_bias = jnp.zeros((share, 1), F32)
    g_decay = jnp.zeros((share, 1), F32)
    for c in range(chunks):
        flow = (
            flow_ref[c] + by_triangle(gy_ref[c], start_sums) + by_triangle(away_s[c], end_sums)
        ) + through
        for d in range(chunks):
            if d > c:
                flow = flow + jnp.sum(gy_ref[d], axis=1, keepdims=True)
            if d < c:
                flow = flow + jnp.sum(away_s[d], axis=1, keepdims=True)
        step = vec_ref[c, STEP]
        grad_step = ((xd_ref[c] + away_s[c]) / step - rate * flow) * vec_ref[c, SIG]
        gs_s[c] = grad_step
        g_bias = g_bias + jnp.sum(grad_step, axis=1, keepdims=True)
        g_decay = g_decay - rate * jnp.sum(flow * step, axis=1, keepdims=True)
    for k, out in enumerate((g0, g1, g2, g3)):
        out[...] = gs_s[me ^ k]
    g_skip = jnp.sum(skips + aux[2], axis=1, keepdims=True)
    lane = lax.broadcasted_iota(jnp.int32, (share, 128), 1)
    heads = jnp.where(lane == 0, g_bias, jnp.where(lane == 1, g_decay, g_skip))
    par_ref[taps + 1 :, :width] = jnp.zeros((8 - taps - 1, width), F32)
    par_ref[:, width : width + 128] = heads[:8]
    par_ref[:, width + 128 :] = heads[8:]


def conv_back_kernel(
    s, du_ref, rim_ref, wx, wb, wc, o0, o1, ext, *, far, sizes, docs, taps
):
    share, headdim, state = sizes
    me = s[0]
    plane = s[1]
    part = share * headdim
    width = part + 2 * state
    tokens = o0.shape[0]
    first = (me & 2) ^ (2 if far else 0)
    ext[: 2 * tokens, :] = du_ref[pl.ds(pl.multiple_of(first * tokens, tokens), 2 * tokens), :]
    ext[2 * tokens :, :] = jnp.where(
        first == 2, rim_ref[...], du_ref[2 * tokens : 2 * tokens + 8, :]
    )
    for k, out in enumerate((o0, o1)):
        place = (me & 1) ^ k
        pos = plane + (first + place) * tokens + lax.broadcasted_iota(jnp.int32, (tokens, 1), 0)
        valid = []
        for reach in range(1, taps):
            ahead = pos + reach
            valid.append((ahead - doc_start(ahead, s, docs) >= reach).astype(F32))
        begin = pl.multiple_of(place * tokens, tokens)
        for lo in range(0, width, 128):
            rows = ext[pl.ds(begin, tokens + 8), lo : lo + 128]
            if lo < part:
                w = wx[:, lo : lo + 128]
            elif lo < part + state:
                w = wb[:, lo - part : lo - part + 128]
            else:
                w = wc[:, lo - part - state : lo - part - state + 128]
            total = w[taps - 1 : taps] * rows[:tokens]
            for reach in range(1, taps):
                k_tap = taps - 1 - reach
                total = total + w[k_tap : k_tap + 1] * (
                    rows[reach : reach + tokens] * valid[reach - 1]
                )
            out[:, lo : lo + 128] = total.astype(BF16)


def join_kernel(s, p0, p1, p2, p3, out_ref, done):
    part = p0.shape[1]
    copies = []
    for k, ref in enumerate((p0, p1, p2, p3)):
        columns = pl.ds(pl.multiple_of((s[0] ^ k) * part, part), part)
        copies.append(pltpu.make_async_copy(ref, out_ref.at[:, columns], done.at[k]))
    for copy in copies:
        copy.start()
    for copy in copies:
        copy.wait()


def join_small_kernel(s, first, *refs):
    groups = 4
    width = first.shape[1]
    received, steps, outs = refs[: -2 * groups], refs[-2 * groups : -groups], refs[-groups:]
    total = first[...]
    for ref in received:
        total = total + ref[...]
    for step, out in zip(steps, outs):
        tokens = step.shape[1]
        out[:, :width] = total
        out[:, width : width + tokens] = step[:8, :]
        out[:, width + tokens :] = step[8:, :]


def join_grads_kernel(
    s, p0, p1, p2, p3, g0, g1, g2, g3, out_ref, gs_ref, conv_ref, head_ref, turned, done,
    *, share, inner, state, groups, scale,
):
    part = inner // groups
    width = part + 2 * state
    copies = []
    for k, ref in enumerate((p0, p1, p2, p3)):
        q = s[0] ^ k
        for i, (size, lo, first) in enumerate((
            (part, 0, q * part),
            (state, part, inner + q * state),
            (state, part + state, inner + (groups + q) * state),
        )):
            columns = pl.ds(pl.multiple_of(first, size), size)
            copies.append(
                pltpu.make_async_copy(
                    ref.at[:, lo : lo + size], out_ref.at[:, columns], done.at[3 * k + i]
                )
            )
    for copy in copies:
        copy.start()
    rows = conv_ref.shape[0]
    tokens = gs_ref.shape[1]
    for k, ref in enumerate((g0, g1, g2, g3)):
        q = s[0] ^ k
        conv_ref[:, pl.ds(pl.multiple_of(q * part, part), part)] = ref[:rows, :part] * scale
        conv_ref[:, pl.ds(pl.multiple_of(inner + q * state, state), state)] = (
            ref[:rows, part : part + state] * scale
        )
        conv_ref[:, pl.ds(pl.multiple_of(inner + (groups + q) * state, state), state)] = (
            ref[:rows, part + state : width] * scale
        )
        first = pl.multiple_of(q * share, share)
        turned[pl.ds(first, 8), :] = ref[:, width : width + 128]
        turned[pl.ds(first + 8, 8), :] = ref[:, width + 128 : width + 256]
        last = width + 256
        gs_ref[pl.ds(first, 8), :] = ref[:, last : last + tokens]
        gs_ref[pl.ds(first + 8, 8), :] = ref[:, last + tokens :]
    head_ref[...] = turned[...].T[: head_ref.shape[0], :] * scale
    for copy in copies:
        copy.wait()


def call(kernel, table, operands, specs, outs, scratch=(), name=None, vmem=True, aliases=None,
         far=()):
    here = pl.BlockSpec(memory_space=pltpu.VMEM)
    in_specs = [here if spec is None else spec for spec in specs]
    return pl.pallas_call(
        kernel,
        out_shape=[
            pltpu.VMEM(shape, kind) if vmem else jax.ShapeDtypeStruct(shape, kind)
            for shape, kind in outs
        ],
        grid_spec=pltpu.PrefetchScalarGridSpec(
            num_scalar_prefetch=1,
            grid=(1,),
            in_specs=in_specs,
            out_specs=[
                pl.BlockSpec(memory_space=pl.ANY) if i in far else here for i in range(len(outs))
            ],
            scratch_shapes=[
                pltpu.VMEM(*entry) if isinstance(entry, tuple) else entry for entry in scratch
            ],
        ),
        compiler_params=pltpu.CompilerParams(vmem_limit_bytes=LIMIT),
        cost_estimate=pl.CostEstimate(flops=1, transcendentals=0, bytes_accessed=1),
        name=name,
        input_output_aliases=aliases or {},
    )(table, *operands)


def swapped(value, bits):
    count = lax.axis_size("ctx")
    return lax.ppermute(value, "ctx", [(i, i ^ bits) for i in range(count)])


def shifted(value, steps):
    count = lax.axis_size("ctx")
    pairs = [(i, i + steps) for i in range(count) if 0 <= i + steps < count]
    return lax.ppermute(value, "ctx", pairs)


def after(value, *others):
    return lax.optimization_barrier((value, *others))[0]


def near_of(payload, state, direction, planes):
    near = shifted(payload, direction * GROUPS)
    covered, window = 1, planes // 2
    while 2 * covered < window:
        far = shifted(near, direction * GROUPS * covered)
        factor = near[state : state + 1]
        near = jnp.concatenate(
            [near[:state] + factor * far[:state], near[state:] * far[state:]], axis=0
        )
        covered *= 2
    return near, covered


def body(
    conv_input, step_raw, step_bias, decay_log, skip_gain, conv_weight, conv_bias, doc_lengths,
    grad_out,
):
    tokens, channels = conv_input.shape
    heads = step_raw.shape[1]
    taps = conv_weight.shape[0]
    inner = grad_out.shape[1]
    headdim = inner // heads
    groups = GROUPS
    share = heads // groups
    state = (channels - inner) // (2 * groups)
    part = inner // groups
    width = part + 2 * state
    docs = doc_lengths.shape[0]
    devices = lax.axis_size("ctx")
    planes = devices // groups
    me = lax.axis_index("ctx")
    sizes = dict(share=share, headdim=headdim, state=state)
    table = jnp.concatenate(
        [
            jnp.stack([me & (groups - 1), (me & -groups) * tokens]).astype(jnp.int32),
            doc_lengths,
        ]
    )
    bias_row = conv_bias[None, :]
    b_first = inner // state

    def column_specs(rows):
        return [
            pl.BlockSpec((rows, part), lambda i, s: (0, s[0])),
            pl.BlockSpec((rows, state), lambda i, s: (0, b_first + s[0])),
            pl.BlockSpec((rows, state), lambda i, s: (0, b_first + groups + s[0])),
        ]

    shapes = dict(share=share, inner=inner, state=state, groups=groups)
    packed = call(
        functools.partial(pack_kernel, **shapes),
        table,
        [conv_input, step_raw.T],
        [None] * 2,
        [((tokens + 8, width), BF16)] * groups + [((16, width), BF16)] * groups,
        name="pack",
    )
    xs, edges = packed[:groups], packed[groups:]
    *gs, hpar = call(
        functools.partial(pack_grad_kernel, groups=groups),
        table,
        [grad_out, step_bias[None, :], decay_log[None, :], skip_gain[None, :]],
        [None] * 4,
        [((tokens, part), BF16)] * groups + [((share, 128), F32)],
        [((128, 128), F32)] * 2,
        name="pack_grad",
    )
    xr = [xs[0]] + [swapped(xs[k], k) for k in range(1, groups)]
    rims = []
    for k in range(groups):
        pairs = []
        for i in range(devices):
            source = i - 1 - i % 2 if k >= 2 else i - 1 - i % groups
            if source >= 0 and (source % groups) ^ (i % groups) == k:
                pairs.append((source, i))
        rims.append(lax.ppermute(edges[k], "ctx", pairs))
    conv_shapes = [
        ((groups, tokens, width), F32),
        ((groups, tokens, width), F32),
        ((groups * tokens + 16, width), BF16),
    ]
    conv_specs = column_specs(taps) + column_specs(1)
    conv_params = [conv_weight] * 3 + [bias_row] * 3
    ext_shape = ((2 * tokens + 8, width), F32)
    act, dsl, xall = call(
        functools.partial(conv_kernel, docs=docs, sizes=(share, headdim, state)),
        table,
        [xr[0], xr[1]] + conv_params,
        [None] * 2 + conv_specs,
        conv_shapes,
        [ext_shape],
        name="conv",
    )
    act, *gs = lax.optimization_barrier((act, *gs))
    gr = [gs[0]] + [swapped(gs[k], k) for k in range(1, groups)]
    act, dsl, xall, spay, schain, vec = call(
        functools.partial(conv_state_kernel, docs=docs, **sizes),
        table,
        xr + rims + conv_params + [hpar, act, dsl, xall],
        [None] * 8 + conv_specs + [None] * 4,
        conv_shapes
        + [
            ((state + 8, part), F32),
            ((groups, state, part), F32),
            ((groups, 8, share, tokens), F32),
        ],
        [ext_shape, ((groups, share, tokens), F32)],
        name="conv_state",
        aliases={16: 0, 17: 1, 18: 2},
    )
    s_near, covered = near_of(spay, state, 1, planes)
    local_shapes = [
        ((groups, tokens, part), F32),
        ((groups, tokens, part), F32),
        ((groups, tokens, state), F32),
        ((groups, tokens, state), F32),
        ((groups, share, tokens), F32),
        ((groups, share, tokens), F32),
    ]
    triple = (share, headdim, state)
    locals_ = call(
        functools.partial(within_kernel, docs=docs, sizes=triple),
        table,
        [act, vec, gs[0]],
        [None] * 3,
        local_shapes[:4],
        [((tokens, share * tokens), F32)],
        name="within",
    )
    *gr, _ = lax.optimization_barrier((*gr, locals_[0]))
    gall, gpay, gchain = call(
        functools.partial(grad_state_kernel, **sizes),
        table,
        gr + [act, vec, spay],
        [None] * 7,
        [
            ((groups, tokens, part), BF16),
            ((state + 8, part), F32),
            ((groups, state, part), F32),
        ],
        name="grad_state",
    )
    g_near, _ = near_of(gpay, state, -1, planes)
    for span in ((0, 2), (2, 3), (3, 4)):
        locals_ = call(
            functools.partial(local_kernel, span=span, docs=docs, sizes=triple),
            table,
            [act, vec, gall, schain, gchain] + list(locals_),
            [None] * (5 + len(locals_)),
            local_shapes,
            [((tokens, share * tokens), F32)],
            name="local",
            aliases={6 + i: i for i in range(len(locals_))},
        )
        if span[1] == 2:
            s_near, *locals_ = lax.optimization_barrier((s_near, *locals_))
            s_far = shifted(s_near, GROUPS * covered)
        elif span[1] == 3:
            g_near, *locals_ = lax.optimization_barrier((g_near, *locals_))
            g_far = shifted(g_near, -GROUPS * covered)
    y_local, dx_local, db_local, dc_local, flow, xd = locals_
    *mixed, gy, state_in, dc = call(
        functools.partial(out_kernel, **sizes),
        table,
        [s_near, s_far, act, y_local, gall, vec, hpar, dc_local],
        [None] * 8,
        [((tokens, part), BF16)] * groups
        + [
            ((groups, share, tokens), F32),
            ((state, part), F32),
            ((groups, tokens, state), F32),
        ],
        name="out",
    )
    mr = [mixed[0]] + [swapped(mixed[k], k) for k in range(1, groups)]
    common = [act, dsl, dx_local, db_local, dc, gall, vec, hpar]
    edge, adjoint, high, low = call(
        functools.partial(edge_kernel, **sizes),
        table,
        [g_near, g_far] + common,
        [None] * 10,
        [
            ((8, width), F32),
            ((state, part), F32),
            ((state, part), BF16),
            ((state, part), BF16),
        ],
        name="edge",
    )
    rim_back = shifted(edge, -groups)
    settings = dict(sizes=triple, docs=docs, taps=taps)
    common = [high, low] + common + [xall]
    du_shape = ((groups * tokens, width), F32)
    par_shape = ((8, width + 256), F32)
    du, par_far, aux = call(
        functools.partial(back_far_kernel, **settings),
        table,
        common,
        [None] * 11,
        [du_shape, par_shape, ((3, share, tokens), F32)],
        name="back_far",
    )
    du, params, *grad_steps = call(
        functools.partial(back_near_kernel, **settings),
        table,
        common
        + [adjoint, state_in, spay, gy, flow, xd, par_far, aux, du],
        [None] * 20,
        [du_shape, par_shape] + [((share, tokens), F32)] * groups,
        [((groups, share, tokens), F32)] * 2,
        name="back_near",
        aliases={20: 0},
    )
    rim_back, *mr = lax.optimization_barrier((rim_back, *mr))
    pair_shapes = [((tokens, width), BF16)] * 2
    ext_back = [((2 * tokens + 8, width), F32)]
    back_far = call(
        functools.partial(conv_back_kernel, far=True, **settings),
        table,
        [du, rim_back] + [conv_weight] * 3,
        [None] * 2 + column_specs(taps),
        pair_shapes,
        ext_back,
        name="conv_back_far",
    )
    br_far = [swapped(back_far[k - 2], k) for k in (2, 3)]
    (mixer_out,) = call(
        join_kernel, table, mr, [None] * groups, [((tokens, inner), BF16)],
        [pltpu.SemaphoreType.DMA((groups,))], name="join_out", vmem=False, far=(0,),
    )
    step = groups
    received = []
    while step < devices:
        ways = 4 if 4 * step <= devices else 2
        params = functools.reduce(jnp.add, received, params)
        received = [swapped(params, way * step) for way in range(ways - 1, 0, -1)]
        step *= ways
    small = call(
        join_small_kernel,
        table,
        [params] + received + list(grad_steps),
        [None] * (1 + len(received) + groups),
        [((8, width + 256 + 2 * tokens), F32)] * groups,
        name="join_small",
    )
    du, br_far[0], mixer_out, *small = lax.optimization_barrier(
        (du, br_far[0], mixer_out, *small)
    )
    back_near = call(
        functools.partial(conv_back_kernel, far=False, **settings),
        table,
        [du, rim_back] + [conv_weight] * 3,
        [None] * 2 + column_specs(taps),
        pair_shapes,
        ext_back,
        name="conv_back_near",
    )
    br = [back_near[0], swapped(back_near[1], 1)] + br_far
    pr = [small[0]] + [swapped(small[k], k) for k in range(1, groups)]
    grad_input, grad_step, grad_conv, grad_heads = call(
        functools.partial(join_grads_kernel, scale=(tokens * devices) ** (-0.5), **shapes),
        table,
        br + pr,
        [None] * (2 * groups),
        [
            ((tokens, channels), BF16),
            ((heads, tokens), F32),
            ((taps + 1, channels), F32),
            ((3, heads), F32),
        ],
        [((heads, 128), F32), pltpu.SemaphoreType.DMA((3 * groups,))],
        name="join_grads",
        vmem=False,
        far=(0,),
    )
    return mixer_out, grad_input, grad_step.T, grad_conv, grad_heads


def solution(mesh):
    rows = P(("groups", "ctx"), None)
    return jax.shard_map(
        body,
        mesh=mesh,
        in_specs=(rows, rows, P(), P(), P(), P(), P(), P("groups"), rows),
        out_specs=(rows, rows, rows, P("groups", None), P("groups", None)),
        check_vma=False,
    )
```

```python
import functools

import jax
import jax.numpy as jnp
from jax import lax
from jax.experimental import pallas as pl
from jax.experimental.pallas import tpu as pltpu
from jax.sharding import PartitionSpec as P

GROUPS = 4
F32 = jnp.float32
BF16 = jnp.bfloat16
NEG = -1e30
LIMIT = 12 * 1024 * 1024
STEP, CUM, TAIL, HEAD, TP, HP, WHOLE, SIG = range(8)

NN = (((1,), (0,)), ((), ()))
NT = (((1,), (1,)), ((), ()))
TN = (((0,), (0,)), ((), ()))


def mm(a, b, dims):
    return lax.dot_general(a, b, dims, preferred_element_type=F32)


def halves(a):
    high = a.astype(BF16)
    return high, (a - high.astype(F32)).astype(BF16)


def thirds(a):
    high = a.astype(BF16)
    rest = a - high.astype(F32)
    mid = rest.astype(BF16)
    return high, mid, (rest - mid.astype(F32)).astype(BF16)


def dot3(a, b, dims):
    return joined3(halves(a), halves(b), dims)


def joined3(a, b, dims):
    (ah, al), (bh, bl) = a, b
    (left,), (right,) = dims[0]
    if ah.shape[left] > 128:
        return mm(ah, bh, dims) + (mm(ah, bl, dims) + mm(al, bh, dims))
    both = mm(
        jnp.concatenate([ah, al], axis=left), jnp.concatenate([bh, bh], axis=right), dims
    )
    return both + mm(ah, bl, dims)


def spread_matrix(share, headdim):
    lanes = lax.broadcasted_iota(jnp.int32, (share, share * headdim), 1)
    rows = lax.broadcasted_iota(jnp.int32, (share, share * headdim), 0)
    return (lanes // headdim == rows).astype(BF16)


def spread(values, matrix):
    return mm(
        jnp.concatenate(thirds(values), axis=0), jnp.concatenate([matrix] * 3, axis=0), TN
    )


def skip_row(hpar, matrix):
    return spread(jnp.broadcast_to(hpar[:, 2:3], (hpar.shape[0], 8)), matrix)[:1]


def head_sums(products, matrix):
    return mm(
        jnp.concatenate([matrix] * 2, axis=1), jnp.concatenate(halves(products), axis=1), NT
    )


def by_triangle(values, triangle):
    return mm(
        jnp.concatenate(thirds(values), axis=1), jnp.concatenate([triangle] * 3, axis=0), NN
    )


def triangle(size, kind):
    rows = lax.broadcasted_iota(jnp.int32, (size, size), 0)
    cols = lax.broadcasted_iota(jnp.int32, (size, size), 1)
    kept = {"upto": rows <= cols, "before": rows < cols, "from": rows >= cols}[kind]
    return kept.astype(BF16)


def doc_start(position, table, docs):
    start = jnp.zeros_like(position)
    first = table[2]
    for i in range(1, docs):
        start = jnp.where(first <= position, first, start)
        first = first + table[2 + i]
    return start


def pack_kernel(s, x_ref, step_ref, *refs, share, inner, state, groups):
    outs, rims = refs[:groups], refs[groups:]
    me = s[0]
    tokens = x_ref.shape[0]
    part = inner // groups
    width = part + 2 * state
    for k in range(groups):
        q = me ^ k
        xs = outs[k]
        xs[:tokens, :part] = x_ref[:, pl.ds(pl.multiple_of(q * part, part), part)]
        xs[:tokens, part : part + state] = x_ref[
            :, pl.ds(pl.multiple_of(inner + q * state, state), state)
        ]
        xs[:tokens, part + state :] = x_ref[
            :, pl.ds(pl.multiple_of(inner + (groups + q) * state, state), state)
        ]
        rims[k][...] = xs[tokens - 16 : tokens, :]
        xs[tokens:, :] = jnp.zeros((8, width), BF16)
        place = 0
        for row in range(0, share, 8):
            raw = step_ref[pl.ds(pl.multiple_of(q * share + row, 8), 8), :]
            for piece in thirds(raw):
                xs[tokens:, place : place + tokens] = piece
                place += tokens


def pack_grad_kernel(s, g_ref, bias, decay, skip, *refs, groups):
    outs, hpar, wide, turned = refs[:groups], *refs[groups:]
    heads = bias.shape[1]
    share = heads // groups
    wide[...] = jnp.zeros_like(wide)
    for i, ref in enumerate((bias, decay, skip)):
        wide[i : i + 1, :heads] = ref[...]
    turned[...] = wide[...].T
    hpar[...] = turned[pl.ds(pl.multiple_of(s[0] * share, share), share), :]
    part = outs[0].shape[1]
    for k, out in enumerate(outs):
        q = s[0] ^ k
        out[...] = g_ref[:, pl.ds(pl.multiple_of(q * part, part), part)]


def activate(rows, weight, bias, valid, paired):
    taps = weight.shape[0]
    tokens = rows.shape[0] - 8
    u = jnp.zeros((tokens, rows.shape[1]), F32) + bias
    for k in range(taps):
        reach = taps - 1 - k
        moved = rows[8 - reach : 8 - reach + tokens]
        if reach:
            moved = moved * valid[reach]
        u = u + weight[k : k + 1] * moved
    sig = 1.0 / (1.0 + jnp.exp(-u))
    value = u * sig
    if paired:
        high, low = halves(value)
        value = high.astype(F32) + low.astype(F32)
    return value, sig * (1.0 + u * (1.0 - sig))


def convolve_head(s, first, rim, wx, wb, wc, bx, bb, bc, act_ref, dsl_ref, xall_ref, sizes, docs):
    share, headdim, state = sizes
    part = share * headdim
    tokens = act_ref.shape[1]
    pos = s[1] + first * tokens + lax.broadcasted_iota(jnp.int32, (8, 1), 0)
    inside = pos - doc_start(pos, s, docs)
    valid = [(inside >= reach).astype(F32) for reach in range(wx.shape[0])]
    own = xall_ref[pl.ds(pl.multiple_of(16 + first * tokens, 16), 16), :].astype(F32)
    rows = jnp.concatenate([rim[8:], own[:8]], axis=0)
    for lo, size, w_ref, b_ref in (
        (0, part, wx, bx), (part, state, wb, bb), (part + state, state, wc, bc)
    ):
        value, slope = activate(rows[:, lo : lo + size], w_ref[...], b_ref[...], valid, lo == 0)
        act_ref[first, :8, lo : lo + size] = value
        dsl_ref[first, :8, lo : lo + size] = slope


def convolve_pair(s, first, pieces, rim, wx, wb, wc, bx, bb, bc, act_ref, dsl_ref, xall_ref, ext,
                  sizes, docs):
    me, plane = s[0], s[1]
    share, headdim, state = sizes
    part = share * headdim
    width = part + 2 * state
    tokens = act_ref.shape[1]
    taps = wx.shape[0]
    ext[:8, :] = rim[8:]
    for k, ref in enumerate(pieces):
        place = (me & 1) ^ k
        value = ref[:tokens, :]
        ext[pl.ds(pl.multiple_of(8 + place * tokens, 8), tokens), :] = value.astype(F32)
        xall_ref[pl.ds(pl.multiple_of(16 + (first + place) * tokens, 16), tokens), :] = value

    for c in range(2):
        chunk = first + c
        pos = plane + chunk * tokens + lax.broadcasted_iota(jnp.int32, (tokens, 1), 0)
        inside = pos - doc_start(pos, s, docs)
        valid = [(inside >= reach).astype(F32) for reach in range(taps)]

        def convolve(lo, w_ref, b_ref, wlo, paired):
            rows = ext[c * tokens : c * tokens + tokens + 8, lo : lo + 128]
            value, slope = activate(
                rows, w_ref[:, wlo : wlo + 128], b_ref[:, wlo : wlo + 128], valid, paired
            )
            act_ref[chunk, :, lo : lo + 128] = value
            dsl_ref[chunk, :, lo : lo + 128] = slope

        for lo in range(0, part, 128):
            convolve(lo, wx, bx, lo, True)
        for lo in range(0, state, 128):
            convolve(part + lo, wb, bb, lo, False)
            convolve(part + state + lo, wc, bc, lo, False)


def conv_kernel(
    s, x0, x1, wx, wb, wc, bx, bb, bc, act_ref, dsl_ref, xall_ref, ext, *, sizes, docs
):
    rim = jnp.zeros((16, ext.shape[1]), F32)
    convolve_pair(
        s, s[0] & 2, (x0, x1), rim, wx, wb, wc, bx, bb, bc, act_ref, dsl_ref, xall_ref, ext,
        sizes, docs,
    )


def conv_state_kernel(
    s, x0, x1, x2, x3, r0, r1, r2, r3, wx, wb, wc, bx, bb, bc, hpar, act_in, dsl_in, xall_in,
    act_ref, dsl_ref, xall_ref, pay_ref, chain_ref, vec_ref,
    ext, raws, *, share, headdim, state, docs,
):
    me = s[0]
    plane = s[1]
    part = share * headdim
    width = part + 2 * state
    tokens = act_ref.shape[1]
    chunks = 4
    for k, ref in enumerate((x0, x1, x2, x3)):
        block = ref[tokens:, :].astype(F32)
        for i in range(share // 8):
            lo = 3 * i * tokens
            raws[me ^ k, 8 * i : 8 * i + 8] = (
                block[:, lo : lo + tokens]
                + block[:, lo + tokens : lo + 2 * tokens]
                + block[:, lo + 2 * tokens : lo + 3 * tokens]
            )
    upper_chip = (me & 2) == 2
    inner_rim = xall_ref[2 * tokens : 2 * tokens + 16, :].astype(F32)
    rim = jnp.where(upper_chip, r0[...].astype(F32) + r1[...].astype(F32), inner_rim)

    own_rim = r2[...].astype(F32) + r3[...].astype(F32)
    xall_ref[:16, :] = jnp.where(upper_chip, rim, own_rim).astype(BF16)
    convolve_head(
        s, me & 2, own_rim, wx, wb, wc, bx, bb, bc, act_ref, dsl_ref, xall_ref,
        (share, headdim, state), docs,
    )
    convolve_pair(
        s, (me & 2) ^ 2, (x2, x3), rim, wx, wb, wc, bx, bb, bc, act_ref, dsl_ref, xall_ref, ext,
        (share, headdim, state), docs,
    )

    bias = hpar[:, 0:1]
    rate = jnp.exp(hpar[:, 1:2])
    upper = triangle(tokens, "upto")
    before = jnp.zeros((share, 1), F32)
    cums, steps, ends = [], [], []
    for c in range(chunks):
        v = raws[c] + bias
        step = jnp.maximum(v, 0.0) + jnp.log1p(jnp.exp(-jnp.abs(v)))
        cum = by_triangle(-step * rate, upper)
        vec_ref[c, STEP] = step
        vec_ref[c, CUM] = cum
        vec_ref[c, SIG] = 1.0 / (1.0 + jnp.exp(-v))
        cums.append(cum)
        steps.append(step)
        ends.append(cum[:, tokens - 1 :])
    total = ends[0] + ends[1] + ends[2] + ends[3]
    last_plane = doc_start(plane + chunks * tokens - 1, s, docs)
    for c in range(chunks):
        base = plane + c * tokens
        pos = base + lax.broadcasted_iota(jnp.int32, (1, tokens), 1)
        start = doc_start(pos, s, docs)
        last = doc_start(base + tokens - 1, s, docs)
        cum, step, end = cums[c], steps[c], ends[c]
        vec_ref[c, TAIL] = jnp.exp(end - cum) * step * (pos >= last).astype(F32)
        vec_ref[c, HEAD] = jnp.exp(cum) * (start < base).astype(F32)
        vec_ref[c, HP] = jnp.exp(cum + before) * (start < plane).astype(F32)
        before = before + end
        vec_ref[c, TP] = (
            jnp.exp(total - before + (end - cum)) * step * (pos >= last_plane).astype(F32)
        )
        open_c = jnp.where(last < base, 1.0, 0.0)
        vec_ref[c, WHOLE] = jnp.broadcast_to(jnp.exp(end) * open_c, (share, tokens))
    matrix = spread_matrix(share, headdim)
    open_plane = jnp.where(last_plane < plane, 1.0, 0.0)
    pay_ref[state:, :] = spread(jnp.broadcast_to(jnp.exp(total) * open_plane, (share, 8)), matrix)

    carried = jnp.zeros((state, part), F32)
    for c in range(chunks):
        chain_ref[c] = carried
        weighted = act_ref[c, :, :part] * spread(vec_ref[c, TAIL], matrix)
        local = dot3(act_ref[c, :, part : part + state], weighted, TN)
        carried = carried * spread(vec_ref[c, WHOLE], matrix) + local
    pay_ref[:state, :] = carried


def grad_state_kernel(
    s, g0, g1, g2, g3, act_ref, vec_ref, pay_in, gall_ref, pay_ref, chain_ref,
    *, share, headdim, state,
):
    me = s[0]
    part = share * headdim
    chunks = 4
    for k, ref in enumerate((g0, g1, g2, g3)):
        gall_ref[me ^ k] = ref[...]
    matrix = spread_matrix(share, headdim)
    carried = jnp.zeros((state, part), F32)
    for c in range(chunks - 1, -1, -1):
        chain_ref[c] = carried
        weighted = gall_ref[c].astype(F32) * spread(vec_ref[c, HEAD], matrix)
        local = dot3(act_ref[c, :, part + state :], weighted, TN)
        carried = carried * spread(vec_ref[c, WHOLE], matrix) + local
    pay_ref[:state, :] = carried
    pay_ref[state:, :] = pay_in[state:, :]


def within_chunk(s, c, g_ref, act_ref, vec_ref, y_ref, dx_ref, db_ref, dc_ref, wide, sizes, docs):
    share, headdim, state = sizes
    part = share * headdim
    tokens = act_ref.shape[1]
    lanes = lax.broadcasted_iota(jnp.int32, (tokens, 2 * headdim), 1)
    left = lanes < headdim
    base = s[1] + c * tokens
    tpos = base + lax.broadcasted_iota(jnp.int32, (tokens, tokens), 0)
    spos = base + lax.broadcasted_iota(jnp.int32, (tokens, tokens), 1)
    tstart = doc_start(tpos, s, docs)
    mask = jnp.where((spos <= tpos) & (spos >= tstart), 0.0, NEG)
    b = act_ref[c, :, part : part + state]
    cc = act_ref[c, :, part + state :]
    m = dot3(cc, b, NT)
    cum = vec_ref[c, CUM]
    step = vec_ref[c, STEP]
    wide[...] = spread(cum, spread_matrix(share, tokens))
    dm = jnp.zeros((tokens, tokens), F32)
    for pair in range(share // 2):
        lo = pair * 2 * headdim
        xp = act_ref[c, :, lo : lo + 2 * headdim]
        gp = g_ref[:, lo : lo + 2 * headdim]
        zero = jnp.zeros_like(gp)
        gst = jnp.concatenate([jnp.where(left, gp, zero), jnp.where(left, zero, gp)], axis=0)
        factors = []
        for h in (2 * pair, 2 * pair + 1):
            diff = wide[:, h * tokens : (h + 1) * tokens] - cum[h : h + 1, :]
            factors.append(jnp.exp(diff + mask) * step[h : h + 1, :])
        pieces = jnp.concatenate(halves(xp), axis=1)
        dw = mm(jnp.concatenate([gst, gst], axis=1), pieces, NT)
        dm = dm + dw[:tokens] * factors[0] + dw[tokens:] * factors[1]
        w = jnp.concatenate([m * factors[0], m * factors[1]], axis=0)
        w = jnp.concatenate(halves(w), axis=1)
        yst = mm(w, jnp.concatenate([pieces, pieces], axis=0), NN)
        yst = yst[:, : 2 * headdim] + yst[:, 2 * headdim :]
        y_ref[c, :, lo : lo + 2 * headdim] = jnp.where(left, yst[:tokens], yst[tokens:])
        dst = mm(w, gst, TN)
        dx_ref[c, :, lo : lo + 2 * headdim] = dst[:tokens] + dst[tokens:]
    dc_ref[c] = dot3(dm, b, NN)
    db_ref[c] = dot3(dm, cc, TN)


def within_kernel(
    s, act_ref, vec_ref, g_ref, y_ref, dx_ref, db_ref, dc_ref, wide, *, sizes, docs
):
    within_chunk(
        s, s[0], g_ref, act_ref, vec_ref, y_ref, dx_ref, db_ref, dc_ref, wide, sizes, docs
    )


def local_kernel(
    s, act_ref, vec_ref, gall_ref, schain, gchain, *refs, span, sizes, docs,
):
    y_ref, dx_ref, db_ref, dc_ref, flow_ref, xd_ref, wide = refs[-7:]
    share, headdim, state = sizes
    part = share * headdim
    tokens = act_ref.shape[1]
    matrix = spread_matrix(share, headdim)
    start_sums = triangle(tokens, "from")
    end_sums = triangle(tokens, "before")

    def across(c):
        b = act_ref[c, :, part : part + state]
        cc = act_ref[c, :, part + state :]
        head_in = spread(vec_ref[c, HEAD], matrix)
        tail = spread(vec_ref[c, TAIL], matrix)
        x = act_ref[c, :, :part]
        g = gall_ref[c].astype(F32)
        y = y_ref[c] + head_in * dot3(cc, schain[c], NN)
        y_ref[c] = y
        dx_tail = tail * dot3(b, gchain[c], NN)
        dx_near = dx_ref[c]
        near = head_sums(x * dx_near, matrix)
        away = head_sums(x * dx_tail, matrix)
        dx_ref[c] = dx_near + dx_tail
        xd_ref[c] = near + away
        inner = jnp.sum(schain[c] * gchain[c], axis=0, keepdims=True)
        through = head_sums(jnp.broadcast_to(inner, (8, part)), matrix)[:, :1]
        flow_ref[c] = (
            by_triangle(head_sums(g * y, matrix) - near, start_sums)
            + by_triangle(away, end_sums)
            + through * vec_ref[c, WHOLE]
        )
        dc_ref[c] = dc_ref[c] + dot3(g * head_in, schain[c], NT)
        db_ref[c] = db_ref[c] + dot3(x * tail, gchain[c], NT)

    def chunk(k, carry):
        c = s[0] ^ k
        within_chunk(
            s, c, gall_ref.at[c], act_ref, vec_ref, y_ref, dx_ref, db_ref, dc_ref, wide, sizes,
            docs,
        )
        across(c)
        return carry

    if span[0] == 0:
        across(s[0])
    lax.fori_loop(max(span[0], 1), span[1], chunk, 0)


def out_kernel(
    s, one, two, act_ref, y_ref, gall_ref, vec_ref, hpar, dcl_ref,
    m0, m1, m2, m3, gy_ref, in_ref, dc_ref, *, share, headdim, state,
):
    me = s[0]
    part = share * headdim
    matrix = spread_matrix(share, headdim)
    arrived = one[:state, :] + one[state : state + 1, :] * two[:state, :]
    in_ref[...] = arrived
    ih, il = halves(arrived)
    skip = skip_row(hpar, matrix)
    for k, out in enumerate((m0, m1, m2, m3)):
        c = me ^ k
        reach = spread(vec_ref[c, HP], matrix)
        ch, cl = halves(act_ref[c, :, part + state :])
        carry = joined3((ch, cl), (ih, il), NN)
        y = reach * carry
        g = gall_ref[c].astype(F32)
        gy_ref[c] = head_sums(g * y, matrix)
        y = y + y_ref[c]
        out[...] = (y + skip * act_ref[c, :, :part]).astype(BF16)
        gh, gl = halves(g * reach)
        dc_ref[c] = dcl_ref[c] + mm(gh, ih, NT) + (mm(gh, il, NT) + mm(gl, ih, NT))


def input_grads(c, rows, high, low, act_ref, dsl_ref, dxl_ref, dbl_ref, dc_ref, gall_ref, vec_ref,
                skip, matrix, part, state):
    x = act_ref[c, :rows, :part]
    g = gall_ref[c, :rows].astype(F32)
    tail = spread(vec_ref[c, TP][:, :rows], matrix)
    bh, bl = halves(act_ref[c, :rows, part : part + state])
    far = tail * joined3((bh, bl), (high, low), NN)
    xh, xl = halves(x * tail)
    db = dbl_ref[c, :rows] + mm(xh, high, NT) + (mm(xh, low, NT) + mm(xl, high, NT))
    dx = far + dxl_ref[c, :rows] + skip * g
    return (
        dx * dsl_ref[c, :rows, :part],
        db * dsl_ref[c, :rows, part : part + state],
        dc_ref[c, :rows] * dsl_ref[c, :rows, part + state :],
        x * far,
        g * x,
    )


def edge_kernel(
    s, one, two, act_ref, dsl_ref, dxl_ref, dbl_ref, dc_ref, gall_ref, vec_ref, hpar,
    edge_ref, adjoint_ref, high_ref, low_ref, *, share, headdim, state,
):
    part = share * headdim
    matrix = spread_matrix(share, headdim)
    adjoint = one[:state, :] + one[state : state + 1, :] * two[:state, :]
    adjoint_ref[...] = adjoint
    high, low = halves(adjoint)
    high_ref[...] = high
    low_ref[...] = low
    grads = input_grads(
        0, 16, high, low, act_ref, dsl_ref, dxl_ref, dbl_ref, dc_ref, gall_ref, vec_ref,
        skip_row(hpar, matrix), matrix, part, state,
    )
    edge_ref[:, :part] = grads[0][:8]
    edge_ref[:, part : part + state] = grads[1][:8]
    edge_ref[:, part + state :] = grads[2][:8]


def pair_grads(s, first, high_ref, low_ref, act_ref, dsl_ref, dxl_ref, dbl_ref, dc_ref, gall_ref,
               vec_ref, hpar, xall_ref, du_ref, par_ref, sizes, docs, taps):
    share, headdim, state = sizes
    part = share * headdim
    width = part + 2 * state
    tokens = act_ref.shape[1]
    plane = s[1]
    matrix = spread_matrix(share, headdim)
    skip = skip_row(hpar, matrix)
    high, low = high_ref[...], low_ref[...]
    away, skips = [], []
    for i in range(2):
        c = first + i
        grads = input_grads(
            c, tokens, high, low, act_ref, dsl_ref, dxl_ref, dbl_ref, dc_ref, gall_ref, vec_ref,
            skip, matrix, part, state,
        )
        rows = pl.ds(pl.multiple_of(c * tokens, tokens), tokens)
        du_ref[rows, :part] = grads[0]
        du_ref[rows, part : part + state] = grads[1]
        du_ref[rows, part + state : width] = grads[2]
        away.append(head_sums(grads[3], matrix))
        skips.append(head_sums(grads[4], matrix))
    for lo in range(0, width, 128):
        sums = [jnp.zeros((8, 128), F32) for _ in range(taps + 1)]
        for i in range(2):
            c = first + i
            begin = pl.multiple_of(c * tokens, tokens)
            rows = xall_ref[pl.ds(begin, tokens + 16), lo : lo + 128].astype(F32)
            pos = plane + c * tokens + lax.broadcasted_iota(jnp.int32, (tokens, 1), 0)
            inside = pos - doc_start(pos, s, docs)
            du = du_ref[pl.ds(begin, tokens), lo : lo + 128]
            for k in range(taps):
                reach = taps - 1 - k
                moved = rows[16 - reach : 16 - reach + tokens]
                if reach:
                    moved = moved * (inside >= reach).astype(F32)
                sums[k] = sums[k] + jnp.sum((du * moved).reshape(tokens // 8, 8, 128), axis=0)
            sums[taps] = sums[taps] + jnp.sum(du.reshape(tokens // 8, 8, 128), axis=0)
        for k in range(taps + 1):
            par_ref[k : k + 1, lo : lo + 128] = jnp.sum(sums[k], axis=0, keepdims=True)
    return away, skips[0] + skips[1]


def back_far_kernel(
    s, high_ref, low_ref, act_ref, dsl_ref, dxl_ref, dbl_ref, dc_ref, gall_ref, vec_ref, hpar,
    xall_ref, du_ref, par_ref, aux_ref, *, sizes, docs, taps,
):
    share, headdim, state = sizes
    part = share * headdim
    width = part + 2 * state
    tokens = act_ref.shape[1]
    par_ref[...] = jnp.zeros_like(par_ref)
    away, skips = pair_grads(
        s, (s[0] & 2) ^ 2, high_ref, low_ref, act_ref, dsl_ref, dxl_ref, dbl_ref, dc_ref, gall_ref,
        vec_ref, hpar, xall_ref, du_ref, par_ref, sizes, docs, taps,
    )
    aux_ref[0], aux_ref[1], aux_ref[2] = away[0], away[1], skips


def back_near_kernel(
    s, high_ref, low_ref, act_ref, dsl_ref, dxl_ref, dbl_ref, dc_ref, gall_ref, vec_ref, hpar,
    xall_ref, adjoint_ref, in_ref, pay, gy_ref, flow_ref, xd_ref, par_in, aux, du_in,
    du_ref, par_ref, g0, g1, g2, g3, away_s, gs_s, *, sizes, docs, taps,
):
    share, headdim, state = sizes
    part = share * headdim
    width = part + 2 * state
    tokens = act_ref.shape[1]
    chunks = 4
    me = s[0]
    matrix = spread_matrix(share, headdim)
    own, skips = pair_grads(
        s, me & 2, high_ref, low_ref, act_ref, dsl_ref, dxl_ref, dbl_ref, dc_ref, gall_ref,
        vec_ref, hpar, xall_ref, du_ref, par_ref, sizes, docs, taps,
    )
    par_ref[: taps + 1, :width] = par_ref[: taps + 1, :width] + par_in[: taps + 1, :width]
    for i in range(2):
        away_s[(me & 2) + i] = own[i]
        away_s[((me & 2) ^ 2) + i] = aux[i]
    inner = jnp.sum(adjoint_ref[...] * in_ref[...], axis=0, keepdims=True)
    inner = inner * pay[state : state + 1, :]
    through = head_sums(jnp.broadcast_to(inner, (8, part)), matrix)[:, :1]
    rate = jnp.exp(hpar[:, 1:2])
    start_sums = triangle(tokens, "from")
    end_sums = triangle(tokens, "before")
    g_bias = jnp.zeros((share, 1), F32)
    g_decay = jnp.zeros((share, 1), F32)
    for c in range(chunks):
        flow = (
            flow_ref[c] + by_triangle(gy_ref[c], start_sums) + by_triangle(away_s[c], end_sums)
        ) + through
        for d in range(chunks):
            if d > c:
                flow = flow + jnp.sum(gy_ref[d], axis=1, keepdims=True)
            if d < c:
                flow = flow + jnp.sum(away_s[d], axis=1, keepdims=True)
        step = vec_ref[c, STEP]
        grad_step = ((xd_ref[c] + away_s[c]) / step - rate * flow) * vec_ref[c, SIG]
        gs_s[c] = grad_step
        g_bias = g_bias + jnp.sum(grad_step, axis=1, keepdims=True)
        g_decay = g_decay - rate * jnp.sum(flow * step, axis=1, keepdims=True)
    for k, out in enumerate((g0, g1, g2, g3)):
        out[...] = gs_s[me ^ k]
    g_skip = jnp.sum(skips + aux[2], axis=1, keepdims=True)
    lane = lax.broadcasted_iota(jnp.int32, (share, 128), 1)
    heads = jnp.where(lane == 0, g_bias, jnp.where(lane == 1, g_decay, g_skip))
    par_ref[taps + 1 :, :width] = jnp.zeros((8 - taps - 1, width), F32)
    par_ref[:, width : width + 128] = heads[:8]
    par_ref[:, width + 128 :] = heads[8:]


def conv_back_kernel(
    s, du_ref, rim_ref, wx, wb, wc, o0, o1, ext, *, far, sizes, docs, taps
):
    share, headdim, state = sizes
    me = s[0]
    plane = s[1]
    part = share * headdim
    width = part + 2 * state
    tokens = o0.shape[0]
    first = (me & 2) ^ (2 if far else 0)
    ext[: 2 * tokens, :] = du_ref[pl.ds(pl.multiple_of(first * tokens, tokens), 2 * tokens), :]
    ext[2 * tokens :, :] = jnp.where(
        first == 2, rim_ref[...], du_ref[2 * tokens : 2 * tokens + 8, :]
    )
    for k, out in enumerate((o0, o1)):
        place = (me & 1) ^ k
        pos = plane + (first + place) * tokens + lax.broadcasted_iota(jnp.int32, (tokens, 1), 0)
        valid = []
        for reach in range(1, taps):
            ahead = pos + reach
            valid.append((ahead - doc_start(ahead, s, docs) >= reach).astype(F32))
        begin = pl.multiple_of(place * tokens, tokens)
        for lo in range(0, width, 128):
            rows = ext[pl.ds(begin, tokens + 8), lo : lo + 128]
            if lo < part:
                w = wx[:, lo : lo + 128]
            elif lo < part + state:
                w = wb[:, lo - part : lo - part + 128]
            else:
                w = wc[:, lo - part - state : lo - part - state + 128]
            total = w[taps - 1 : taps] * rows[:tokens]
            for reach in range(1, taps):
                k_tap = taps - 1 - reach
                total = total + w[k_tap : k_tap + 1] * (
                    rows[reach : reach + tokens] * valid[reach - 1]
                )
            out[:, lo : lo + 128] = total.astype(BF16)


def join_kernel(s, p0, p1, p2, p3, out_ref, done):
    part = p0.shape[1]
    copies = []
    for k, ref in enumerate((p0, p1, p2, p3)):
        columns = pl.ds(pl.multiple_of((s[0] ^ k) * part, part), part)
        copies.append(pltpu.make_async_copy(ref, out_ref.at[:, columns], done.at[k]))
    for copy in copies:
        copy.start()
    for copy in copies:
        copy.wait()


def join_small_kernel(s, first, *refs):
    groups = 4
    width = first.shape[1]
    received, steps, outs = refs[: -2 * groups], refs[-2 * groups : -groups], refs[-groups:]
    total = first[...]
    for ref in received:
        total = total + ref[...]
    for step, out in zip(steps, outs):
        tokens = step.shape[1]
        out[:, :width] = total
        out[:, width : width + tokens] = step[:8, :]
        out[:, width + tokens :] = step[8:, :]


def join_grads_kernel(
    s, p0, p1, p2, p3, g0, g1, g2, g3, out_ref, gs_ref, conv_ref, head_ref, turned, done,
    *, share, inner, state, groups, scale,
):
    part = inner // groups
    width = part + 2 * state
    copies = []
    for k, ref in enumerate((p0, p1, p2, p3)):
        q = s[0] ^ k
        for i, (size, lo, first) in enumerate((
            (part, 0, q * part),
            (state, part, inner + q * state),
            (state, part + state, inner + (groups + q) * state),
        )):
            columns = pl.ds(pl.multiple_of(first, size), size)
            copies.append(
                pltpu.make_async_copy(
                    ref.at[:, lo : lo + size], out_ref.at[:, columns], done.at[3 * k + i]
                )
            )
    for copy in copies:
        copy.start()
    rows = conv_ref.shape[0]
    tokens = gs_ref.shape[1]
    for k, ref in enumerate((g0, g1, g2, g3)):
        q = s[0] ^ k
        conv_ref[:, pl.ds(pl.multiple_of(q * part, part), part)] = ref[:rows, :part] * scale
        conv_ref[:, pl.ds(pl.multiple_of(inner + q * state, state), state)] = (
            ref[:rows, part : part + state] * scale
        )
        conv_ref[:, pl.ds(pl.multiple_of(inner + (groups + q) * state, state), state)] = (
            ref[:rows, part + state : width] * scale
        )
        first = pl.multiple_of(q * share, share)
        turned[pl.ds(first, 8), :] = ref[:, width : width + 128]
        turned[pl.ds(first + 8, 8), :] = ref[:, width + 128 : width + 256]
        last = width + 256
        gs_ref[pl.ds(first, 8), :] = ref[:, last : last + tokens]
        gs_ref[pl.ds(first + 8, 8), :] = ref[:, last + tokens :]
    head_ref[...] = turned[...].T[: head_ref.shape[0], :] * scale
    for copy in copies:
        copy.wait()


def call(kernel, table, operands, specs, outs, scratch=(), name=None, vmem=True, aliases=None,
         far=()):
    here = pl.BlockSpec(memory_space=pltpu.VMEM)
    in_specs = [here if spec is None else spec for spec in specs]
    return pl.pallas_call(
        kernel,
        out_shape=[
            pltpu.VMEM(shape, kind) if vmem else jax.ShapeDtypeStruct(shape, kind)
            for shape, kind in outs
        ],
        grid_spec=pltpu.PrefetchScalarGridSpec(
            num_scalar_prefetch=1,
            grid=(1,),
            in_specs=in_specs,
            out_specs=[
                pl.BlockSpec(memory_space=pl.ANY) if i in far else here for i in range(len(outs))
            ],
            scratch_shapes=[
                pltpu.VMEM(*entry) if isinstance(entry, tuple) else entry for entry in scratch
            ],
        ),
        compiler_params=pltpu.CompilerParams(vmem_limit_bytes=LIMIT),
        cost_estimate=pl.CostEstimate(flops=1, transcendentals=0, bytes_accessed=1),
        name=name,
        input_output_aliases=aliases or {},
    )(table, *operands)


def swapped(value, bits):
    count = lax.axis_size("ctx")
    return lax.ppermute(value, "ctx", [(i, i ^ bits) for i in range(count)])


def shifted(value, steps):
    count = lax.axis_size("ctx")
    pairs = [(i, i + steps) for i in range(count) if 0 <= i + steps < count]
    return lax.ppermute(value, "ctx", pairs)


def after(value, *others):
    return lax.optimization_barrier((value, *others))[0]


def near_of(payload, state, direction, planes):
    near = shifted(payload, direction * GROUPS)
    covered, window = 1, planes // 2
    while 2 * covered < window:
        far = shifted(near, direction * GROUPS * covered)
        factor = near[state : state + 1]
        near = jnp.concatenate(
            [near[:state] + factor * far[:state], near[state:] * far[state:]], axis=0
        )
        covered *= 2
    return near, covered


def body(
    conv_input, step_raw, step_bias, decay_log, skip_gain, conv_weight, conv_bias, doc_lengths,
    grad_out,
):
    tokens, channels = conv_input.shape
    heads = step_raw.shape[1]
    taps = conv_weight.shape[0]
    inner = grad_out.shape[1]
    headdim = inner // heads
    groups = GROUPS
    share = heads // groups
    state = (channels - inner) // (2 * groups)
    part = inner // groups
    width = part + 2 * state
    docs = doc_lengths.shape[0]
    devices = lax.axis_size("ctx")
    planes = devices // groups
    me = lax.axis_index("ctx")
    sizes = dict(share=share, headdim=headdim, state=state)
    table = jnp.concatenate(
        [
            jnp.stack([me & (groups - 1), (me & -groups) * tokens]).astype(jnp.int32),
            doc_lengths,
        ]
    )
    bias_row = conv_bias[None, :]
    b_first = inner // state

    def column_specs(rows):
        return [
            pl.BlockSpec((rows, part), lambda i, s: (0, s[0])),
            pl.BlockSpec((rows, state), lambda i, s: (0, b_first + s[0])),
            pl.BlockSpec((rows, state), lambda i, s: (0, b_first + groups + s[0])),
        ]

    shapes = dict(share=share, inner=inner, state=state, groups=groups)
    packed = call(
        functools.partial(pack_kernel, **shapes),
        table,
        [conv_input, step_raw.T],
        [None] * 2,
        [((tokens + 8, width), BF16)] * groups + [((16, width), BF16)] * groups,
        name="pack",
    )
    xs, edges = packed[:groups], packed[groups:]
    *gs, hpar = call(
        functools.partial(pack_grad_kernel, groups=groups),
        table,
        [grad_out, step_bias[None, :], decay_log[None, :], skip_gain[None, :]],
        [None] * 4,
        [((tokens, part), BF16)] * groups + [((share, 128), F32)],
        [((128, 128), F32)] * 2,
        name="pack_grad",
    )
    xr = [xs[0]] + [swapped(xs[k], k) for k in range(1, groups)]
    rims = []
    for k in range(groups):
        pairs = []
        for i in range(devices):
            source = i - 1 - i % 2 if k >= 2 else i - 1 - i % groups
            if source >= 0 and (source % groups) ^ (i % groups) == k:
                pairs.append((source, i))
        rims.append(lax.ppermute(edges[k], "ctx", pairs))
    conv_shapes = [
        ((groups, tokens, width), F32),
        ((groups, tokens, width), F32),
        ((groups * tokens + 16, width), BF16),
    ]
    conv_specs = column_specs(taps) + column_specs(1)
    conv_params = [conv_weight] * 3 + [bias_row] * 3
    ext_shape = ((2 * tokens + 8, width), F32)
    act, dsl, xall = call(
        functools.partial(conv_kernel, docs=docs, sizes=(share, headdim, state)),
        table,
        [xr[0], xr[1]] + conv_params,
        [None] * 2 + conv_specs,
        conv_shapes,
        [ext_shape],
        name="conv",
    )
    act, *gs = lax.optimization_barrier((act, *gs))
    gr = [gs[0]] + [swapped(gs[k], k) for k in range(1, groups)]
    act, dsl, xall, spay, schain, vec = call(
        functools.partial(conv_state_kernel, docs=docs, **sizes),
        table,
        xr + rims + conv_params + [hpar, act, dsl, xall],
        [None] * 8 + conv_specs + [None] * 4,
        conv_shapes
        + [
            ((state + 8, part), F32),
            ((groups, state, part), F32),
            ((groups, 8, share, tokens), F32),
        ],
        [ext_shape, ((groups, share, tokens), F32)],
        name="conv_state",
        aliases={16: 0, 17: 1, 18: 2},
    )
    s_near, covered = near_of(spay, state, 1, planes)
    local_shapes = [
        ((groups, tokens, part), F32),
        ((groups, tokens, part), F32),
        ((groups, tokens, state), F32),
        ((groups, tokens, state), F32),
        ((groups, share, tokens), F32),
        ((groups, share, tokens), F32),
    ]
    triple = (share, headdim, state)
    locals_ = call(
        functools.partial(within_kernel, docs=docs, sizes=triple),
        table,
        [act, vec, gs[0]],
        [None] * 3,
        local_shapes[:4],
        [((tokens, share * tokens), F32)],
        name="within",
    )
    *gr, _ = lax.optimization_barrier((*gr, locals_[0]))
    gall, gpay, gchain = call(
        functools.partial(grad_state_kernel, **sizes),
        table,
        gr + [act, vec, spay],
        [None] * 7,
        [
            ((groups, tokens, part), BF16),
            ((state + 8, part), F32),
            ((groups, state, part), F32),
        ],
        name="grad_state",
    )
    g_near, _ = near_of(gpay, state, -1, planes)
    for span in ((0, 2), (2, 3), (3, 4)):
        locals_ = call(
            functools.partial(local_kernel, span=span, docs=docs, sizes=triple),
            table,
            [act, vec, gall, schain, gchain] + list(locals_),
            [None] * (5 + len(locals_)),
            local_shapes,
            [((tokens, share * tokens), F32)],
            name="local",
            aliases={6 + i: i for i in range(len(locals_))},
        )
        if span[1] == 2:
            s_near, *locals_ = lax.optimization_barrier((s_near, *locals_))
            s_far = shifted(s_near, GROUPS * covered)
        elif span[1] == 3:
            g_near, *locals_ = lax.optimization_barrier((g_near, *locals_))
            g_far = shifted(g_near, -GROUPS * covered)
    y_local, dx_local, db_local, dc_local, flow, xd = locals_
    *mixed, gy, state_in, dc = call(
        functools.partial(out_kernel, **sizes),
        table,
        [s_near, s_far, act, y_local, gall, vec, hpar, dc_local],
        [None] * 8,
        [((tokens, part), BF16)] * groups
        + [
            ((groups, share, tokens), F32),
            ((state, part), F32),
            ((groups, tokens, state), F32),
        ],
        name="out",
    )
    mr = [mixed[0]] + [swapped(mixed[k], k) for k in range(1, groups)]
    common = [act, dsl, dx_local, db_local, dc, gall, vec, hpar]
    edge, adjoint, high, low = call(
        functools.partial(edge_kernel, **sizes),
        table,
        [g_near, g_far] + common,
        [None] * 10,
        [
            ((8, width), F32),
            ((state, part), F32),
            ((state, part), BF16),
            ((state, part), BF16),
        ],
        name="edge",
    )
    rim_back = shifted(edge, -groups)
    settings = dict(sizes=triple, docs=docs, taps=taps)
    common = [high, low] + common + [xall]
    du_shape = ((groups * tokens, width), F32)
    par_shape = ((8, width + 256), F32)
    du, par_far, aux = call(
        functools.partial(back_far_kernel, **settings),
        table,
        common,
        [None] * 11,
        [du_shape, par_shape, ((3, share, tokens), F32)],
        name="back_far",
    )
    du, params, *grad_steps = call(
        functools.partial(back_near_kernel, **settings),
        table,
        common
        + [adjoint, state_in, spay, gy, flow, xd, par_far, aux, du],
        [None] * 20,
        [du_shape, par_shape] + [((share, tokens), F32)] * groups,
        [((groups, share, tokens), F32)] * 2,
        name="back_near",
        aliases={20: 0},
    )
    rim_back, *mr = lax.optimization_barrier((rim_back, *mr))
    pair_shapes = [((tokens, width), BF16)] * 2
    ext_back = [((2 * tokens + 8, width), F32)]
    back_far = call(
        functools.partial(conv_back_kernel, far=True, **settings),
        table,
        [du, rim_back] + [conv_weight] * 3,
        [None] * 2 + column_specs(taps),
        pair_shapes,
        ext_back,
        name="conv_back_far",
    )
    br_far = [swapped(back_far[k - 2], k) for k in (2, 3)]
    (mixer_out,) = call(
        join_kernel, table, mr, [None] * groups, [((tokens, inner), BF16)],
        [pltpu.SemaphoreType.DMA((groups,))], name="join_out", vmem=False, far=(0,),
    )
    step = groups
    received = []
    while step < devices:
        ways = 4 if 4 * step <= devices else 2
        params = functools.reduce(jnp.add, received, params)
        received = [swapped(params, way * step) for way in range(ways - 1, 0, -1)]
        step *= ways
    small = call(
        join_small_kernel,
        table,
        [params] + received + list(grad_steps),
        [None] * (1 + len(received) + groups),
        [((8, width + 256 + 2 * tokens), F32)] * groups,
        name="join_small",
    )
    du, br_far[0], mixer_out, *small = lax.optimization_barrier(
        (du, br_far[0], mixer_out, *small)
    )
    back_near = call(
        functools.partial(conv_back_kernel, far=False, **settings),
        table,
        [du, rim_back] + [conv_weight] * 3,
        [None] * 2 + column_specs(taps),
        pair_shapes,
        ext_back,
        name="conv_back_near",
    )
    br = [back_near[0], swapped(back_near[1], 1)] + br_far
    pr = [small[0]] + [swapped(small[k], k) for k in range(1, groups)]
    grad_input, grad_step, grad_conv, grad_heads = call(
        functools.partial(join_grads_kernel, scale=(tokens * devices) ** (-0.5), **shapes),
        table,
        br + pr,
        [None] * (2 * groups),
        [
            ((tokens, channels), BF16),
            ((heads, tokens), F32),
            ((taps + 1, channels), F32),
            ((3, heads), F32),
        ],
        [((heads, 128), F32), pltpu.SemaphoreType.DMA((3 * groups,))],
        name="join_grads",
        vmem=False,
        far=(0,),
    )
    return mixer_out, grad_input, grad_step.T, grad_conv, grad_heads


def solution(mesh):
    rows = P(("groups", "ctx"), None)
    return jax.shard_map(
        body,
        mesh=mesh,
        in_specs=(rows, rows, P(), P(), P(), P(), P(), P("groups"), rows),
        out_specs=(rows, rows, rows, P("groups", None), P("groups", None)),
        check_vma=False,
    )
```
